32 devices in a mesh: shard: 4 (over y, x), expert: 8 (over z, core).
Axes of the slice: x: 2, y: 2, z: 4, core: 2. Of those that a mesh axis runs over, the one named last changes fastest.
Arguments:
- block_input: bfloat16 [8, 512, 2048], P('expert', 'shard'), may hold values from -6 to 6
- segment_ids: int32 [8, 512], P('expert'), may hold values from 0 to 1, never falling along the last dimension, each value on 1 to 384 neighbouring positions
- expert_routes: int32 [8, 512, 8], P('expert', 'shard'), may hold values from 0 to 15, all different within a row; in each aligned block of 128 rows (0 to 127, 128 to 255, ..., all dimensions but the last counted through in order) at most 96 rows name the same one
- attn_gain: bfloat16 [2048], P('shard'), may hold values from 0.5 to 1.5
- w_query: bfloat16 [2048, 2048], P('shard'), may hold values from -0.125 to 0.125
- w_key: bfloat16 [2048, 2048], P('shard'), may hold values from -0.125 to 0.125
- w_value: bfloat16 [2048, 2048], P('shard'), may hold values from -0.125 to 0.125
- query_gain: bfloat16 [2048], P('shard'), may hold values from 0.5 to 1.5
- key_gain: bfloat16 [2048], P('shard'), may hold values from 0.5 to 1.5
- w_output: bfloat16 [2048, 2048], P('shard'), may hold values from -0.75 to 0.75
- moe_gain: bfloat16 [2048], P('shard'), may hold values from 0.5 to 1.5
- w_router: bfloat16 [2048, 16], P('shard'), may hold values from -0.0625 to 0.0625
- w_gate: bfloat16 [16, 2048, 1024], P('expert', None, 'shard'), may hold values from -0.125 to 0.125
- w_up: bfloat16 [16, 2048, 1024], P('expert', None, 'shard'), may hold values from -0.125 to 0.125
- w_down: bfloat16 [16, 1024, 2048], P('expert', 'shard'), may hold values from -3 to 3
- out_cotangent: float32 [8, 512, 2048], P('expert', 'shard'), may hold values from -6 to 6
Outputs:
- block_output: float32 [8, 512, 2048], P('expert', 'shard')
- grad_input: float32 [8, 512, 2048], P('expert', 'shard')
- grad_attn_gain: float32 [2048], P('shard')
- grad_w_query: float32 [2048, 2048], P('shard')
- grad_w_key: float32 [2048, 2048], P('shard')
- grad_w_value: float32 [2048, 2048], P('shard')
- grad_query_gain: float32 [2048], P('shard')
- grad_key_gain: float32 [2048], P('shard')
- grad_w_output: float32 [2048, 2048], P('shard')
- grad_moe_gain: float32 [2048], P('shard')
- grad_w_router: float32 [2048, 16], P('shard')
- grad_w_gate: float32 [16, 2048, 1024], P('expert', None, 'shard')
- grad_w_up: float32 [16, 2048, 1024], P('expert', None, 'shard')
- grad_w_down: float32 [16, 1024, 2048], P('expert', 'shard')
The draws below stay inside these ranges and needn't reach their ends.
Inputs may be any that keep to these rules, and one draw needn't show every extreme that they name: `expert_routes`: each row names 8 different experts. The rows of one device name any one expert at most 96 times, and in some device's rows some expert is named exactly 96 times. `segment_ids`: segment ids never fall along a group; each sequence has 128 to 384 tokens.
All inputs are finite; a program needn't handle non-finite values.
Results may differ from the reference program's by a relative error of at most 0.025.
Values may be sent and summed in bfloat16 or wider, within the bound.
No kernel may reach another device: no remote copies, remote signals or barrier semaphores. Data moves between devices by JAX's collectives and lax.ppermute only.
A program may use at most 448 MiB of HBM per device.

```python
import math
import jax
import jax.numpy as jnp
import numpy as np
from jax import lax

D = 2048
HEADS = 16
HEAD_DIM = 128
FFE = 1024
TOP = 8
EXP_DEV = 2
TOK_DEV = 128
SEGS = 2
GROUPS = 8
GROUP_TOK = 512
EXPERTS = 16
CAP = 96
SEG_MOST = 384
N_SHARD = 4
N_EXPERT = 8


def levels(key, dims, cuts, smallest, high):
    loudness = 1.0
    for axis_at, parts in cuts:
        draws = jax.random.uniform(jax.random.fold_in(jax.random.fold_in(key, 6), axis_at), (parts,), jnp.float32, smallest / len(cuts), high / len(cuts))
        loudness = loudness * jnp.repeat(jnp.exp(draws), dims[axis_at] // parts).reshape((-1,) + (1,) * (len(dims) - 1 - axis_at))
    return loudness


def length_profile(count, total, bound, skew):
    weights = [(1 << 20) // math.isqrt(grade ** skew) + 1 for grade in range(2, count + 1)]
    surplus, holding = total - bound - (count - 1), [1] * (count - 1)
    while surplus > 0:
        free = [i for i in range(count - 1) if holding[i] < bound]
        whole, budget = sum([weights[i] for i in free]), surplus
        for i in free:
            addition = min(bound - holding[i], max(1, budget * weights[i] // whole), surplus)
            holding[i] = holding[i] + addition
            surplus = surplus - addition
    return np.array([bound] + holding)


def ragged_sizes(rng, number_of, total, bound, lean):
    if number_of == 2:
        one = jax.random.randint(rng, (), max(1, total - bound), min(bound, total - 1) + 1)
        return jnp.stack([one, total - one])
    sizes = jnp.asarray(length_profile(number_of, total, bound, lean), jnp.int32)
    twos = (number_of - 1) // 2
    giver, sink = sizes[1:1 + 2 * twos:2], sizes[2:2 + 2 * twos:2]
    margin = jnp.minimum(giver - 1, bound - sink)
    moved = jax.random.randint(jax.random.fold_in(rng, 1), (twos,), 0, 1 << 20) % (margin + 1)
    sizes = sizes.at[1:1 + 2 * twos:2].set(giver - moved).at[2:2 + 2 * twos:2].set(sink + moved)
    return sizes[jax.random.permutation(jax.random.fold_in(rng, 2), number_of)]


def shared_out(own_key, own, number, rows, count, top, limit, lean):
    order = jax.random.permutation(own_key, count)
    heavy_load, usual = load_shares(count, rows * top, limit, lean, True), load_shares(count, rows * top, limit, lean, False)
    places = jnp.arange(count)

    def named(sizes, turn):
        used = int((sizes > 0).sum())
        fixed = max(1, used // 4)
        shifted = fixed + (places - fixed + turn * (used - fixed)) % max(1, count - fixed)
        return jnp.zeros((count,), jnp.int32).at[order[jnp.where(places < fixed, places, shifted)]].set(jnp.asarray(sizes, jnp.int32))

    sizes = jnp.where(number % 4 == 0, named(heavy_load, number // 4), named(usual, number - number // 4 - 1))
    mixed = jax.random.permutation(jax.random.fold_in(own, 3), count)
    source_of, receiver = mixed[0:count // 2 * 2:2], mixed[1:count // 2 * 2:2]
    slack = jnp.minimum(sizes[source_of] - 1, limit - sizes[receiver]) // 2
    slack = jnp.where((source_of == order[0]) | (receiver == order[0]) | (sizes[receiver] == 0), 0, jnp.maximum(slack, 0))
    shifted = jax.random.randint(jax.random.fold_in(own, 4), (count // 2,), 0, 1 << 20) % (slack + 1)
    sizes = sizes.at[source_of].add(-shifted).at[receiver].add(shifted)
    labels = jnp.searchsorted(jnp.cumsum(sizes), jnp.arange(rows * top), side="right").astype(jnp.int32)
    grid = labels.reshape(top, rows).T
    grid = grid[jax.random.permutation(jax.random.fold_in(own, 1), rows)]
    turn = jax.random.randint(jax.random.fold_in(own, 2), (rows, 1), 0, top)
    return jnp.take_along_axis(grid, (jnp.arange(top)[None, :] + turn) % top, axis=1)


def load_shares(number_of, total, most, skew, full):
    weights = [(1 << 20) // math.isqrt(grade ** skew) + 1 for grade in range(1, number_of + 1)]
    largest = most if full else min(most, max(-(-total // number_of), total * weights[0] // sum(weights)))
    least = 1 if total - largest >= number_of - 1 else 0
    counts, rest = [largest] + [least] * (number_of - 1), total - largest - least * (number_of - 1)
    while rest > 0:
        candidates = [i for i in range(1, number_of) if counts[i] < largest] or [i for i in range(1, number_of) if counts[i] < most]
        whole, budget = sum([weights[i] for i in candidates]), rest
        for i in candidates:
            addition = min(most - counts[i], max(1, budget * weights[i] // whole), rest)
            counts[i] = counts[i] + addition
            rest = rest - addition
    return np.array(counts)


def centred(key, extent, scale, bound, split=(), held_as=jnp.bfloat16):
    values = scale * jax.random.normal(key, extent, jnp.float32)
    if split:
        values = values * levels(key, extent, split, -0.22, 0.18)
    return jnp.clip(values, -bound, bound).astype(held_as)


def setup_inputs(seed: int = 0) -> dict:
    keys = jax.random.split(jax.random.key(seed), 17)
    block_input = centred(keys[0], (GROUPS, GROUP_TOK, D), 1.0, 6.0, ((0, 8), (1, 4)))
    segment_ids = jax.vmap(lambda own: jnp.searchsorted(jnp.cumsum(ragged_sizes(own, SEGS, GROUP_TOK, SEG_MOST, 2)), jnp.arange(GROUP_TOK), side="right"))(jax.random.split(keys[1], GROUPS)).reshape((GROUPS, GROUP_TOK)).astype(jnp.int32)
    expert_routes_keys = jax.random.split(jax.random.fold_in(keys[2], 1), GROUPS * GROUP_TOK // TOK_DEV)
    expert_routes_turns = jax.random.permutation(jax.random.fold_in(keys[2], 3), GROUPS * GROUP_TOK // TOK_DEV)
    expert_routes = jax.vmap(lambda own, number: shared_out(jax.random.fold_in(keys[2], 2), own, number, TOK_DEV, EXPERTS, TOP, CAP, 2))(expert_routes_keys, expert_routes_turns).reshape((GROUPS, GROUP_TOK, TOP))
    attn_gain = jnp.clip(1.0 + 0.1 * jax.random.normal(keys[3], (D,), jnp.float32), 0.5, 1.5).astype(jnp.bfloat16)
    w_query = centred(keys[4], (D, D), D ** -0.5, 0.125, ((0, 4),))
    w_key = centred(keys[5], (D, D), D ** -0.5, 0.125, ((0, 4),))
    w_value = centred(keys[6], (D, D), D ** -0.5, 0.125, ((0, 4),))
    query_gain = jnp.clip(1.0 + 0.1 * jax.random.normal(keys[7], (D,), jnp.float32), 0.5, 1.5).astype(jnp.bfloat16)
    key_gain = jnp.clip(1.0 + 0.1 * jax.random.normal(keys[8], (D,), jnp.float32), 0.5, 1.5).astype(jnp.bfloat16)
    w_output = centred(keys[9], (D, D), (D // 32) ** -0.5, 0.75, ((0, 4),))
    moe_gain = jnp.clip(1.0 + 0.1 * jax.random.normal(keys[10], (D,), jnp.float32), 0.5, 1.5).astype(jnp.bfloat16)
    w_router = centred(keys[11], (D, EXPERTS), (4 * D) ** -0.5, 0.0625, ((0, 4),))
    w_gate = centred(keys[12], (EXPERTS, D, FFE), D ** -0.5, 0.125, ((0, 8), (2, 4)))
    w_up = centred(keys[13], (EXPERTS, D, FFE), D ** -0.5, 0.125, ((0, 8), (2, 4)))
    w_down = centred(keys[14], (EXPERTS, FFE, D), (max(1, FFE // 256)) ** -0.5, 3.0, ((0, 8), (1, 4)))
    out_cotangent = centred(keys[15], (GROUPS, GROUP_TOK, D), 1.0, 6.0, ((0, 8), (1, 4)), jnp.float32)
    return dict(block_input=block_input, segment_ids=segment_ids, expert_routes=expert_routes, attn_gain=attn_gain, w_query=w_query, w_key=w_key, w_value=w_value, query_gain=query_gain, key_gain=key_gain, w_output=w_output, moe_gain=moe_gain, w_router=w_router, w_gate=w_gate, w_up=w_up, w_down=w_down, out_cotangent=out_cotangent)


epsilon = 1e-05

def rms_scale(values):
    return lax.rsqrt(lax.optimization_barrier(jnp.mean(values * values, axis=-1, keepdims=True)) + epsilon)

def rope_tables(positions):
    half_dim = HEAD_DIM // 2
    inverse = 10000.0 ** (-(jnp.arange(half_dim).astype(jnp.float32) * 2.0) / HEAD_DIM)
    angles = positions[:, None] * inverse[None, :]
    cosine = jnp.concatenate([jnp.cos(angles), jnp.cos(angles)], axis=-1)[:, None, :]
    sine_part = jnp.concatenate([jnp.sin(angles), jnp.sin(angles)], axis=-1)[:, None, :]
    return (cosine, sine_part)

def rope_apply(values, cosine, sine_part):
    half_dim = values.shape[-1] // 2
    turned = jnp.concatenate([-values[..., half_dim:], values[..., :half_dim]], axis=-1)
    return values * cosine + turned * sine_part

def rope_back(grad_values, cosine, sine_part):
    half_dim = grad_values.shape[-1] // 2
    scaled = grad_values * sine_part
    turned = jnp.concatenate([scaled[..., half_dim:], -scaled[..., :half_dim]], axis=-1)
    return grad_values * cosine + turned

def norm_back(grad_out, source, scale_now, gain_now):
    weighted = grad_out * gain_now
    inner_mean = lax.optimization_barrier(jnp.mean(weighted * source, axis=-1, keepdims=True))
    grad_source = scale_now * (weighted - source * scale_now * scale_now * inner_mean)
    grad_gain = lax.optimization_barrier(jnp.sum(grad_out * source * scale_now, axis=0))
    return (grad_source, grad_gain)

def masked_scores(q_heads, k_heads, allowed):
    raw_scores = jnp.einsum('qhd,khd->hqk', q_heads.astype(jnp.float32), k_heads.astype(jnp.float32)) * HEAD_DIM ** (-0.5)
    return jnp.where(allowed[None], raw_scores, -1e+30)

def attn_front(x_group, seg_group, weights):
    attn_gain, w_query, w_key, w_value, query_gain, key_gain = weights
    row_count = x_group.shape[0]
    source = x_group.astype(jnp.float32)
    scale_one = rms_scale(source)
    normed = (source * scale_one * attn_gain.astype(jnp.float32)).astype(jnp.bfloat16)
    q_proj = jnp.dot(normed, w_query, preferred_element_type=jnp.float32)
    k_proj = jnp.dot(normed, w_key, preferred_element_type=jnp.float32)
    v_heads = jnp.dot(normed, w_value, preferred_element_type=jnp.float32).astype(jnp.bfloat16).reshape(row_count, HEADS, HEAD_DIM)
    q_scale = rms_scale(q_proj)
    k_scale = rms_scale(k_proj)
    positions = jnp.arange(row_count).astype(jnp.float32)
    cosine, sine_part = rope_tables(positions)
    q_heads = rope_apply((q_proj * q_scale * query_gain.astype(jnp.float32)).reshape(row_count, HEADS, HEAD_DIM), cosine, sine_part).astype(jnp.bfloat16)
    k_heads = rope_apply((k_proj * k_scale * key_gain.astype(jnp.float32)).reshape(row_count, HEADS, HEAD_DIM), cosine, sine_part).astype(jnp.bfloat16)
    index_row = jnp.arange(row_count)
    allowed = (seg_group[:, None] == seg_group[None, :]) & (index_row[None, :] <= index_row[:, None])
    scores = masked_scores(q_heads, k_heads, allowed)
    top_score = lax.optimization_barrier(jnp.max(scores, axis=-1, keepdims=True))
    log_total = top_score + jnp.log(lax.optimization_barrier(jnp.sum(jnp.exp(scores - top_score), axis=-1, keepdims=True)))
    probs_b = jnp.exp(scores - log_total).astype(jnp.bfloat16)
    attended = jnp.einsum('hqk,khd->qhd', probs_b.astype(jnp.float32), v_heads.astype(jnp.float32)).reshape(row_count, HEADS * HEAD_DIM).astype(jnp.bfloat16)
    return (source, scale_one, normed, q_proj, q_scale, k_proj, k_scale, cosine, sine_part, q_heads, k_heads, v_heads, allowed, log_total, probs_b, attended)

def reference(block_input, segment_ids, expert_routes, attn_gain, w_query, w_key, w_value, query_gain, key_gain, w_output, moe_gain, w_router, w_gate, w_up, w_down, out_cotangent):
    experts_all = EXP_DEV * N_EXPERT
    slot_limit = N_SHARD * N_EXPERT * CAP
    front_weights = (attn_gain, w_query, w_key, w_value, query_gain, key_gain)

    def forward_group(group_pair):
        pieces = attn_front(group_pair[0], group_pair[1], front_weights)
        return pieces[0] + jnp.dot(pieces[-1], w_output, preferred_element_type=jnp.float32)
    residual = lax.map(forward_group, (block_input, segment_ids)).reshape(-1, D)
    token_count = residual.shape[0]
    scale_two = rms_scale(residual)
    mixed_in = (residual * scale_two * moe_gain.astype(jnp.float32)).astype(jnp.bfloat16)
    logits = jnp.dot(mixed_in, w_router, preferred_element_type=jnp.float32)
    powers = jnp.exp(logits)
    router_probs = powers / lax.optimization_barrier(jnp.sum(powers, axis=-1, keepdims=True))
    routes = expert_routes.reshape(-1, TOP)
    one_hot = (routes[:, :, None] == jnp.arange(experts_all)[None, None, :]).astype(jnp.float32)
    chosen = lax.optimization_barrier(jnp.sum(router_probs[:, None, :] * one_hot, axis=-1))
    cotangent = out_cotangent.reshape(-1, D)
    flat_routes = routes.reshape(-1)
    flat_chosen = chosen.reshape(-1)

    def expert_step(totals_now, inputs):
        mixture, back_sum, chosen_grad = totals_now
        expert_id, gate_w, up_w, down_w = inputs
        route_hits = flat_routes == expert_id
        picked = jnp.nonzero(route_hits, size=slot_limit, fill_value=0)[0].astype(jnp.int32)
        live_rows = (jnp.arange(slot_limit) < jnp.sum(route_hits.astype(jnp.int32))).astype(jnp.float32)
        token_index = (picked // TOP).astype(jnp.int32)
        entries = mixed_in[token_index]
        gate_pre = jnp.dot(entries, gate_w, preferred_element_type=jnp.float32)
        up_pre = jnp.dot(entries, up_w, preferred_element_type=jnp.float32)
        sigmoid_gate = jax.nn.sigmoid(gate_pre)
        silu_gate = gate_pre * sigmoid_gate
        hidden_b = (silu_gate * up_pre).astype(jnp.bfloat16)
        y_float = jnp.dot(hidden_b, down_w, preferred_element_type=jnp.float32).astype(jnp.bfloat16).astype(jnp.float32)
        weight_now = flat_chosen[picked] * live_rows
        cot_rows = cotangent[token_index]
        mixture = mixture.at[token_index].add(weight_now[:, None] * y_float)
        chosen_grad = chosen_grad.at[picked].add(lax.optimization_barrier(jnp.sum(cot_rows * y_float, axis=-1)) * live_rows)
        grad_rows = (weight_now[:, None] * cot_rows).astype(jnp.bfloat16)
        grad_down = jnp.dot(hidden_b.T, grad_rows, preferred_element_type=jnp.float32)
        grad_hidden = jnp.dot(grad_rows, down_w.T, preferred_element_type=jnp.float32)
        gate_grad_b = (grad_hidden * up_pre * sigmoid_gate * (1.0 + gate_pre * (1.0 - sigmoid_gate))).astype(jnp.bfloat16)
        up_grad_b = (grad_hidden * silu_gate).astype(jnp.bfloat16)
        grad_gate = jnp.dot(entries.T, gate_grad_b, preferred_element_type=jnp.float32)
        grad_up = jnp.dot(entries.T, up_grad_b, preferred_element_type=jnp.float32)
        back_rows = (jnp.dot(gate_grad_b, gate_w.T, preferred_element_type=jnp.float32) + jnp.dot(up_grad_b, up_w.T, preferred_element_type=jnp.float32)).astype(jnp.bfloat16)
        back_sum = back_sum.at[token_index].add(back_rows.astype(jnp.float32) * live_rows[:, None])
        return ((mixture, back_sum, chosen_grad), (grad_gate, grad_up, grad_down))
    start_totals = (jnp.zeros((token_count, D), jnp.float32), jnp.zeros((token_count, D), jnp.float32), jnp.zeros((token_count * TOP,), jnp.float32))
    expert_inputs = (jnp.arange(experts_all).astype(jnp.int32), w_gate, w_up, w_down)
    (mixture, back_sum, chosen_grad), expert_grads = lax.scan(expert_step, start_totals, expert_inputs)
    grad_w_gate, grad_w_up, grad_w_down = expert_grads
    block_output = residual + mixture
    prob_grad = lax.optimization_barrier(jnp.sum(chosen_grad.reshape(token_count, TOP)[:, :, None] * one_hot, axis=1))
    logit_grad = (router_probs * (prob_grad - lax.optimization_barrier(jnp.sum(router_probs * prob_grad, axis=-1, keepdims=True)))).astype(jnp.bfloat16)
    grad_w_router = jnp.dot(mixed_in.T, logit_grad, preferred_element_type=jnp.float32)
    mixed_grad = back_sum + jnp.dot(logit_grad, w_router.T, preferred_element_type=jnp.float32)
    residual_norm_grad, grad_moe_gain = norm_back(mixed_grad, residual, scale_two, moe_gain.astype(jnp.float32))
    residual_grad = cotangent + residual_norm_grad

    def backward_group(totals_now, inputs):
        x_group, seg_group, grad_group = inputs
        source, scale_one, normed, q_proj, q_scale, k_proj, k_scale, cosine, sine_part, q_heads, k_heads, v_heads, allowed, log_total, probs_b, attended = attn_front(x_group, seg_group, front_weights)
        row_count = x_group.shape[0]
        grad_b = grad_group.astype(jnp.bfloat16)
        grad_output_w = jnp.dot(attended.T, grad_b, preferred_element_type=jnp.float32)
        attended_grad = jnp.dot(grad_b, w_output.T, preferred_element_type=jnp.float32).astype(jnp.bfloat16).reshape(row_count, HEADS, HEAD_DIM)
        probs_full = jnp.exp(masked_scores(q_heads, k_heads, allowed) - log_total)
        delta_rows = jnp.einsum('qhd,qhd->hq', attended_grad.astype(jnp.float32), attended.reshape(row_count, HEADS, HEAD_DIM).astype(jnp.float32))
        prob_value = jnp.einsum('qhd,khd->hqk', attended_grad.astype(jnp.float32), v_heads.astype(jnp.float32))
        score_grad = (probs_full * (prob_value - delta_rows[:, :, None])).astype(jnp.bfloat16)
        query_grad = jnp.einsum('hqk,khd->qhd', score_grad.astype(jnp.float32), k_heads.astype(jnp.float32)) * HEAD_DIM ** (-0.5)
        key_grad = jnp.einsum('hqk,qhd->khd', score_grad.astype(jnp.float32), q_heads.astype(jnp.float32)) * HEAD_DIM ** (-0.5)
        value_grad = jnp.einsum('hqk,qhd->khd', probs_b.astype(jnp.float32), attended_grad.astype(jnp.float32)).reshape(row_count, D).astype(jnp.bfloat16)
        query_pre = rope_back(query_grad, cosine, sine_part).reshape(row_count, D)
        key_pre = rope_back(key_grad, cosine, sine_part).reshape(row_count, D)
        q_proj_grad, grad_gain_query = norm_back(query_pre, q_proj, q_scale, query_gain.astype(jnp.float32))
        k_proj_grad, grad_gain_key = norm_back(key_pre, k_proj, k_scale, key_gain.astype(jnp.float32))
        q_grad_b = q_proj_grad.astype(jnp.bfloat16)
        k_grad_b = k_proj_grad.astype(jnp.bfloat16)
        grad_query_w = jnp.dot(normed.T, q_grad_b, preferred_element_type=jnp.float32)
        grad_key_w = jnp.dot(normed.T, k_grad_b, preferred_element_type=jnp.float32)
        grad_value_w = jnp.dot(normed.T, value_grad, preferred_element_type=jnp.float32)
        normed_grad = jnp.dot(q_grad_b, w_query.T, preferred_element_type=jnp.float32) + jnp.dot(k_grad_b, w_key.T, preferred_element_type=jnp.float32) + jnp.dot(value_grad, w_value.T, preferred_element_type=jnp.float32)
        input_norm_grad, grad_gain_one = norm_back(normed_grad, source, scale_one, attn_gain.astype(jnp.float32))
        updates = (grad_gain_one, grad_query_w, grad_key_w, grad_value_w, grad_gain_query, grad_gain_key, grad_output_w)
        totals_next = tuple((before + after for before, after in zip(totals_now, updates)))
        return (totals_next, grad_group + input_norm_grad)
    start_grads = (jnp.zeros((D,), jnp.float32), jnp.zeros((D, D), jnp.float32), jnp.zeros((D, D), jnp.float32), jnp.zeros((D, D), jnp.float32), jnp.zeros((D,), jnp.float32), jnp.zeros((D,), jnp.float32), jnp.zeros((D, D), jnp.float32))
    group_grads = residual_grad.reshape(block_input.shape)
    attn_totals, grad_input = lax.scan(backward_group, start_grads, (block_input, segment_ids, group_grads))
    grad_attn_gain, grad_w_query, grad_w_key, grad_w_value, grad_query_gain, grad_key_gain, grad_w_output = attn_totals
    return (block_output.reshape(block_input.shape), grad_input, grad_attn_gain, grad_w_query, grad_w_key, grad_w_value, grad_query_gain, grad_key_gain, grad_w_output, grad_moe_gain, grad_w_router, grad_w_gate, grad_w_up, grad_w_down)
```

```python
import jax
import jax.numpy as jnp
from jax import lax
from jax.experimental import pallas as pl
from jax.experimental.pallas import tpu as pltpu
from jax.sharding import PartitionSpec as P

HEAD_DIM = 128
LANES = 128
EPSILON = 1e-05
SCORE_SCALE = HEAD_DIM ** (-0.5)
F32 = jnp.float32
BF16 = jnp.bfloat16
ORDER = (((0, 0), (0, 1)), ((0, 2), (0, 3)), ((1, 0), (1, 2)), ((1, 1), (1, 3)))


def dot(a, b):
    return jnp.dot(a, b, preferred_element_type=F32)


def dot_t(a, b):
    return lax.dot_general(a, b, (((1,), (1,)), ((), ())), preferred_element_type=F32)


def t_dot(a, b):
    return lax.dot_general(a, b, (((0,), (0,)), ((), ())), preferred_element_type=F32)


def flip_shard(values, bit):
    count = lax.axis_size("shard")
    return lax.ppermute(values, "shard", [(i, i ^ bit) for i in range(count)])


def swap_x(values):
    return flip_shard(values, 1)


def swap_y(values):
    return flip_shard(values, 2)


def swap_far(values):
    return flip_shard(values, 3)


def flip_expert(values, bit):
    count = lax.axis_size("expert")
    return lax.ppermute(values, "expert", [(i, i ^ bit) for i in range(count)])


def swap_core(values):
    return flip_expert(values, 1)


def ring_up(values):
    count = lax.axis_size("expert")
    return lax.ppermute(values, "expert", [(i, (i + 2) % count) for i in range(count)])


def after(values, *others):
    return lax.optimization_barrier((values, others))[0]


def spread_xy(first, second):
    pair_a = jnp.stack([first, swap_x(first)])
    pair_b = jnp.stack([second, swap_y(second)])
    return [pair_a, swap_y(pair_a), pair_b, swap_x(pair_b)]


def reduce_xy(blocks):
    keep_a, send_a, keep_b, send_b = blocks
    got_a, got_b = swap_y(send_a), swap_x(send_b)
    far_a = swap_x((keep_a[1].astype(F32) + got_a[1].astype(F32)).astype(BF16))
    far_b = swap_y((keep_b[1].astype(F32) + got_b[1].astype(F32)).astype(BF16))
    return (keep_a[0], got_a[0], far_a), (keep_b[0], got_b[0], far_b)


def total_of(terms):
    total = terms[0].astype(F32)
    for term in terms[1:]:
        total = total + term.astype(F32)
    return total


def exchange_blocks(for_x, for_y):
    got_x, got_y = swap_x(for_x), swap_y(for_y)
    depth = 2 * for_x.shape[0] // 3
    far = jnp.concatenate([swap_y(got_x[depth:]), swap_x(got_y[depth:])], axis=0)
    return [got_x[:depth], got_y[:depth], far]


def gather_parts(part):
    return [part, swap_x(part), swap_y(part), swap_far(part)]


def ring_gather(piece):
    pieces = [piece]
    for _ in range(lax.axis_size("expert") // 2 - 1):
        pieces.append(ring_up(pieces[-1]))
    return pieces


def ring_sum(pieces):
    chips = lax.axis_size("expert") // 2
    total = pieces(1).astype(BF16)
    for j in range(2, chips):
        total = (ring_up(total).astype(F32) + pieces(j).astype(F32)).astype(BF16)
    return ring_up(total), pieces(0)


def expert_sum(own, chip):
    chips = lax.axis_size("expert") // 2
    parts, rows, columns = own.shape
    split = own.reshape(parts, chips, rows // chips, columns)

    def piece(j):
        at = lax.rem(chip + chips - j, chips)
        return lax.dynamic_index_in_dim(split, at, 1, keepdims=False)

    total, mine = ring_sum(piece)
    return (total.astype(F32) + mine).astype(BF16)


def expert_spread(piece, core, chip):
    chips = lax.axis_size("expert") // 2
    parts, rows, columns = piece.shape
    spread = jnp.zeros((parts, chips, rows, columns), piece.dtype)
    for j, got in enumerate(ring_gather(piece)):
        spread = lax.dynamic_update_slice_in_dim(
            spread, got[:, None], lax.rem(chip + chips - j, chips), 1
        )
    half = spread.reshape(parts, 1, chips * rows, columns)
    other = swap_core(half)
    first = jnp.where(core == 0, half, other)
    second = jnp.where(core == 0, other, half)
    return jnp.concatenate([first, second], axis=1).reshape(parts, 2 * chips * rows, columns)


def rms_scale(values):
    return lax.rsqrt(jnp.mean(values * values, axis=-1, keepdims=True) + EPSILON)


def norm_back(grad_out, source, scale_now, gain_now):
    weighted = grad_out * gain_now
    inner_mean = jnp.mean(weighted * source, axis=-1, keepdims=True)
    grad_source = scale_now * (weighted - source * scale_now * scale_now * inner_mean)
    grad_gain = jnp.sum(grad_out * source * scale_now, axis=0, keepdims=True)
    return (grad_source, grad_gain)


def whole(shape):
    return pl.BlockSpec(shape, lambda *_: (0,) * len(shape))


def scalars():
    return pl.BlockSpec(memory_space=pltpu.SMEM)


def call(kernel, name, args, outs, flops, smem=(), transcendentals=0):
    moved = sum(a.size * a.dtype.itemsize for a in args) + sum(
        o.size * o.dtype.itemsize for o in outs
    )
    return pl.pallas_call(
        kernel,
        in_specs=[scalars() if n in smem else whole(a.shape) for n, a in enumerate(args)],
        out_specs=[whole(o.shape) for o in outs],
        out_shape=outs,
        cost_estimate=pl.CostEstimate(
            flops=flops, bytes_accessed=moved, transcendentals=transcendentals
        ),
        name=name,
    )(*args)


def out(shape, dtype):
    return jax.ShapeDtypeStruct(shape, dtype)


def pack_stats(first, second):
    rows = first.shape[0]
    lane = lax.broadcasted_iota(jnp.int32, (rows, LANES), 1)
    spread = jnp.where(lane == 0, first, jnp.where(lane == 1, second, 0.0))
    return [spread[n : n + LANES].T[:8] for n in range(0, rows, LANES)]


def sum_stats(mine, from_x, from_y, far):
    def turn(values):
        return pltpu.roll(values, LANES // 2, 1)

    totals = [
        mine[0] + turn(from_x[0]) + from_y[1] + turn(far[1]),
        mine[1] + turn(from_x[1]) + from_y[0] + turn(far[0]),
        mine[2] + from_x[3] + turn(from_y[2]) + turn(far[3]),
        mine[3] + from_x[2] + turn(from_y[3]) + turn(far[2]),
    ]
    pad = jnp.zeros((LANES - 8, LANES), F32)
    return jnp.concatenate([jnp.concatenate([t, pad], axis=0).T for t in totals], axis=0)


def project_kernel(
    at_ref, r0, r1, r2, r3, gain_ref, *refs
):
    weight_refs, (normed_ref, proj_ref, stats_ref, scale_ref) = refs[:8], refs[8:]
    part = proj_ref.shape[1] // 3
    for n, ref in enumerate((r0, r1, r2, r3)):
        source = ref[...].reshape(LANES, ref.shape[2]).astype(F32)
        scale = rms_scale(source)
        rows = slice(n * LANES, (n + 1) * LANES)
        normed_ref[rows, :] = (source * scale * gain_ref[...]).astype(BF16)
        scale_ref[rows, :] = jnp.broadcast_to(scale, (LANES, LANES))
    depth = weight_refs[0].shape[0]
    for third in range(3):
        cols = slice(third * part, (third + 1) * part)
        total = None
        for n, ref in enumerate(weight_refs):
            rows = pl.ds(pl.multiple_of(at_ref[n] * depth, depth), depth)
            more = dot(normed_ref[:, rows], ref[:, cols])
            total = more if total is None else total + more
        proj_ref[:, cols] = total
    q_proj, k_proj = proj_ref[:, :part], proj_ref[:, part : 2 * part]
    packed = pack_stats(
        jnp.sum(q_proj * q_proj, axis=-1, keepdims=True),
        jnp.sum(k_proj * k_proj, axis=-1, keepdims=True),
    )
    for n, stats in enumerate(packed):
        stats_ref[n] = stats


def attend_kernel(
    width, proj_ref, s0, s1, s2, s3, gain_q_ref, gain_k_ref, cos_ref, sin_ref, bias_ref, w_ref, *refs
):
    q_ref, k_ref, v_ref, lse_ref, scales_ref, attended_ref = refs[:6]
    part_refs = refs[6:]
    part = w_ref.shape[0]
    rows = proj_ref.shape[0]
    sums = sum_stats(s0, s1, s2, s3)
    scales = lax.rsqrt(sums / width + EPSILON)
    scales_ref[...] = scales
    lane = lax.broadcasted_iota(jnp.int32, (rows, LANES), 1)
    q_scale, k_scale = scales[:, 0:1], scales[:, 1:2]
    cosine, sine_part = cos_ref[...], sin_ref[...]
    lse_all = jnp.zeros((rows, LANES), F32)
    for h in range(part // HEAD_DIM):
        cols = slice(h * HEAD_DIM, (h + 1) * HEAD_DIM)
        k_cols = slice(part + h * HEAD_DIM, part + (h + 1) * HEAD_DIM)
        v_cols = slice(2 * part + h * HEAD_DIM, 2 * part + (h + 1) * HEAD_DIM)
        query = proj_ref[:, cols] * q_scale * gain_q_ref[:, cols]
        key = proj_ref[:, k_cols] * k_scale * gain_k_ref[:, cols]
        query = (query * cosine + pltpu.roll(query, HEAD_DIM // 2, 1) * sine_part).astype(BF16)
        key = (key * cosine + pltpu.roll(key, HEAD_DIM // 2, 1) * sine_part).astype(BF16)
        value = proj_ref[:, v_cols].astype(BF16)
        q_ref[:, cols] = query
        k_ref[:, cols] = key
        v_ref[:, cols] = value
        scores = dot_t(query, key) * SCORE_SCALE + bias_ref[...]
        top = jnp.max(scores, axis=-1, keepdims=True)
        powers = jnp.exp(scores - top)
        total = jnp.sum(powers, axis=-1, keepdims=True)
        lse_all = jnp.where(lane == h, top + jnp.log(total), lse_all)
        attended_ref[:, cols] = dot((powers / total).astype(BF16), value).astype(BF16)
    lse_ref[...] = lse_all
    step = 512
    for c in range(w_ref.shape[1] // step):
        cols = slice(c * step, (c + 1) * step)
        for n, ref in enumerate(part_refs):
            got = dot(attended_ref[n * LANES : (n + 1) * LANES, :], w_ref[:, cols])
            ref[:, :, cols] = got.astype(BF16).reshape(2, LANES // 2, step)


def settle_kernel(x_ref, a0, a1, a2, b0, b1, b2, gain_ref, residual_ref, mixed_ref):
    for n, refs in enumerate(((a0, a1, a2), (b0, b1, b2))):
        residual = x_ref[n].astype(F32) + total_of([r[...] for r in refs])
        residual_ref[n] = residual
        mixed_ref[n] = (residual * rms_scale(residual) * gain_ref[...]).astype(BF16)


def flip_kernel(gate_ref, up_ref, down_ref, gate_up_t_ref, down_t_ref):
    unit_part = gate_ref.shape[2]
    for e in range(2):
        low = e * unit_part
        gate_up_t_ref[low : low + unit_part, :] = gate_ref[e].T
        gate_up_t_ref[2 * unit_part + low : 2 * unit_part + low + unit_part, :] = up_ref[e].T
        down_t_ref[:, low : low + unit_part] = down_ref[e].T


def flip_call(w_gate, w_up, w_down):
    two, width, unit_part = w_gate.shape
    step = 512
    tall = pl.BlockSpec((two, step, unit_part), lambda i: (0, i, 0))
    return pl.pallas_call(
        flip_kernel,
        grid=(width // step,),
        in_specs=[tall, tall, pl.BlockSpec((two, unit_part, step), lambda i: (0, 0, i))],
        out_specs=[
            pl.BlockSpec((4 * unit_part, step), lambda i: (0, i)),
            pl.BlockSpec((step, 2 * unit_part), lambda i: (i, 0)),
        ],
        out_shape=[out((4 * unit_part, width), BF16), out((width, 2 * unit_part), BF16)],
        cost_estimate=pl.CostEstimate(flops=0, bytes_accessed=12 * w_gate.size, transcendentals=0),
        name="flip",
    )(w_gate, w_up, w_down)


def lead_kernel(cot_ref, down_t_ref, lead_ref):
    width = down_t_ref.shape[0]
    count = lead_ref.shape[1]
    cot = cot_ref[...].reshape(count, cot_ref.shape[4])[:, :width]
    lead_ref[0] = dot(cot, down_t_ref[...])


def lead_call(cot, down_t):
    shards, chips, two, rows, columns = cot.shape
    width, units = down_t.shape
    count = shards * two * rows
    return pl.pallas_call(
        lead_kernel,
        grid=(chips,),
        in_specs=[
            pl.BlockSpec((shards, 1, two, rows, columns), lambda i: (0, i, 0, 0, 0)),
            whole(down_t.shape),
        ],
        out_specs=pl.BlockSpec((1, count, units), lambda i: (i, 0, 0)),
        out_shape=out((chips, count, units), F32),
        cost_estimate=pl.CostEstimate(
            flops=2 * chips * count * down_t.size,
            bytes_accessed=2 * cot.size + 4 * chips * count * units + 2 * down_t.size,
            transcendentals=0,
        ),
        name="lead",
    )(cot, down_t)


def expert_kernel(m, experts_all, at_ref, *refs):
    row_refs = refs[: 8 * m]
    routed_refs, lead_refs = refs[8 * m : 8 * m + 2], refs[8 * m + 2 : 8 * m + 4]
    gate_ref, up_ref, gate_up_t_ref, router_ref = refs[8 * m + 4 : 8 * m + 8]
    own_refs, other_ref, grads_ref, scaled_out = (
        refs[8 * m + 8 : 8 * m + 12],
        refs[8 * m + 12],
        refs[8 * m + 13],
        refs[8 * m + 14],
    )
    rows_ref, routed_ref, lead_ref, scaled_ref = refs[8 * m + 15 :]
    width = router_ref.shape[0]
    units = lead_ref.shape[1]
    unit_part = units // 2
    half = LANES // 2
    me = at_ref[1]
    now = pl.program_id(0)
    blocks = [block for pair in ORDER for block in pair]
    for side in range(2):
        for j in range(m):

            @pl.when(now == side * m + j)
            def _():
                for n in range(4):
                    ref = row_refs[(side * m + j) * 4 + n]
                    rows_ref[n * LANES : (n + 1) * LANES, :] = ref[...].reshape(LANES, width)

        @pl.when(now // m == side)
        def _():
            for n, (part, d) in enumerate(blocks):
                to = slice(n * half, (n + 1) * half)
                routed_ref[to, :] = routed_refs[side][me ^ d, 0, part]
                lead_ref[to, :] = lead_refs[side][0, 2 * (me ^ d) + part]

    rows = rows_ref[...]
    count = rows.shape[0]
    lane = lax.broadcasted_iota(jnp.int32, (count, LANES), 1)
    routed = routed_ref[...].astype(F32)
    powers = jnp.where(lane < experts_all, jnp.exp(dot(rows, router_ref[...])), 0.0)
    weights = powers * routed / jnp.sum(powers, axis=-1, keepdims=True)
    spot = jnp.zeros((count, LANES), F32)
    for e in range(2):
        here = (lane == at_ref[0] * 2 + e).astype(F32)
        chosen = jnp.sum(weights * here, axis=-1, keepdims=True)
        low = e * unit_part
        gate_pre = dot(rows, gate_ref[e])
        up_pre = dot(rows, up_ref[e])
        lead = lead_ref[:, low : low + unit_part]
        sigmoid_gate = 1.0 / (1.0 + jnp.exp(-gate_pre))
        silu_gate = gate_pre * sigmoid_gate
        hidden = (silu_gate * up_pre).astype(BF16).astype(F32)
        spot = spot + jnp.sum(hidden * lead, axis=-1, keepdims=True) * (here * routed)
        grad_hidden = lead * chosen
        gate_grad = grad_hidden * up_pre * sigmoid_gate * (1.0 + gate_pre * (1.0 - sigmoid_gate))
        grads_ref[0, :, low : low + unit_part] = gate_grad.astype(BF16)
        grads_ref[0, :, units + low : units + low + unit_part] = (grad_hidden * silu_gate).astype(
            BF16
        )
        scaled_ref[:, low : low + unit_part] = (hidden * chosen).astype(BF16)
    for n, (part, d) in enumerate(blocks):
        scaled_out[0, 2 * (me ^ d) + part] = scaled_ref[n * half : (n + 1) * half, :]
    spot = spot.astype(BF16)
    step = 512
    parts = [
        dot(grads_ref[0], gate_up_t_ref[:, c * step : (c + 1) * step]).astype(BF16)
        for c in range(width // step)
    ]

    @pl.when(now < m)
    def _():
        for n, ref in enumerate(own_refs):
            at = slice(n * LANES, (n + 1) * LANES)
            ref[:, 0, :, width:] = spot[at].reshape(2, half, LANES)
            for c in range(width // step):
                ref[:, 0, :, c * step : (c + 1) * step] = parts[c][at].reshape(2, half, step)

    @pl.when(now >= m)
    def _():
        for n in range(4):
            at = slice(n * LANES, (n + 1) * LANES)
            other_ref[n, :, 0, :, width:] = spot[at].reshape(2, half, LANES)
            for c in range(width // step):
                other_ref[n, :, 0, :, c * step : (c + 1) * step] = parts[c][at].reshape(
                    2, half, step
                )


def expert_call(at, rows, cots, first, leads, w_gate, w_up, gate_up_t, router, experts_all):
    m = len(rows[0])
    two, half, width = rows[0][0][0].shape
    shards, _, _, _, columns = cots[0].shape
    units = leads[0].shape[2]
    count = 8 * half
    leads = [v.reshape(v.shape[0], 8, half, units) for v in leads]
    own_shape = (two, m, half, width + LANES)
    flat = [array for side in rows for chip_rows in side for array in chip_rows]

    def where(side, i):
        return jnp.minimum(i, m - 1) if side == 0 else jnp.maximum(i - m, 0)

    def routed_spec(side):
        return pl.BlockSpec(
            (shards, 1, two, half, LANES),
            lambda i, _: (0, where(side, i) + first, 0, 0, width // LANES),
        )

    def lead_spec(side):
        return pl.BlockSpec((1, 8, half, units), lambda i, _: (where(side, i) + first, 0, 0, 0))

    return pl.pallas_call(
        lambda *refs: expert_kernel(m, experts_all, *refs),
        grid_spec=pltpu.PrefetchScalarGridSpec(
            num_scalar_prefetch=1,
            grid=(2 * m,),
            in_specs=[
                pl.BlockSpec(a.shape, lambda i, _: (0, 0, 0), pipeline_mode=pl.Buffered(1))
                for a in flat
            ]
            + [routed_spec(0), routed_spec(1), lead_spec(0), lead_spec(1)]
            + [whole(w_gate.shape), whole(w_up.shape), whole(gate_up_t.shape), whole(router.shape)],
            out_specs=[
                pl.BlockSpec(
                    (two, 1, half, width + LANES), lambda i, _: (0, where(0, i), 0, 0)
                )
                for _ in range(4)
            ]
            + [
                pl.BlockSpec(
                    (4, two, 1, half, width + LANES), lambda i, _: (0, 0, where(1, i), 0, 0)
                ),
                pl.BlockSpec((1, count, 2 * units), lambda i, _: (i, 0, 0)),
                pl.BlockSpec((1, 8, half, units), lambda i, _: (i, 0, 0, 0)),
            ],
            scratch_shapes=[
                pltpu.VMEM((count, width), BF16),
                pltpu.VMEM((count, LANES), BF16),
                pltpu.VMEM((count, units), F32),
                pltpu.VMEM((count, units), BF16),
            ],
        ),
        out_shape=[out(own_shape, BF16)] * 4
        + [
            out((4,) + own_shape, BF16),
            out((2 * m, count, 2 * units), BF16),
            out((2 * m, 8, half, units), BF16),
        ],
        compiler_params=pltpu.CompilerParams(vmem_limit_bytes=48 << 20),
        cost_estimate=pl.CostEstimate(
            flops=8 * m * count * gate_up_t.size,
            bytes_accessed=8 * m * count * width + 4 * gate_up_t.size + 20 * m * count * units,
            transcendentals=2 * m * count * units,
        ),
        name="experts",
    )(at, *flat, *cots, *leads, w_gate, w_up, gate_up_t, router)


def mix_kernel(scaled_ref, down_ref, *refs):
    out_ref = refs[-1]
    width = down_ref.shape[1]
    shards, _, rows, _ = out_ref.shape
    step = 512
    for c in range(width // step):
        cols = slice(c * step, (c + 1) * step)
        part = dot(scaled_ref[0], down_ref[:, cols]).reshape(shards, rows, step)
        if len(refs) == 2:
            part = part + refs[0][:, 0, :, cols].astype(F32)
        out_ref[:, 0, :, cols] = part.astype(BF16)


def mix_call(scaled, down, shards, *others):
    chips, count, units = scaled.shape
    width = down.shape[1]
    rows = count // shards
    result = pl.BlockSpec((shards, 1, rows, width), lambda i: (0, i, 0, 0))
    return pl.pallas_call(
        mix_kernel,
        grid=(chips,),
        in_specs=[pl.BlockSpec((1, count, units), lambda i: (i, 0, 0)), whole(down.shape)]
        + [result] * len(others),
        out_specs=result,
        out_shape=out((shards, chips, rows, width), BF16),
        cost_estimate=pl.CostEstimate(
            flops=2 * scaled.size * width,
            bytes_accessed=2 * scaled.size + 2 * down.size + 4 * chips * count * width,
            transcendentals=0,
        ),
        name="mix",
    )(scaled, down, *others)


def row_grad_kernel(plan, grad_columns, *refs):
    out_ref = refs[-1]
    _, step, unit_part = out_ref.shape
    total = jnp.zeros((step, 2 * unit_part), F32)
    for row_at, grads_at, k in plan:
        rows = jnp.concatenate([refs[n][...].reshape(LANES, step) for n in row_at], axis=0)
        total = total + t_dot(rows, refs[grads_at][k])
    for e in range(2):
        out_ref[e] = total[:, e * unit_part : (e + 1) * unit_part]


def row_grad_call(groups, which):
    step = 256
    half, width = groups[0][0][0][0][0].shape[1:]
    count, four = groups[0][2].shape[1:]
    units = four // 2
    args, specs, plan = [], [], []

    def add(array, spec):
        args.append(array)
        specs.append(spec)
        return len(args) - 1

    for rows, _, grads, _ in groups:
        m = len(rows[0])
        held = add(
            grads,
            pl.BlockSpec(
                (2 * m, count, units), lambda i: (0, 0, which), pipeline_mode=pl.Buffered(1)
            ),
        )
        for side in range(2):
            for j in range(m):
                tiles = [
                    add(r, pl.BlockSpec((2, half, step), lambda i: (0, 0, i)))
                    for r in rows[side][j]
                ]
                plan.append((tiles, held, side * m + j))
    return pl.pallas_call(
        lambda *refs: row_grad_kernel(plan, which, *refs),
        grid=(width // step,),
        in_specs=specs,
        out_specs=pl.BlockSpec((2, step, units // 2), lambda i: (0, i, 0)),
        out_shape=out((2, width, units // 2), F32),
        cost_estimate=pl.CostEstimate(
            flops=2 * len(plan) * count * width * units,
            bytes_accessed=2 * len(plan) * count * (width + units) + 4 * width * units,
            transcendentals=0,
        ),
        name="row_grads",
    )(*args)


def down_grad_kernel(scaled_a, scaled_b, cot_a, cot_b, out_ref):
    _, unit_part, step = out_ref.shape
    shards, chips, two, half, _ = cot_a.shape
    count = shards * two * half
    total = jnp.zeros((2 * unit_part, step), F32)
    for scaled_ref, cot_ref in ((scaled_a, cot_a), (scaled_b, cot_b)):
        for j in range(chips):
            total = total + t_dot(scaled_ref[j], cot_ref[:, j].reshape(count, step))
    for e in range(2):
        out_ref[e] = total[e * unit_part : (e + 1) * unit_part]


def down_grad_call(scaled, cots, first, chips_now):
    step = 256
    shards, _, two, half, _ = cots[0].shape
    _, count, units = scaled[0].shape
    width = (cots[0].shape[4] // step) * step
    held = pl.BlockSpec(
        (chips_now, count, units),
        lambda i: (first // chips_now, 0, 0),
        pipeline_mode=pl.Buffered(1),
    )
    tile = pl.BlockSpec(
        (shards, chips_now, two, half, step), lambda i: (0, first // chips_now, 0, 0, i)
    )
    return pl.pallas_call(
        down_grad_kernel,
        grid=(width // step,),
        in_specs=[held, held, tile, tile],
        out_specs=pl.BlockSpec((2, units // 2, step), lambda i: (0, 0, i)),
        out_shape=out((2, units // 2, width), F32),
        cost_estimate=pl.CostEstimate(
            flops=4 * chips_now * count * width * units,
            bytes_accessed=4 * chips_now * count * (width + units) + 4 * width * units,
            transcendentals=0,
        ),
        name="down_grads",
    )(*scaled, *cots)


def add_up(parts):
    total = parts[0]
    for part in parts[1:]:
        total = total + part
    return total


def turn_kernel(
    experts_all,
    ring_ref,
    a0,
    a1,
    a2,
    b0,
    b1,
    b2,
    residual_ref,
    cot_ref,
    mixed_ref,
    router_ref,
    router_rows_ref,
    gain_ref,
    grad_ref,
    grad_b_ref,
    gain_grad_ref,
    router_grad_ref,
):
    width = residual_ref.shape[2]
    half = residual_ref.shape[1]
    lane = lax.broadcasted_iota(jnp.int32, (half, LANES), 1)
    gain_grad, router_grad = None, None
    for n, refs in enumerate(((a0, a1, a2), (b0, b1, b2))):
        back = ring_ref[n].astype(F32) + total_of([r[...] for r in refs])
        mixed = mixed_ref[n]
        powers = jnp.where(lane < experts_all, jnp.exp(dot(mixed, router_ref[...])), 0.0)
        probs = powers / jnp.sum(powers, axis=-1, keepdims=True)
        prob_grad = back[:, width:]
        logit_grad = (
            probs * (prob_grad - jnp.sum(probs * prob_grad, axis=-1, keepdims=True))
        ).astype(BF16)
        mixed_grad = back[:, :width] + dot(logit_grad, router_rows_ref[...])
        residual = residual_ref[n]
        norm_grad, gain_now = norm_back(mixed_grad, residual, rms_scale(residual), gain_ref[...])
        total = cot_ref[n] + norm_grad
        grad_ref[n] = total
        grad_b_ref[n] = total.astype(BF16)
        router_now = t_dot(logit_grad, mixed)
        gain_grad = gain_now if gain_grad is None else gain_grad + gain_now
        router_grad = router_now if router_grad is None else router_grad + router_now
    gain_grad_ref[...] = jnp.broadcast_to(gain_grad, gain_grad_ref.shape)
    router_grad_ref[...] = router_grad[: router_grad_ref.shape[0]]


def output_grad_kernel(core_ref, g0, g1, g2, g3, attended_ref, own_ref, other_ref):
    part, width = attended_ref.shape[1], g0.shape[2]
    half = part // 2
    step = 512
    own_cols = pl.ds(pl.multiple_of(core_ref[0] * half, half), half)
    other_cols = pl.ds(pl.multiple_of((1 - core_ref[0]) * half, half), half)
    for c in range(width // step):
        cols = slice(c * step, (c + 1) * step)
        grads = jnp.concatenate(
            [g[:, :, cols].reshape(LANES, step) for g in (g0, g1, g2, g3)], axis=0
        )
        own_ref[0, :, cols] = t_dot(attended_ref[:, own_cols], grads)
        other_ref[0, :, cols] = t_dot(attended_ref[:, other_cols], grads).astype(BF16)


def attend_back_kernel(
    g0,
    g1,
    g2,
    g3,
    w_ref,
    attended_ref,
    q_ref,
    k_ref,
    v_ref,
    lse_ref,
    scales_ref,
    bias_ref,
    cos_ref,
    sin_ref,
    gain_q_ref,
    gain_k_ref,
    proj_ref,
    query_ref,
    key_ref,
    value_ref,
    stats_ref,
    gains_ref,
    grad_ref,
):
    part, width = w_ref.shape
    rows = proj_ref.shape[0]
    grad_ref[...] = jnp.concatenate(
        [g[...].reshape(LANES, width) for g in (g0, g1, g2, g3)], axis=0
    )
    q_scale, k_scale = scales_ref[:, 0:1], scales_ref[:, 1:2]
    cosine, sine_part = cos_ref[...], sin_ref[...]
    q_inner = jnp.zeros((rows, 1), F32)
    k_inner = jnp.zeros((rows, 1), F32)
    for h in range(part // HEAD_DIM):
        cols = slice(h * HEAD_DIM, (h + 1) * HEAD_DIM)
        k_cols = slice(part + h * HEAD_DIM, part + (h + 1) * HEAD_DIM)
        attended_grad = dot_t(grad_ref[...], w_ref[cols, :]).astype(BF16)
        query, key, value = q_ref[:, cols], k_ref[:, cols], v_ref[:, cols]
        probs = jnp.exp(
            dot_t(query, key) * SCORE_SCALE + bias_ref[...] - lse_ref[:, h : h + 1]
        )
        delta = jnp.sum(
            attended_grad.astype(F32) * attended_ref[:, cols].astype(F32), axis=-1, keepdims=True
        )
        score_grad = (probs * (dot_t(attended_grad, value) - delta)).astype(BF16)
        value_ref[:, cols] = t_dot(probs.astype(BF16), attended_grad).astype(BF16)
        query_grad = dot(score_grad, key) * SCORE_SCALE
        key_grad = t_dot(score_grad, query) * SCORE_SCALE
        query_pre = query_grad * cosine + pltpu.roll(query_grad * sine_part, HEAD_DIM // 2, 1)
        key_pre = key_grad * cosine + pltpu.roll(key_grad * sine_part, HEAD_DIM // 2, 1)
        q_proj, k_proj = proj_ref[:, cols], proj_ref[:, k_cols]
        gains_ref[0:1, cols] = jnp.sum(query_pre * q_proj * q_scale, axis=0, keepdims=True)
        gains_ref[1:2, cols] = jnp.sum(key_pre * k_proj * k_scale, axis=0, keepdims=True)
        query_pre = query_pre * gain_q_ref[:, cols]
        key_pre = key_pre * gain_k_ref[:, cols]
        query_ref[:, cols] = query_pre
        key_ref[:, cols] = key_pre
        q_inner = q_inner + jnp.sum(query_pre * q_proj, axis=-1, keepdims=True)
        k_inner = k_inner + jnp.sum(key_pre * k_proj, axis=-1, keepdims=True)
    for n, stats in enumerate(pack_stats(q_inner, k_inner)):
        stats_ref[n] = stats


def project_back_kernel(
    at_ref, core_ref, s0, s1, s2, s3, query_ref, key_ref, value_ref, proj_ref, scales_ref, normed_ref, *refs
):
    weight_refs = refs[:8]
    part_refs, own_ref, other_ref, all_ref = refs[8:12], refs[12], refs[13], refs[14]
    width = normed_ref.shape[1]
    part = query_ref.shape[1]
    inner = sum_stats(s0, s1, s2, s3) / width
    for n, (grad_ref, low) in enumerate(((query_ref, 0), (key_ref, part))):
        scale = scales_ref[:, n : n + 1]
        factor = scale * scale * inner[:, n : n + 1]
        all_ref[:, low : low + part] = (
            scale * (grad_ref[...] - proj_ref[:, low : low + part] * factor)
        ).astype(BF16)
    all_ref[:, 2 * part :] = value_ref[...]
    depth = weight_refs[0].shape[0]
    for n, ref in enumerate(weight_refs):
        at = pl.ds(pl.multiple_of(at_ref[n] * depth, depth), depth)
        got = dot_t(all_ref[...], ref[...]).astype(BF16)
        for k, part_ref in enumerate(part_refs):
            part_ref[:, :, at] = got[k * LANES : (k + 1) * LANES].reshape(2, LANES // 2, depth)
    for p in range(width // (2 * depth)):
        for ref, side in ((own_ref, core_ref[0]), (other_ref, 1 - core_ref[0])):
            at = pl.ds(pl.multiple_of((2 * p + side) * depth, depth), depth)
            for third in range(3):
                cols = slice(third * part, (third + 1) * part)
                ref[p, :, cols] = t_dot(normed_ref[:, at], all_ref[:, cols]).astype(ref.dtype)


def finish_kernel(a0, a1, a2, b0, b1, b2, x_ref, grad_ref, gain_ref, out_ref, gain_grad_ref):
    gain_grad = None
    for n, refs in enumerate(((a0, a1, a2), (b0, b1, b2))):
        source = x_ref[n].astype(F32)
        normed_grad = total_of([r[...] for r in refs])
        norm_grad, gain_now = norm_back(normed_grad, source, rms_scale(source), gain_ref[...])
        out_ref[n] = grad_ref[n] + norm_grad
        gain_grad = gain_now if gain_grad is None else gain_grad + gain_now
    gain_grad_ref[...] = jnp.broadcast_to(gain_grad, gain_grad_ref.shape)


def cut_kernel(at_ref, *refs):
    sources, (own_ref, spare_ref, x_ref, y_ref) = refs[:15], refs[15:]
    depth, part = sources[0].shape
    rows = depth // 2
    for w in range(3):
        cols = slice(w * part, (w + 1) * part)
        own_ref[:, cols] = sources[w][...]
        x_ref[:depth, cols] = sources[3 + w][...]
        y_ref[:depth, cols] = sources[6 + w][...]
        x_ref[depth:, cols] = sources[9 + w][:rows, :]
        y_ref[depth:, cols] = sources[9 + w][rows:, :]
        spare_ref[:, cols] = sources[12 + w][...]


def cut_call(at, w_query, w_key, w_value):
    rows, width = w_query.shape
    part = width // 4
    depth = rows // 2

    def block(member, core):
        return pl.BlockSpec((depth, part), lambda i, at: (at[core], at[member]))

    full, more = (depth, 3 * part), (3 * depth // 2, 3 * part)
    fulls = [full, full, more, more]
    return pl.pallas_call(
        cut_kernel,
        grid_spec=pltpu.PrefetchScalarGridSpec(
            num_scalar_prefetch=1,
            grid=(1,),
            in_specs=[block(d, 4) for d in range(4) for _ in range(3)]
            + [block(0, 5) for _ in range(3)],
            out_specs=[whole(s) for s in fulls],
        ),
        out_shape=[out(s, BF16) for s in fulls],
        name="cut",
    )(at, *([w_query, w_key, w_value] * 5))


def on_device(
    block_input,
    segment_ids,
    expert_routes,
    attn_gain,
    w_query,
    w_key,
    w_value,
    query_gain,
    key_gain,
    w_output,
    moe_gain,
    w_router,
    w_gate,
    w_up,
    w_down,
    out_cotangent,
):
    expert_count = lax.axis_size("expert")
    shard_count = lax.axis_size("shard")
    chips = expert_count // 2
    me = lax.axis_index("shard")
    place = lax.axis_index("expert")
    core = lax.rem(place, 2)
    chip = place // 2
    tok_count = block_input.shape[1]
    half = tok_count // 2
    group_count = segment_ids.shape[1]
    width = block_input.shape[2]
    part = width // shard_count
    local_experts = w_gate.shape[0]
    experts_all = local_experts * expert_count
    unit_part = w_gate.shape[2]
    units = local_experts * unit_part
    core_at = jnp.reshape(core, (1,))

    own_input = block_input.reshape(2, half, width)
    group_input = [b.reshape(2, half, width) for b in spread_xy(own_input[:1], own_input[1:])]

    small = jnp.concatenate([attn_gain[None], moe_gain[None], w_router.T], axis=0)
    small = jnp.pad(small, ((0, (-small.shape[0]) % 32), (0, 0)))
    small_all = jnp.zeros((small.shape[0], width), BF16)
    small_parts = gather_parts(small)
    for d, got in enumerate(small_parts):
        small_all = lax.dynamic_update_slice_in_dim(small_all, got, (me ^ d) * part, 1)
    gain_one = small_all[0:1].astype(F32)
    gain_two = small_all[1:2].astype(F32)
    router = small_all[2 : 2 + experts_all]
    router = jnp.pad(router, ((0, LANES - experts_all), (0, 0)))
    router_t = router.T

    depth = part // 2
    at = jnp.stack([me, me ^ 1, me ^ 2, me ^ 3, core, 1 - core])
    cuts = cut_call(at, w_query, w_key, w_value)
    direct = exchange_blocks(*after(cuts[2:], group_input[0], group_input[2], small_parts))
    passed = [swap_core(block) for block in direct]
    weight_blocks = list(cuts[:2]) + direct + passed
    weight_at = jnp.stack(
        [2 * me + core, 2 * me + 1 - core]
        + [2 * (me ^ d) + core for d in (1, 2, 3)]
        + [2 * (me ^ d) + 1 - core for d in (1, 2, 3)]
    )

    routes = expert_routes[0]
    routed = jnp.sum(
        (routes[:, :, None] == jnp.arange(experts_all)[None, None, :]).astype(F32), axis=1
    )
    cotangent = out_cotangent[0]
    cot_block = (
        jnp.concatenate(
            [cotangent, routed, jnp.zeros((tok_count, LANES - experts_all), F32)], axis=1
        )
        .astype(BF16)
        .reshape(2, half, width + LANES)
    )
    cot_block = after(cot_block, group_input[0], group_input[2])
    cot_pieces = jnp.concatenate(ring_gather(cot_block), axis=0)
    cot = lax.all_gather(after(cot_pieces, direct), "shard", axis=0, tiled=True)

    down_w = w_down.reshape(units, width)
    gate_up_t, down_t = flip_call(w_gate, w_up, w_down)

    starts = [(me ^ d) * tok_count + side * half for pair in ORDER for side, d in pair]
    position = jnp.concatenate([p + jnp.arange(half) for p in starts])
    seg_all = segment_ids[0]
    seg_here = jnp.concatenate([lax.dynamic_slice_in_dim(seg_all, p, half) for p in starts])
    allowed = (seg_here[:, None] == seg_here[None, :]) & (position[None, :] <= position[:, None])
    bias = jnp.where(allowed, 0.0, -1e30).astype(F32)
    half_dim = HEAD_DIM // 2
    inverse = 10000.0 ** (-(jnp.arange(half_dim).astype(F32) * 2.0) / HEAD_DIM)
    angles = position.astype(F32)[:, None] * inverse[None, :]
    cosine = jnp.concatenate([jnp.cos(angles), jnp.cos(angles)], axis=-1)
    sine_part = jnp.concatenate([-jnp.sin(angles), jnp.sin(angles)], axis=-1)
    gain_query = query_gain.astype(F32)[None]
    gain_key = key_gain.astype(F32)[None]
    normed, proj, squares, scale_one = call(
        project_kernel,
        "project",
        [weight_at] + group_input + [after(gain_one, gate_up_t)] + weight_blocks,
        [
            out((group_count, width), BF16),
            out((group_count, 3 * part), F32),
            out((4, 8, LANES), F32),
            out((group_count, LANES), F32),
        ],
        2 * group_count * width * 3 * part,
        smem=(0,),
    )
    quad = out((2, half, width), BF16)
    square_parts = out((group_count, part), BF16)
    heads = call(
        lambda *refs: attend_kernel(width, *refs),
        "attend",
        [proj] + gather_parts(squares) + [gain_query, gain_key, cosine, sine_part, bias, w_output],
        [square_parts] * 3
        + [out((group_count, LANES), F32)] * 2
        + [square_parts]
        + [quad] * 4,
        4 * group_count * group_count * part + 2 * group_count * part * width,
    )
    q_heads, k_heads, v_heads, log_total, scales, attended = heads[:6]
    terms_a, terms_b = reduce_xy([b.reshape(2, 1, half, width) for b in heads[6:]])
    residual, mixed_in = call(
        settle_kernel,
        "settle",
        [own_input]
        + [t.reshape(half, width) for t in terms_a + terms_b]
        + [gain_two],
        [out((2, half, width), F32), out((2, half, width), BF16)],
        tok_count * width,
    )

    pieces = ring_gather(mixed_in)
    cot = after(cot, mixed_in).reshape(shard_count, chips, 2, half, width + LANES)
    cots = (cot, swap_core(cot))
    leads = [lead_call(c, down_t) for c in cots]
    size = 1
    at = jnp.stack([place, me])
    all_rows = []
    for piece in pieces:
        own = [b.reshape(2, half, width) for b in spread_xy(piece[:1], piece[1:])]
        all_rows.append((own, [swap_core(r) for r in own]))
    groups, back_terms, scaled_all, totals_all = [], [None] * chips, ([], []), []
    for low in range(0, chips, size):
        rows = [[all_rows[j][side] for j in range(low, low + size)] for side in range(2)]
        at_now = after(at, totals_all[low - 2]) if low > 1 else at
        got = expert_call(
            at_now, rows, cots, low, leads, w_gate, w_up, gate_up_t, router_t, experts_all
        )
        groups.append((rows, low, got[5], got[6]))
        for side in range(2):
            scaled_all[side].append(got[6][side * size : (side + 1) * size])
        passed_back = swap_core(got[4])
        totals_all.append(
            [
                (a.astype(F32) + passed_back[n].astype(F32)).astype(BF16)
                for n, a in enumerate(got[:4])
            ]
        )
    for n, low in enumerate(range(0, chips, size)):
        terms_a, terms_b = reduce_xy(after(totals_all[n], [r[0] for r in all_rows]))
        for j in range(low, low + size):
            back_terms[j] = [[t[j - low] for t in terms] for terms in (terms_a, terms_b)]

    def back_piece(j):
        return jnp.stack([total_of(terms) for terms in back_terms[j]])

    ring_total = back_piece(1).astype(BF16)
    for j in range(2, chips):
        ring_total = (ring_up(ring_total).astype(F32) + back_piece(j)).astype(BF16)
    ring_total = ring_up(ring_total)
    grad_res, grad_res_b, grad_gain_two, grad_router = call(
        lambda *refs: turn_kernel(experts_all, *refs),
        "turn",
        [ring_total]
        + back_terms[0][0]
        + back_terms[0][1]
        + [residual, cotangent.reshape(2, half, width), mixed_in, router_t, router]
        + [gain_two],
        [
            out((2, half, width), F32),
            out((2, half, width), BF16),
            out((8, width), F32),
            out((experts_all, width), F32),
        ],
        8 * tok_count * width * LANES,
    )

    scaled_all = [
        jnp.concatenate(s, axis=0).reshape(chips, group_count, units) for s in scaled_all
    ]
    mix_other = mix_call(after(scaled_all[1], grad_res_b), down_w, shard_count)
    mix_passed = swap_core(mix_other)

    group_grad = [b.reshape(2, half, width) for b in spread_xy(grad_res_b[:1], grad_res_b[1:])]
    output_own, output_other = call(
        output_grad_kernel,
        "output_grad",
        [core_at] + after(group_grad, mix_other) + [attended],
        [out((1, part // 2, width), F32), out((1, part // 2, width), BF16)],
        2 * group_count * part * width,
        smem=(0,),
    )
    query_pre, key_pre, value_grad, inner, gain_grads, _ = call(
        attend_back_kernel,
        "attend_back",
        after(group_grad, output_other)
        + [w_output, attended, q_heads, k_heads, v_heads, log_total, scales, bias]
        + [cosine, sine_part, gain_query, gain_key, proj],
        [
            out((group_count, part), F32),
            out((group_count, part), F32),
            square_parts,
            out((4, 8, LANES), F32),
            out((8, part), F32),
            out((group_count, width), BF16),
        ],
        10 * group_count * group_count * part + 2 * group_count * part * width,
    )
    output_total = output_own + swap_core(output_other).astype(F32)
    out_total = mix_call(
        after(scaled_all[0], query_pre), down_w, shard_count, mix_passed
    ).reshape(-1, width)
    out_sums = lax.psum_scatter(out_total, "shard", scatter_dimension=0, tiled=True)
    got = call(
        project_back_kernel,
        "project_back",
        [weight_at, core_at]
        + gather_parts(inner)
        + [query_pre, key_pre, value_grad, proj, scales, normed]
        + weight_blocks,
        [quad] * 4
        + [
            out((4, depth, 3 * part), F32),
            out((4, depth, 3 * part), BF16),
            out((group_count, 3 * part), BF16),
        ],
        4 * group_count * width * 3 * part,
        smem=(0, 1),
    )
    terms_a, terms_b = reduce_xy([b.reshape(2, 1, half, width) for b in got[:4]])
    grad_input, grad_gain_one = call(
        finish_kernel,
        "finish",
        [t.reshape(half, width) for t in terms_a + terms_b] + [own_input, grad_res, gain_one],
        [out((2, half, width), F32), out((8, width), F32)],
        tok_count * width,
    )

    out_sums = out_sums.reshape(chips, tok_count, width)
    ring_part, own_part = ring_sum(lambda j: out_sums[j])
    block_output = residual.reshape(tok_count, width) + (
        ring_part.astype(F32) + own_part.astype(F32)
    )

    output_piece = expert_sum(output_total, chip)
    grad_w_output = expert_spread(output_piece, core, chip)[0].astype(F32)
    qkv_total = got[4] + swap_core(got[5]).astype(F32)
    qkv_piece = expert_sum(qkv_total, chip)
    sent = [lax.dynamic_index_in_dim(qkv_piece, me ^ d, 0, keepdims=False) for d in range(4)]
    low = sent[3].shape[0] // 2
    arrived = exchange_blocks(
        jnp.concatenate([sent[1], sent[3][:low]], axis=0),
        jnp.concatenate([sent[2], sent[3][low:]], axis=0),
    )
    qkv_rows = expert_spread(jnp.stack([sent[0]] + arrived), core, chip)
    shares = [lax.dynamic_index_in_dim(qkv_rows, me ^ p, 0, keepdims=False) for p in range(4)]
    grad_w_query, grad_w_key, grad_w_value = (
        jnp.concatenate([share[:, n * part : (n + 1) * part] for share in shares], axis=1).astype(
            F32
        )
        for n in range(3)
    )

    span = min(chips, 4)
    sets = [groups[low : low + span] for low in range(0, chips, span)]
    grad_w_gate = add_up([row_grad_call(some, 0) for some in sets])
    grad_w_up = add_up([row_grad_call(some, 1) for some in sets])
    grad_w_down = add_up(
        [down_grad_call(scaled_all, cots, low, span) for low in range(0, chips, span)]
    )

    packed = jnp.concatenate([grad_gain_one[:1], grad_gain_two[:1], grad_router], axis=0)
    rows_used = packed.shape[0]
    packed = jnp.pad(packed, ((0, (-rows_used) % 16), (0, 0)))
    quarters = jnp.stack(
        [lax.dynamic_slice_in_dim(packed, (me ^ d) * part, part, 1) for d in range(4)]
    )
    quarters = quarters[:2] + swap_y(quarters[2:])
    packed = (quarters[0] + swap_x(quarters[1]))[:rows_used]
    packed = jnp.concatenate([packed, gain_grads[:2]], axis=0)
    bit = 1
    while bit < expert_count:
        packed = packed + flip_expert(packed, bit)
        bit *= 2
    return (
        block_output.reshape(1, tok_count, width),
        grad_input.reshape(1, tok_count, width),
        packed[0],
        grad_w_query,
        grad_w_key,
        grad_w_value,
        packed[rows_used],
        packed[rows_used + 1],
        grad_w_output,
        packed[1],
        packed[2 : 2 + experts_all].T,
        grad_w_gate,
        grad_w_up,
        grad_w_down,
    )


def solution(mesh):
    placed = (
        P("expert", "shard", None),
        P("expert", None),
        P("expert", "shard", None),
        P("shard"),
        P("shard", None),
        P("shard", None),
        P("shard", None),
        P("shard"),
        P("shard"),
        P("shard", None),
        P("shard"),
        P("shard", None),
        P("expert", None, "shard"),
        P("expert", None, "shard"),
        P("expert", "shard", None),
        P("expert", "shard", None),
    )
    return jax.shard_map(
        on_device,
        mesh=mesh,
        in_specs=placed,
        out_specs=(
            P("expert", "shard", None),
            P("expert", "shard", None),
            P("shard"),
            P("shard", None),
            P("shard", None),
            P("shard", None),
            P("shard"),
            P("shard"),
            P("shard", None),
            P("shard"),
            P("shard", None),
            P("expert", None, "shard"),
            P("expert", None, "shard"),
            P("expert", "shard", None),
        ),
        check_vma=False,
    )
```

```python
import jax
import jax.numpy as jnp
from jax import lax
from jax.experimental import pallas as pl
from jax.experimental.pallas import tpu as pltpu
from jax.sharding import PartitionSpec as P

HEAD_DIM = 128
LANES = 128
EPSILON = 1e-05
SCORE_SCALE = HEAD_DIM ** (-0.5)
F32 = jnp.float32
BF16 = jnp.bfloat16
ORDER = (((0, 0), (0, 1)), ((0, 2), (0, 3)), ((1, 0), (1, 2)), ((1, 1), (1, 3)))


def dot(a, b):
    return jnp.dot(a, b, preferred_element_type=F32)


def dot_t(a, b):
    return lax.dot_general(a, b, (((1,), (1,)), ((), ())), preferred_element_type=F32)


def t_dot(a, b):
    return lax.dot_general(a, b, (((0,), (0,)), ((), ())), preferred_element_type=F32)


def flip_shard(values, bit):
    count = lax.axis_size("shard")
    return lax.ppermute(values, "shard", [(i, i ^ bit) for i in range(count)])


def swap_x(values):
    return flip_shard(values, 1)


def swap_y(values):
    return flip_shard(values, 2)


def swap_far(values):
    return flip_shard(values, 3)


def flip_expert(values, bit):
    count = lax.axis_size("expert")
    return lax.ppermute(values, "expert", [(i, i ^ bit) for i in range(count)])


def swap_core(values):
    return flip_expert(values, 1)


def ring_up(values):
    count = lax.axis_size("expert")
    return lax.ppermute(values, "expert", [(i, (i + 2) % count) for i in range(count)])


def after(values, *others):
    return lax.optimization_barrier((values, others))[0]


def spread_xy(first, second):
    pair_a = jnp.stack([first, swap_x(first)])
    pair_b = jnp.stack([second, swap_y(second)])
    return [pair_a, swap_y(pair_a), pair_b, swap_x(pair_b)]


def reduce_xy(blocks, *others):
    keep_a, send_a, keep_b, send_b = blocks
    got_a, got_b = after((swap_y(send_a), swap_x(send_b)), *others)
    far_a = swap_x((keep_a[1].astype(F32) + got_a[1].astype(F32)).astype(BF16))
    far_b = swap_y((keep_b[1].astype(F32) + got_b[1].astype(F32)).astype(BF16))
    return (keep_a[0], got_a[0], far_a), (keep_b[0], got_b[0], far_b)


def total_of(terms):
    total = terms[0].astype(F32)
    for term in terms[1:]:
        total = total + term.astype(F32)
    return total


def exchange_blocks(for_x, for_y, *others):
    got_x, got_y = after((swap_x(for_x), swap_y(for_y)), *others)
    depth = 2 * for_x.shape[0] // 3
    far = jnp.concatenate([swap_y(got_x[depth:]), swap_x(got_y[depth:])], axis=0)
    return [got_x[:depth], got_y[:depth], far]


def gather_parts(part):
    return [part, swap_x(part), swap_y(part), swap_far(part)]


def ring_gather(piece):
    pieces = [piece]
    for _ in range(lax.axis_size("expert") // 2 - 1):
        pieces.append(ring_up(pieces[-1]))
    return pieces


def ring_sum(total, pieces):
    for piece in pieces:
        total = (ring_up(total).astype(F32) + piece).astype(BF16)
    return total


def expert_spread(pieces, core, chip):
    chips = lax.axis_size("expert") // 2
    parts, rows, columns = pieces[0].shape
    spread = jnp.zeros((parts, chips, rows, columns), pieces[0].dtype)
    for j, got in enumerate(pieces):
        spread = lax.dynamic_update_slice_in_dim(
            spread, got[:, None], lax.rem(chip + chips - j, chips), 1
        )
    half = spread.reshape(parts, 1, chips * rows, columns)
    other = swap_core(half)
    first = jnp.where(core == 0, half, other)
    second = jnp.where(core == 0, other, half)
    return jnp.concatenate([first, second], axis=1).reshape(parts, 2 * chips * rows, columns)


def rms_scale(values):
    return lax.rsqrt(jnp.mean(values * values, axis=-1, keepdims=True) + EPSILON)


def norm_back(grad_out, source, scale_now, gain_now):
    weighted = grad_out * gain_now
    inner_mean = jnp.mean(weighted * source, axis=-1, keepdims=True)
    grad_source = scale_now * (weighted - source * scale_now * scale_now * inner_mean)
    grad_gain = jnp.sum(grad_out * source * scale_now, axis=0, keepdims=True)
    return (grad_source, grad_gain)


def whole(shape):
    return pl.BlockSpec(shape, lambda *_: (0,) * len(shape))


def scalars():
    return pl.BlockSpec(memory_space=pltpu.SMEM)


def call(kernel, name, args, outs, flops, smem=(), transcendentals=0):
    moved = sum(a.size * a.dtype.itemsize for a in args) + sum(
        o.size * o.dtype.itemsize for o in outs
    )
    return pl.pallas_call(
        kernel,
        in_specs=[scalars() if n in smem else whole(a.shape) for n, a in enumerate(args)],
        out_specs=[whole(o.shape) for o in outs],
        out_shape=outs,
        cost_estimate=pl.CostEstimate(
            flops=flops, bytes_accessed=moved, transcendentals=transcendentals
        ),
        name=name,
    )(*args)


def out(shape, dtype):
    return jax.ShapeDtypeStruct(shape, dtype)


def pack_stats(first, second):
    rows = first.shape[0]
    lane = lax.broadcasted_iota(jnp.int32, (rows, LANES), 1)
    spread = jnp.where(lane == 0, first, jnp.where(lane == 1, second, 0.0))
    return [spread[n : n + LANES].T[:8] for n in range(0, rows, LANES)]


def sum_stats(mine, from_x, from_y, far):
    def turn(values):
        return pltpu.roll(values, LANES // 2, 1)

    totals = [
        mine[0] + turn(from_x[0]) + from_y[1] + turn(far[1]),
        mine[1] + turn(from_x[1]) + from_y[0] + turn(far[0]),
        mine[2] + from_x[3] + turn(from_y[2]) + turn(far[3]),
        mine[3] + from_x[2] + turn(from_y[3]) + turn(far[2]),
    ]
    pad = jnp.zeros((LANES - 8, LANES), F32)
    return jnp.concatenate([jnp.concatenate([t, pad], axis=0).T for t in totals], axis=0)


def project_kernel(
    at_ref, r0, r1, r2, r3, gain_ref, *refs
):
    weight_refs, (normed_ref, proj_ref, stats_ref, scale_ref) = refs[:8], refs[8:]
    part = proj_ref.shape[1] // 3
    for n, ref in enumerate((r0, r1, r2, r3)):
        source = ref[...].reshape(LANES, ref.shape[2]).astype(F32)
        scale = rms_scale(source)
        rows = slice(n * LANES, (n + 1) * LANES)
        normed_ref[rows, :] = (source * scale * gain_ref[...]).astype(BF16)
        scale_ref[rows, :] = jnp.broadcast_to(scale, (LANES, LANES))
    depth = weight_refs[0].shape[0]
    for third in range(3):
        cols = slice(third * part, (third + 1) * part)
        total = None
        for n, ref in enumerate(weight_refs):
            rows = pl.ds(pl.multiple_of(at_ref[n] * depth, depth), depth)
            more = dot(normed_ref[:, rows], ref[:, cols])
            total = more if total is None else total + more
        proj_ref[:, cols] = total
    q_proj, k_proj = proj_ref[:, :part], proj_ref[:, part : 2 * part]
    packed = pack_stats(
        jnp.sum(q_proj * q_proj, axis=-1, keepdims=True),
        jnp.sum(k_proj * k_proj, axis=-1, keepdims=True),
    )
    for n, stats in enumerate(packed):
        stats_ref[n] = stats


def attend_kernel(
    width, proj_ref, s0, s1, s2, s3, gain_q_ref, gain_k_ref, cos_ref, sin_ref, bias_ref, w_ref, *refs
):
    q_ref, k_ref, v_ref, lse_ref, scales_ref, attended_ref = refs[:6]
    part_refs = refs[6:]
    part = w_ref.shape[0]
    rows = proj_ref.shape[0]
    sums = sum_stats(s0, s1, s2, s3)
    scales = lax.rsqrt(sums / width + EPSILON)
    scales_ref[...] = scales
    lane = lax.broadcasted_iota(jnp.int32, (rows, LANES), 1)
    q_scale, k_scale = scales[:, 0:1], scales[:, 1:2]
    cosine, sine_part = cos_ref[...], sin_ref[...]
    lse_all = jnp.zeros((rows, LANES), F32)
    for h in range(part // HEAD_DIM):
        cols = slice(h * HEAD_DIM, (h + 1) * HEAD_DIM)
        k_cols = slice(part + h * HEAD_DIM, part + (h + 1) * HEAD_DIM)
        v_cols = slice(2 * part + h * HEAD_DIM, 2 * part + (h + 1) * HEAD_DIM)
        query = proj_ref[:, cols] * q_scale * gain_q_ref[:, cols]
        key = proj_ref[:, k_cols] * k_scale * gain_k_ref[:, cols]
        query = (query * cosine + pltpu.roll(query, HEAD_DIM // 2, 1) * sine_part).astype(BF16)
        key = (key * cosine + pltpu.roll(key, HEAD_DIM // 2, 1) * sine_part).astype(BF16)
        value = proj_ref[:, v_cols].astype(BF16)
        q_ref[:, cols] = query
        k_ref[:, cols] = key
        v_ref[:, cols] = value
        scores = dot_t(query, key) * SCORE_SCALE + bias_ref[...]
        top = jnp.max(scores, axis=-1, keepdims=True)
        powers = jnp.exp(scores - top)
        total = jnp.sum(powers, axis=-1, keepdims=True)
        lse_all = jnp.where(lane == h, top + jnp.log(total), lse_all)
        attended_ref[:, cols] = dot((powers / total).astype(BF16), value).astype(BF16)
    lse_ref[...] = lse_all
    step = 512
    for c in range(w_ref.shape[1] // step):
        cols = slice(c * step, (c + 1) * step)
        for n, ref in enumerate(part_refs):
            got = dot(attended_ref[n * LANES : (n + 1) * LANES, :], w_ref[:, cols])
            ref[:, :, cols] = got.astype(BF16).reshape(2, LANES // 2, step)


def settle_kernel(x_ref, a0, a1, a2, b0, b1, b2, gain_ref, residual_ref, mixed_ref):
    for n, refs in enumerate(((a0, a1, a2), (b0, b1, b2))):
        residual = x_ref[n].astype(F32) + total_of([r[...] for r in refs])
        residual_ref[n] = residual
        mixed_ref[n] = (residual * rms_scale(residual) * gain_ref[...]).astype(BF16)


def flip_kernel(gate_ref, up_ref, down_ref, gate_up_t_ref, down_t_ref):
    unit_part = gate_ref.shape[2]
    for e in range(2):
        low = e * unit_part
        gate_up_t_ref[low : low + unit_part, :] = gate_ref[e].T
        gate_up_t_ref[2 * unit_part + low : 2 * unit_part + low + unit_part, :] = up_ref[e].T
        down_t_ref[:, low : low + unit_part] = down_ref[e].T


def flip_call(w_gate, w_up, w_down):
    two, width, unit_part = w_gate.shape
    step = 512
    tall = pl.BlockSpec((two, step, unit_part), lambda i: (0, i, 0))
    return pl.pallas_call(
        flip_kernel,
        grid=(width // step,),
        in_specs=[tall, tall, pl.BlockSpec((two, unit_part, step), lambda i: (0, 0, i))],
        out_specs=[
            pl.BlockSpec((4 * unit_part, step), lambda i: (0, i)),
            pl.BlockSpec((step, 2 * unit_part), lambda i: (i, 0)),
        ],
        out_shape=[out((4 * unit_part, width), BF16), out((width, 2 * unit_part), BF16)],
        cost_estimate=pl.CostEstimate(flops=0, bytes_accessed=12 * w_gate.size, transcendentals=0),
        name="flip",
    )(w_gate, w_up, w_down)


def lead_kernel(cot_ref, down_t_ref, lead_ref):
    width = down_t_ref.shape[0]
    cot = cot_ref[...].reshape(-1, cot_ref.shape[5])[:, :width]
    lead_ref[0, 0] = dot(cot, down_t_ref[...]).reshape(lead_ref.shape[2:])


def lead_call(cot, down_t):
    shards, chips, cores, two, rows, columns = cot.shape
    width, units = down_t.shape
    count = shards * two * rows
    return pl.pallas_call(
        lead_kernel,
        grid=(chips, cores),
        in_specs=[
            pl.BlockSpec((shards, 1, 1, two, rows, columns), lambda i, c: (0, i, c, 0, 0, 0)),
            whole(down_t.shape),
        ],
        out_specs=pl.BlockSpec((1, 1, shards * two, rows, units), lambda i, c: (i, c, 0, 0, 0)),
        out_shape=out((chips, cores, shards * two, rows, units), F32),
        cost_estimate=pl.CostEstimate(
            flops=2 * chips * cores * count * down_t.size,
            bytes_accessed=2 * cot.size + 4 * chips * cores * count * units,
            transcendentals=0,
        ),
        name="lead",
    )(cot, down_t)


def join_kernel(a_ref, b_ref, c_ref, d_ref, out_ref):
    for n, ref in enumerate((a_ref, b_ref, c_ref, d_ref)):
        out_ref[2 * n : 2 * n + 2] = ref[:, 0]


def join_call(parts, j):
    two, _, rows, width = parts[0].shape
    step = rows // 2
    return pl.pallas_call(
        join_kernel,
        grid=(2,),
        in_specs=[pl.BlockSpec((two, 1, step, width), lambda i: (0, j, i, 0))] * 4,
        out_specs=pl.BlockSpec((4 * two, step, width), lambda i: (0, i, 0)),
        out_shape=out((4 * two, rows, width), BF16),
        cost_estimate=pl.CostEstimate(
            flops=0, bytes_accessed=16 * two * rows * width, transcendentals=0
        ),
        name="join",
    )(*parts)


def expert_kernel(experts_all, at_ref, *refs):
    row_refs, routed_ref, lead_ref = refs[:2], refs[2], refs[3]
    gate_ref, up_ref, gate_up_t_ref, router_ref = refs[4:8]
    own_refs, other_ref, grads_ref, scaled_out, scaled_ref = (
        refs[8:12],
        refs[12],
        refs[13],
        refs[14],
        refs[15],
    )
    rows_ref, mask_ref, lead_here_ref = refs[16:]
    width = router_ref.shape[0]
    units = lead_here_ref.shape[1]
    unit_part = units // 2
    half = LANES // 2
    me = at_ref[1]
    now = pl.program_id(0)
    blocks = [block for pair in ORDER for block in pair]
    for side in range(2):

        @pl.when(now == side)
        def _():
            rows_ref[...] = row_refs[side][...].reshape(rows_ref.shape)

    for n, (part, d) in enumerate(blocks):
        to = slice(n * half, (n + 1) * half)
        mask_ref[to, :] = routed_ref[me ^ d, 0, 0, part]
        lead_here_ref[to, :] = lead_ref[0, 0, 2 * (me ^ d) + part]
    rows = rows_ref[...]
    count = rows.shape[0]
    lane = lax.broadcasted_iota(jnp.int32, (count, LANES), 1)
    routed = mask_ref[...].astype(F32)
    powers = jnp.where(lane < experts_all, jnp.exp(dot(rows, router_ref[...])), 0.0)
    weights = powers * routed / jnp.sum(powers, axis=-1, keepdims=True)
    spot = jnp.zeros((count, LANES), F32)
    for e in range(2):
        here = (lane == at_ref[0] * 2 + e).astype(F32)
        chosen = jnp.sum(weights * here, axis=-1, keepdims=True)
        low = e * unit_part
        gate_pre = dot(rows, gate_ref[e])
        up_pre = dot(rows, up_ref[e])
        lead = lead_here_ref[:, low : low + unit_part]
        sigmoid_gate = 1.0 / (1.0 + jnp.exp(-gate_pre))
        silu_gate = gate_pre * sigmoid_gate
        hidden = (silu_gate * up_pre).astype(BF16).astype(F32)
        spot = spot + jnp.sum(hidden * lead, axis=-1, keepdims=True) * (here * routed)
        grad_hidden = lead * chosen
        gate_grad = grad_hidden * up_pre * sigmoid_gate * (1.0 + gate_pre * (1.0 - sigmoid_gate))
        grads_ref[0, :, low : low + unit_part] = gate_grad.astype(BF16)
        grads_ref[0, :, units + low : units + low + unit_part] = (grad_hidden * silu_gate).astype(
            BF16
        )
        scaled_ref[0, :, low : low + unit_part] = (hidden * chosen).astype(BF16)
    for n, (part, d) in enumerate(blocks):
        scaled_out[0, 2 * (me ^ d) + part] = scaled_ref[0, n * half : (n + 1) * half, :]
    mask_ref[...] = spot.astype(BF16)
    step = 512

    @pl.when(now == 0)
    def _():
        for n, ref in enumerate(own_refs):
            at = slice(n * LANES, (n + 1) * LANES)
            ref[:, 0, :, width:] = mask_ref[at, :].reshape(2, half, LANES)
        for c in range(width // step):
            cols = slice(c * step, (c + 1) * step)
            part = dot(grads_ref[0], gate_up_t_ref[:, cols]).astype(BF16)
            for n, ref in enumerate(own_refs):
                at = slice(n * LANES, (n + 1) * LANES)
                ref[:, 0, :, cols] = part[at].reshape(2, half, step)

    @pl.when(now == 1)
    def _():
        for n in range(4):
            at = slice(n * LANES, (n + 1) * LANES)
            other_ref[n, :, 0, :, width:] = mask_ref[at, :].reshape(2, half, LANES)
        for c in range(width // step):
            cols = slice(c * step, (c + 1) * step)
            part = dot(grads_ref[0], gate_up_t_ref[:, cols]).astype(BF16)
            for n in range(4):
                at = slice(n * LANES, (n + 1) * LANES)
                other_ref[n, :, 0, :, cols] = part[at].reshape(2, half, step)


def expert_call(at, rows, cot, lead, w_gate, w_up, gate_up_t, router, experts_all):
    eight, half, width = rows[0].shape
    shards, units = cot.shape[0], lead.shape[4]
    count = eight * half
    own_shape = (2, 1, half, width + LANES)

    def core_of(i, at):
        return lax.rem(at[3] + i, 2)

    return pl.pallas_call(
        lambda *refs: expert_kernel(experts_all, *refs),
        grid_spec=pltpu.PrefetchScalarGridSpec(
            num_scalar_prefetch=1,
            grid=(2,),
            in_specs=[
                pl.BlockSpec(r.shape, lambda i, _: (0, 0, 0), pipeline_mode=pl.Buffered(1))
                for r in rows
            ]
            + [
                pl.BlockSpec(
                    (shards, 1, 1, 2, half, LANES),
                    lambda i, at: (0, at[2], core_of(i, at), 0, 0, width // LANES),
                ),
                pl.BlockSpec(
                    (1, 1, eight, half, units), lambda i, at: (at[2], core_of(i, at), 0, 0, 0)
                ),
            ]
            + [whole(w_gate.shape), whole(w_up.shape), whole(gate_up_t.shape), whole(router.shape)],
            out_specs=[whole(own_shape) for _ in range(4)]
            + [
                whole((4,) + own_shape),
                pl.BlockSpec((1, count, 2 * units), lambda i, _: (i, 0, 0)),
                pl.BlockSpec((1, eight, half, units), lambda i, _: (i, 0, 0, 0)),
                pl.BlockSpec((1, count, units), lambda i, _: (i, 0, 0)),
            ],
            scratch_shapes=[
                pltpu.VMEM((count, width), BF16),
                pltpu.VMEM((count, LANES), BF16),
                pltpu.VMEM((count, units), F32),
            ],
        ),
        out_shape=[out(own_shape, BF16)] * 4
        + [
            out((4,) + own_shape, BF16),
            out((2, count, 2 * units), BF16),
            out((2, eight, half, units), BF16),
            out((2, count, units), BF16),
        ],
        compiler_params=pltpu.CompilerParams(vmem_limit_bytes=48 << 20),
        cost_estimate=pl.CostEstimate(
            flops=8 * count * gate_up_t.size,
            bytes_accessed=8 * count * width + 4 * gate_up_t.size + 20 * count * units,
            transcendentals=2 * count * units,
        ),
        name="experts",
    )(at, *rows, cot, lead, w_gate, w_up, gate_up_t, router)


def mix_kernel(scaled_ref, down_ref, *refs):
    width = down_ref.shape[1]
    half = LANES // 2
    step = 512
    for c in range(width // step):
        cols = slice(c * step, (c + 1) * step)
        part = dot(scaled_ref[0], down_ref[:, cols])
        for n in range(4):
            some = part[n * LANES : (n + 1) * LANES].reshape(2, half, step)
            if len(refs) == 1:
                refs[0][n, :, 0, :, cols] = some.astype(BF16)
            else:
                more = refs[0][n, :, 0, :, cols].astype(F32)
                refs[1 + n][:, 0, :, cols] = (some + more).astype(BF16)


def mix_call(scaled, down, *others):
    chips, count, units = scaled.shape
    width = down.shape[1]
    shape = (2, chips, LANES // 2, width)
    quad = pl.BlockSpec((2, 1, LANES // 2, width), lambda i: (0, i, 0, 0))
    quads = pl.BlockSpec((4, 2, 1, LANES // 2, width), lambda i: (0, 0, i, 0, 0))
    return pl.pallas_call(
        mix_kernel,
        grid=(chips,),
        in_specs=[
            pl.BlockSpec((1, count, units), lambda i: (i, 0, 0)),
            whole(down.shape),
        ]
        + [quads] * len(others),
        out_specs=[quad] * 4 if others else quads,
        out_shape=[out(shape, BF16)] * 4 if others else out((4,) + shape, BF16),
        cost_estimate=pl.CostEstimate(
            flops=2 * scaled.size * width,
            bytes_accessed=2 * scaled.size + 2 * down.size + 4 * chips * count * width,
            transcendentals=0,
        ),
        name="mix",
    )(scaled, down, *others)


def row_grad_kernel(count, *refs):
    rows_refs, grads_refs, out_ref = refs[:count], refs[count:-1], refs[-1]
    _, step, unit_part = out_ref.shape
    total = jnp.zeros((step, 2 * unit_part), F32)
    for n, ref in enumerate(rows_refs):
        total = total + t_dot(ref[...].reshape(-1, step), grads_refs[n // 2][n % 2])
    for e in range(2):
        out_ref[e] = total[:, e * unit_part : (e + 1) * unit_part]


def row_grad_call(groups, which):
    step = 256
    rows = [r for pair, _ in groups for r in pair]
    eight, half, width = rows[0].shape
    _, count, four = groups[0][1].shape
    units = four // 2
    held = pl.BlockSpec((2, count, units), lambda i: (0, 0, which), pipeline_mode=pl.Buffered(1))
    return pl.pallas_call(
        lambda *refs: row_grad_kernel(len(rows), *refs),
        grid=(width // step,),
        in_specs=[pl.BlockSpec((eight, half, step), lambda i: (0, 0, i))] * len(rows)
        + [held] * len(groups),
        out_specs=pl.BlockSpec((2, step, units // 2), lambda i: (0, i, 0)),
        out_shape=out((2, width, units // 2), F32),
        cost_estimate=pl.CostEstimate(
            flops=2 * len(rows) * count * width * units,
            bytes_accessed=2 * len(rows) * count * (width + units) + 4 * width * units,
            transcendentals=0,
        ),
        name="row_grads",
    )(*rows, *[g for _, g in groups])


def down_grad_kernel(count, at_ref, *refs):
    scaled_refs, cot_refs, out_ref = refs[:count], refs[count:-1], refs[-1]
    _, unit_part, step = out_ref.shape
    total = jnp.zeros((2 * unit_part, step), F32)
    for n, scaled_ref in enumerate(scaled_refs):
        for side in range(2):
            cot = cot_refs[2 * n + side][...].reshape(-1, step)
            total = total + t_dot(scaled_ref[side].reshape(-1, 2 * unit_part), cot)
    for e in range(2):
        out_ref[e] = total[e * unit_part : (e + 1) * unit_part]


def down_grad_call(at, scaled, cot):
    step = 256
    shards, _, _, two, half, columns = cot.shape
    _, eight, _, units = scaled[0].shape
    width = (columns // step) * step
    count = len(scaled)

    def tile(n, side):
        return pl.BlockSpec(
            (shards, 1, 1, two, half, step),
            lambda i, at: (0, at[1 + n], lax.rem(at[0] + side, 2), 0, 0, i),
        )

    return pl.pallas_call(
        lambda *refs: down_grad_kernel(count, *refs),
        grid_spec=pltpu.PrefetchScalarGridSpec(
            num_scalar_prefetch=1,
            grid=(width // step,),
            in_specs=[
                pl.BlockSpec(
                    s.shape, lambda i, _: (0, 0, 0, 0), pipeline_mode=pl.Buffered(1)
                )
                for s in scaled
            ]
            + [tile(n, side) for n in range(count) for side in range(2)],
            out_specs=pl.BlockSpec((2, units // 2, step), lambda i, _: (0, 0, i)),
        ),
        out_shape=out((2, units // 2, width), F32),
        cost_estimate=pl.CostEstimate(
            flops=4 * count * eight * half * width * units,
            bytes_accessed=4 * count * eight * half * (width + units) + 4 * width * units,
            transcendentals=0,
        ),
        name="down_grads",
    )(at, *scaled, *([cot] * (2 * count)))


def add_up(parts):
    total = parts[0]
    for part in parts[1:]:
        total = total + part
    return total


def turn_kernel(
    experts_all,
    ring_ref,
    a0,
    a1,
    a2,
    b0,
    b1,
    b2,
    residual_ref,
    cot_ref,
    mixed_ref,
    router_ref,
    router_rows_ref,
    gain_ref,
    grad_ref,
    grad_b_ref,
    gain_grad_ref,
    router_grad_ref,
):
    width = residual_ref.shape[2]
    half = residual_ref.shape[1]
    lane = lax.broadcasted_iota(jnp.int32, (half, LANES), 1)
    gain_grad, router_grad = None, None
    for n, refs in enumerate(((a0, a1, a2), (b0, b1, b2))):
        back = ring_ref[n].astype(F32) + total_of([r[...] for r in refs])
        mixed = mixed_ref[n]
        powers = jnp.where(lane < experts_all, jnp.exp(dot(mixed, router_ref[...])), 0.0)
        probs = powers / jnp.sum(powers, axis=-1, keepdims=True)
        prob_grad = back[:, width:]
        logit_grad = (
            probs * (prob_grad - jnp.sum(probs * prob_grad, axis=-1, keepdims=True))
        ).astype(BF16)
        mixed_grad = back[:, :width] + dot(logit_grad, router_rows_ref[...])
        residual = residual_ref[n]
        norm_grad, gain_now = norm_back(mixed_grad, residual, rms_scale(residual), gain_ref[...])
        total = cot_ref[n] + norm_grad
        grad_ref[n] = total
        grad_b_ref[n] = total.astype(BF16)
        router_now = t_dot(logit_grad, mixed)
        gain_grad = gain_now if gain_grad is None else gain_grad + gain_now
        router_grad = router_now if router_grad is None else router_grad + router_now
    gain_grad_ref[...] = jnp.broadcast_to(gain_grad, gain_grad_ref.shape)
    router_grad_ref[...] = router_grad[: router_grad_ref.shape[0]]


def output_grad_kernel(core_ref, g0, g1, g2, g3, attended_ref, own_ref, other_ref):
    blocks, half, step = own_ref.shape
    own_cols = pl.ds(pl.multiple_of(core_ref[0] * half, half), half)
    other_cols = pl.ds(pl.multiple_of((1 - core_ref[0]) * half, half), half)
    for c in range(blocks):
        cols = slice(c * step, (c + 1) * step)
        grads = jnp.concatenate(
            [g[:, :, cols].reshape(LANES, step) for g in (g0, g1, g2, g3)], axis=0
        )
        own_ref[c] = t_dot(attended_ref[:, own_cols], grads)
        other_ref[c] = t_dot(attended_ref[:, other_cols], grads).astype(BF16)


def attend_back_kernel(
    g0,
    g1,
    g2,
    g3,
    w_ref,
    attended_ref,
    q_ref,
    k_ref,
    v_ref,
    lse_ref,
    scales_ref,
    bias_ref,
    cos_ref,
    sin_ref,
    gain_q_ref,
    gain_k_ref,
    proj_ref,
    query_ref,
    key_ref,
    value_ref,
    stats_ref,
    gains_ref,
    grad_ref,
):
    part, width = w_ref.shape
    rows = proj_ref.shape[0]
    grad_ref[...] = jnp.concatenate(
        [g[...].reshape(LANES, width) for g in (g0, g1, g2, g3)], axis=0
    )
    q_scale, k_scale = scales_ref[:, 0:1], scales_ref[:, 1:2]
    cosine, sine_part = cos_ref[...], sin_ref[...]
    q_inner = jnp.zeros((rows, 1), F32)
    k_inner = jnp.zeros((rows, 1), F32)
    for h in range(part // HEAD_DIM):
        cols = slice(h * HEAD_DIM, (h + 1) * HEAD_DIM)
        k_cols = slice(part + h * HEAD_DIM, part + (h + 1) * HEAD_DIM)
        attended_grad = dot_t(grad_ref[...], w_ref[cols, :]).astype(BF16)
        query, key, value = q_ref[:, cols], k_ref[:, cols], v_ref[:, cols]
        probs = jnp.exp(
            dot_t(query, key) * SCORE_SCALE + bias_ref[...] - lse_ref[:, h : h + 1]
        )
        delta = jnp.sum(
            attended_grad.astype(F32) * attended_ref[:, cols].astype(F32), axis=-1, keepdims=True
        )
        score_grad = (probs * (dot_t(attended_grad, value) - delta)).astype(BF16)
        value_ref[:, cols] = t_dot(probs.astype(BF16), attended_grad).astype(BF16)
        query_grad = dot(score_grad, key) * SCORE_SCALE
        key_grad = t_dot(score_grad, query) * SCORE_SCALE
        query_pre = query_grad * cosine + pltpu.roll(query_grad * sine_part, HEAD_DIM // 2, 1)
        key_pre = key_grad * cosine + pltpu.roll(key_grad * sine_part, HEAD_DIM // 2, 1)
        q_proj, k_proj = proj_ref[:, cols], proj_ref[:, k_cols]
        gains_ref[0:1, cols] = jnp.sum(query_pre * q_proj * q_scale, axis=0, keepdims=True)
        gains_ref[1:2, cols] = jnp.sum(key_pre * k_proj * k_scale, axis=0, keepdims=True)
        query_pre = query_pre * gain_q_ref[:, cols]
        key_pre = key_pre * gain_k_ref[:, cols]
        query_ref[:, cols] = query_pre
        key_ref[:, cols] = key_pre
        q_inner = q_inner + jnp.sum(query_pre * q_proj, axis=-1, keepdims=True)
        k_inner = k_inner + jnp.sum(key_pre * k_proj, axis=-1, keepdims=True)
    for n, stats in enumerate(pack_stats(q_inner, k_inner)):
        stats_ref[n] = stats


def project_back_kernel(
    at_ref, s0, s1, s2, s3, query_ref, key_ref, value_ref, proj_ref, scales_ref, normed_ref, *refs
):
    weight_refs = refs[:8]
    part_refs, pair_ref, all_ref = refs[8:12], refs[12], refs[13]
    width = normed_ref.shape[1]
    part = query_ref.shape[1]
    inner = sum_stats(s0, s1, s2, s3) / width
    for n, (grad_ref, low) in enumerate(((query_ref, 0), (key_ref, part))):
        scale = scales_ref[:, n : n + 1]
        factor = scale * scale * inner[:, n : n + 1]
        all_ref[:, low : low + part] = (
            scale * (grad_ref[...] - proj_ref[:, low : low + part] * factor)
        ).astype(BF16)
    all_ref[:, 2 * part :] = value_ref[...]
    depth = weight_refs[0].shape[0]
    for n, ref in enumerate(weight_refs):
        at = pl.ds(pl.multiple_of(at_ref[n] * depth, depth), depth)
        got = dot_t(all_ref[...], ref[...]).astype(BF16)
        for k, part_ref in enumerate(part_refs):
            part_ref[:, :, at] = got[k * LANES : (k + 1) * LANES].reshape(2, LANES // 2, depth)
    members, parts, rows, _ = pair_ref.shape
    for p in range(parts):
        for third in range(2):
            cols = slice(third * part, (third + 1) * part)
            got = t_dot(normed_ref[:, p * part : (p + 1) * part], all_ref[:, cols]).astype(BF16)
            for e in range(members):
                pair_ref[e, p, :, cols] = got[e * rows : (e + 1) * rows]


def value_back_kernel(core_ref, value_ref, normed_ref, own_ref, other_ref):
    parts, depth, _ = own_ref.shape
    for p in range(parts):
        for ref, side in ((own_ref, core_ref[0]), (other_ref, 1 - core_ref[0])):
            at = pl.ds(pl.multiple_of((2 * p + side) * depth, depth), depth)
            ref[p] = t_dot(normed_ref[:, at], value_ref[...]).astype(ref.dtype)


def finish_kernel(a0, a1, a2, b0, b1, b2, x_ref, grad_ref, gain_ref, out_ref, gain_grad_ref):
    gain_grad = None
    for n, refs in enumerate(((a0, a1, a2), (b0, b1, b2))):
        source = x_ref[n].astype(F32)
        normed_grad = total_of([r[...] for r in refs])
        norm_grad, gain_now = norm_back(normed_grad, source, rms_scale(source), gain_ref[...])
        out_ref[n] = grad_ref[n] + norm_grad
        gain_grad = gain_now if gain_grad is None else gain_grad + gain_now
    gain_grad_ref[...] = jnp.broadcast_to(gain_grad, gain_grad_ref.shape)


def cut_kernel(at_ref, *refs):
    sources, (own_ref, spare_ref, x_ref, y_ref) = refs[:15], refs[15:]
    depth, part = sources[0].shape
    rows = depth // 2
    for w in range(3):
        cols = slice(w * part, (w + 1) * part)
        own_ref[:, cols] = sources[w][...]
        x_ref[:depth, cols] = sources[3 + w][...]
        y_ref[:depth, cols] = sources[6 + w][...]
        x_ref[depth:, cols] = sources[9 + w][:rows, :]
        y_ref[depth:, cols] = sources[9 + w][rows:, :]
        spare_ref[:, cols] = sources[12 + w][...]


def cut_call(at, w_query, w_key, w_value):
    rows, width = w_query.shape
    part = width // 4
    depth = rows // 2

    def block(member, core):
        return pl.BlockSpec((depth, part), lambda i, at: (at[core], at[member]))

    full, more = (depth, 3 * part), (3 * depth // 2, 3 * part)
    fulls = [full, full, more, more]
    return pl.pallas_call(
        cut_kernel,
        grid_spec=pltpu.PrefetchScalarGridSpec(
            num_scalar_prefetch=1,
            grid=(1,),
            in_specs=[block(d, 4) for d in range(4) for _ in range(3)]
            + [block(0, 5) for _ in range(3)],
            out_specs=[whole(s) for s in fulls],
        ),
        out_shape=[out(s, BF16) for s in fulls],
        name="cut",
    )(at, *([w_query, w_key, w_value] * 5))


def on_device(
    block_input,
    segment_ids,
    expert_routes,
    attn_gain,
    w_query,
    w_key,
    w_value,
    query_gain,
    key_gain,
    w_output,
    moe_gain,
    w_router,
    w_gate,
    w_up,
    w_down,
    out_cotangent,
):
    expert_count = lax.axis_size("expert")
    shard_count = lax.axis_size("shard")
    chips = expert_count // 2
    me = lax.axis_index("shard")
    place = lax.axis_index("expert")
    core = lax.rem(place, 2)
    chip = place // 2
    tok_count = block_input.shape[1]
    half = tok_count // 2
    group_count = segment_ids.shape[1]
    width = block_input.shape[2]
    part = width // shard_count
    local_experts = w_gate.shape[0]
    experts_all = local_experts * expert_count
    unit_part = w_gate.shape[2]
    units = local_experts * unit_part
    core_at = jnp.reshape(core, (1,))

    own_input = block_input.reshape(2, half, width)
    group_input = [b.reshape(2, half, width) for b in spread_xy(own_input[:1], own_input[1:])]

    small = jnp.concatenate([attn_gain[None], moe_gain[None], w_router.T], axis=0)
    small = jnp.pad(small, ((0, (-small.shape[0]) % 32), (0, 0)))
    small_all = jnp.zeros((small.shape[0], width), BF16)
    small_parts = gather_parts(small)
    for d, got in enumerate(small_parts):
        small_all = lax.dynamic_update_slice_in_dim(small_all, got, (me ^ d) * part, 1)
    gain_one = small_all[0:1].astype(F32)
    gain_two = small_all[1:2].astype(F32)
    router = small_all[2 : 2 + experts_all]
    router = jnp.pad(router, ((0, LANES - experts_all), (0, 0)))
    router_t = router.T

    depth = part // 2
    at = jnp.stack([me, me ^ 1, me ^ 2, me ^ 3, core, 1 - core])
    cuts = cut_call(at, w_query, w_key, w_value)
    gate_up_t, down_t = flip_call(w_gate, w_up, w_down)
    direct = exchange_blocks(
        *after(cuts[2:], group_input[0], group_input[2], small_parts), group_input, gate_up_t
    )
    passed = [swap_core(block) for block in direct]
    weight_blocks = list(cuts[:2]) + direct + passed
    weight_at = jnp.stack(
        [2 * me + core, 2 * me + 1 - core]
        + [2 * (me ^ d) + core for d in (1, 2, 3)]
        + [2 * (me ^ d) + 1 - core for d in (1, 2, 3)]
    )

    routes = expert_routes[0]
    routed = jnp.sum(
        (routes[:, :, None] == jnp.arange(experts_all)[None, None, :]).astype(F32), axis=1
    )
    cotangent = out_cotangent[0]
    cot_block = (
        jnp.concatenate(
            [cotangent, routed, jnp.zeros((tok_count, LANES - experts_all), F32)], axis=1
        )
        .astype(BF16)
    )
    cot = lax.all_gather(cot_block, ("shard", "expert"), axis=0, tiled=True)

    down_w = w_down.reshape(units, width)

    starts = [(me ^ d) * tok_count + side * half for pair in ORDER for side, d in pair]
    position = jnp.concatenate([p + jnp.arange(half) for p in starts])
    seg_all = segment_ids[0]
    seg_here = jnp.concatenate([lax.dynamic_slice_in_dim(seg_all, p, half) for p in starts])
    allowed = (seg_here[:, None] == seg_here[None, :]) & (position[None, :] <= position[:, None])
    bias = jnp.where(allowed, 0.0, -1e30).astype(F32)
    half_dim = HEAD_DIM // 2
    inverse = 10000.0 ** (-(jnp.arange(half_dim).astype(F32) * 2.0) / HEAD_DIM)
    angles = position.astype(F32)[:, None] * inverse[None, :]
    cosine = jnp.concatenate([jnp.cos(angles), jnp.cos(angles)], axis=-1)
    sine_part = jnp.concatenate([-jnp.sin(angles), jnp.sin(angles)], axis=-1)
    gain_query = query_gain.astype(F32)[None]
    gain_key = key_gain.astype(F32)[None]
    normed, proj, squares, scale_one = call(
        project_kernel,
        "project",
        [weight_at] + group_input + [gain_one] + weight_blocks,
        [
            out((group_count, width), BF16),
            out((group_count, 3 * part), F32),
            out((4, 8, LANES), F32),
            out((group_count, LANES), F32),
        ],
        2 * group_count * width * 3 * part,
        smem=(0,),
    )
    quad = out((2, half, width), BF16)
    square_parts = out((group_count, part), BF16)
    heads = call(
        lambda *refs: attend_kernel(width, *refs),
        "attend",
        [proj] + gather_parts(squares) + [gain_query, gain_key, cosine, sine_part, bias, w_output],
        [square_parts] * 3
        + [out((group_count, LANES), F32)] * 2
        + [square_parts]
        + [quad] * 4,
        4 * group_count * group_count * part + 2 * group_count * part * width,
    )
    q_heads, k_heads, v_heads, log_total, scales, attended = heads[:6]
    terms_a, terms_b = reduce_xy([b.reshape(2, 1, half, width) for b in heads[6:]])
    residual, mixed_in = call(
        settle_kernel,
        "settle",
        [own_input]
        + [t.reshape(half, width) for t in terms_a + terms_b]
        + [gain_two],
        [out((2, half, width), F32), out((2, half, width), BF16)],
        tok_count * width,
    )

    pieces = [mixed_in, ring_up(mixed_in)]
    cot = after(cot, mixed_in).reshape(shard_count, chips, 2, 2, half, width + LANES)
    lead = lead_call(cot, down_t)
    pieces[1] = after(pieces[1], lead)
    while len(pieces) < chips:
        pieces.append(ring_up(pieces[-1]))
    chip_at = [lax.rem(chip + chips - j, chips) for j in range(chips)]
    lows, low = [0, 1], 2
    while low < chips:
        lows.append(low)
        low *= 2
    lows.append(chips)
    all_rows, firsts = [], []
    for low, high in zip(lows[:-1], lows[1:]):
        sides = [jnp.stack([p[s] for p in pieces[low:high]]) for s in range(2)]
        pair_a = jnp.stack([sides[0], swap_x(sides[0])])
        pair_b = jnp.stack([sides[1], swap_y(sides[1])])
        firsts.append((pair_a, pair_b))
        if low > 1:
            pair_a, pair_b = after((pair_a, pair_b), all_rows[1][0])
        parts = [pair_a, swap_y(pair_a), pair_b, swap_x(pair_b)]
        for j in range(high - low):
            own = join_call(parts, j)
            all_rows.append((own, swap_core(own)))
    groups, totals_all = [], []
    for j in range(chips):
        at = jnp.stack([place, me, chip_at[j], core])
        at = after(at, totals_all[j - 2] if j > 1 else firsts[:3])
        got = expert_call(
            at, all_rows[j], cot, lead, w_gate, w_up, gate_up_t, router_t, experts_all
        )
        groups.append((all_rows[j], got[5], got[6], got[7]))
        if 0 < j < chips - 1:
            passed_back = swap_core(after(got[4], all_rows[j + 1][1]))
        else:
            passed_back = swap_core(got[4])
        totals_all.append(
            [
                (a.astype(F32) + passed_back[n].astype(F32)).astype(BF16)
                for n, a in enumerate(got[:4])
            ]
        )
    back_terms = [None] * chips

    def back_piece(j):
        return jnp.stack([total_of(terms) for terms in back_terms[j]])

    back_pieces, arrived = [], []
    for j in list(range(1, chips)) + [0]:
        totals = totals_all[j]
        if j == 0:
            totals = after(totals, totals_all[-1], arrived[0])
        back_terms[j] = [
            [t[0] for t in terms]
            for terms in reduce_xy(
                after(totals, [r[0] for r in all_rows]),
                totals_all[min(j + 2, chips - 1)],
                back_pieces[-1:],
                arrived[-1:],
            )
        ]
        if j:
            back_pieces.append(back_piece(j))
        if j == 1:
            ring_total = back_pieces[0].astype(BF16)
        elif j:
            arrived.append(ring_up(ring_total))
            ring_total = (arrived[-1].astype(F32) + back_pieces[-1]).astype(BF16)
    scaled_sides = [
        jnp.concatenate([g[3][side : side + 1] for g in groups]) for side in range(2)
    ]
    mix_passed = swap_core(mix_call(after(scaled_sides[1], arrived[0], back_pieces[1]), down_w))

    ring_total = ring_up(ring_total)
    grad_res, grad_res_b, grad_gain_two, grad_router = call(
        lambda *refs: turn_kernel(experts_all, *refs),
        "turn",
        [ring_total]
        + back_terms[0][0]
        + back_terms[0][1]
        + [residual, cotangent.reshape(2, half, width), mixed_in, router_t, router]
        + [gain_two],
        [
            out((2, half, width), F32),
            out((2, half, width), BF16),
            out((8, width), F32),
            out((experts_all, width), F32),
        ],
        8 * tok_count * width * LANES,
    )

    group_grad = [b.reshape(2, half, width) for b in spread_xy(grad_res_b[:1], grad_res_b[1:])]
    out_totals = mix_call(
        after(scaled_sides[0], group_grad[0], group_grad[2]), down_w, mix_passed
    )
    output_own, output_other = call(
        output_grad_kernel,
        "output_grad",
        [core_at] + after(group_grad, out_totals) + [attended],
        [out((4, part // 2, width // 4), F32), out((4, part // 2, width // 4), BF16)],
        2 * group_count * part * width,
        smem=(0,),
    )
    query_pre, key_pre, value_grad, inner, gain_grads, _ = call(
        attend_back_kernel,
        "attend_back",
        after(group_grad, output_other)
        + [w_output, attended, q_heads, k_heads, v_heads, log_total, scales, bias]
        + [cosine, sine_part, gain_query, gain_key, proj],
        [
            out((group_count, part), F32),
            out((group_count, part), F32),
            square_parts,
            out((4, 8, LANES), F32),
            out((8, part), F32),
            out((group_count, width), BF16),
        ],
        10 * group_count * group_count * part + 2 * group_count * part * width,
    )
    def split_rows(own):
        parts, rows, columns = own.shape
        split = own.reshape(parts, chips, rows // chips, columns)
        return [lax.dynamic_index_in_dim(split, at, 1, keepdims=False) for at in chip_at]

    inner_parts = gather_parts(inner)
    keep_a, send_a, keep_b, send_b = after(out_totals, inner_parts)
    got_a, got_b = swap_y(send_a), swap_x(send_b)
    out_far = (
        (keep_a[1].astype(F32) + got_a[1].astype(F32)).astype(BF16),
        (keep_b[1].astype(F32) + got_b[1].astype(F32)).astype(BF16),
    )
    out_terms = (
        (keep_a[0], got_a[0], swap_x(out_far[0])),
        (keep_b[0], got_b[0], swap_y(out_far[1])),
    )

    def out_piece(j):
        return jnp.stack([total_of([t[j] for t in side]) for side in out_terms])

    def ring_add(total, pieces, *others):
        moved = after(ring_up(total), *others)
        return (moved.astype(F32) + pieces.pop(0)).astype(BF16)

    output_passed = after(swap_core(output_other), query_pre)
    output_pieces = split_rows(output_own + output_passed.astype(F32))
    output_pieces = output_pieces[1:] + output_pieces[:1]
    output_total = output_pieces.pop(0).astype(BF16)
    value_own, value_other = call(
        value_back_kernel,
        "value_back",
        [core_at] + after([value_grad], inner, output_total) + [normed],
        [out((4, depth, part), F32), out((4, depth, part), BF16)],
        2 * group_count * width * part,
        smem=(0,),
    )
    value_passed = swap_core(value_other)
    output_total = ring_add(output_total, output_pieces, value_other)
    got = call(
        project_back_kernel,
        "project_back",
        [weight_at]
        + inner_parts
        + after([query_pre, key_pre, value_grad, proj, scales, normed], output_total)
        + weight_blocks,
        [quad] * 4
        + [
            out((expert_count, 4, part // expert_count, 2 * part), BF16),
            out((group_count, 3 * part), BF16),
        ],
        4 * group_count * width * 3 * part,
        smem=(0,),
    )
    def exchange_grads(piece):
        sent = [lax.dynamic_index_in_dim(piece, me ^ d, 0, keepdims=False) for d in range(4)]
        low = sent[3].shape[0] // 2
        arrived = exchange_blocks(
            jnp.concatenate([sent[1], sent[3][:low]], axis=0),
            jnp.concatenate([sent[2], sent[3][low:]], axis=0),
        )
        return jnp.stack([sent[0]] + arrived)

    def whole_grads(rows):
        shares = [lax.dynamic_index_in_dim(rows, me ^ p, 0, keepdims=False) for p in range(4)]
        return [
            jnp.concatenate(
                [share[:, n * part : (n + 1) * part] for share in shares], axis=1
            ).astype(F32)
            for n in range(rows.shape[2] // part)
        ]

    pair_sums = lax.psum_scatter(got[4], "expert", scatter_dimension=0, tiled=True)[0]

    output_total = ring_add(output_total, output_pieces, got[0])
    value_pieces = split_rows(after(value_own + value_passed.astype(F32), output_total))
    value_pieces = value_pieces[1:] + value_pieces[:1]
    total = value_pieces.pop(0).astype(BF16)
    span = min(chips, 4)
    starts = range(0, chips, span)

    def row_grads(which, *others):
        late = after([g[1] for g in groups], *others)
        return add_up(
            [
                row_grad_call([(g[0], v) for g, v in zip(groups, late)][low : low + span], which)
                for low in starts
            ]
        )

    def down_grads(*others):
        late = after([g[2] for g in groups], *others)
        return add_up(
            [
                down_grad_call(
                    jnp.stack([core] + chip_at[low : low + span]), late[low : low + span], cot
                )
                for low in starts
            ]
        )

    expert_grads = []
    out_spread = []
    while len(value_pieces) > 1:
        if not expert_grads:
            expert_grads.append(down_grads(total))
            terms_a, terms_b = reduce_xy(
                [b.reshape(2, 1, half, width) for b in got[:4]], expert_grads[0]
            )
        elif len(expert_grads) == 1:
            expert_grads.append(row_grads(0, total, out_far, output_total))
            grad_input, grad_gain_one = call(
                finish_kernel,
                "finish",
                [t.reshape(half, width) for t in terms_a + terms_b]
                + [own_input, grad_res, after(gain_one, expert_grads[1])],
                [out((2, half, width), F32), out((8, width), F32)],
                tok_count * width,
            )
        total = ring_add(total, value_pieces, expert_grads[-1])
        if output_pieces:
            output_total = ring_add(output_total, output_pieces, total)
        if not output_pieces:
            out_spread.append(
                after(ring_up(out_spread[-1]), total) if out_spread else output_total
            )
    out_now = out_piece(1).astype(BF16)
    pair_mine = exchange_grads(after(pair_sums, grad_gain_one, out_spread[-1], out_now))
    pair_rows = lax.all_gather(pair_mine, "expert", axis=0)
    total = ring_add(total, value_pieces, pair_mine)
    spread = [exchange_grads(total)]
    expert_grads.append(row_grads(1, spread[0], out_now))
    grad_w_down, grad_w_gate, grad_w_up = expert_grads
    for j in range(1, chips):
        moved = after(ring_up(out_now), grad_w_up)
        if j + 1 < chips:
            out_now = (moved.astype(F32) + out_piece(j + 1)).astype(BF16)
        spread.append(after(ring_up(spread[-1]), out_now if j + 1 < chips else moved))
        if len(out_spread) < chips:
            out_spread.append(after(ring_up(out_spread[-1]), spread[-1]))
    while len(out_spread) < chips:
        out_spread.append(ring_up(out_spread[-1]))
    block_output = residual + (moved.astype(F32) + out_piece(0))
    early_rows = expert_spread(out_spread, core, chip)
    grad_w_output = jnp.concatenate([early_rows[c] for c in range(4)], axis=1).astype(F32)
    (grad_w_value,) = whole_grads(expert_spread(spread, core, chip))
    pair_rows = jnp.transpose(pair_rows, (1, 0, 2, 3)).reshape(4, part, 2 * part)
    grad_w_query, grad_w_key = whole_grads(pair_rows)

    grad_gain_one = after(grad_gain_one, spread[0])
    packed = jnp.concatenate([grad_gain_one[:1], grad_gain_two[:1], grad_router], axis=0)
    rows_used = packed.shape[0]
    packed = jnp.pad(packed, ((0, (-rows_used) % 16), (0, 0)))
    quarters = jnp.stack(
        [lax.dynamic_slice_in_dim(packed, (me ^ d) * part, part, 1) for d in range(4)]
    )
    quarters = quarters[:2] + swap_y(quarters[2:])
    packed = (quarters[0] + swap_x(quarters[1]))[:rows_used]
    packed = after(jnp.concatenate([packed, gain_grads[:2]], axis=0), spread[-1])
    bit = 1
    while bit < expert_count:
        packed = packed + flip_expert(packed, bit)
        bit *= 2
    return (
        block_output.reshape(1, tok_count, width),
        grad_input.reshape(1, tok_count, width),
        packed[0],
        grad_w_query,
        grad_w_key,
        grad_w_value,
        packed[rows_used],
        packed[rows_used + 1],
        grad_w_output,
        packed[1],
        packed[2 : 2 + experts_all].T,
        grad_w_gate,
        grad_w_up,
        grad_w_down,
    )


def solution(mesh):
    placed = (
        P("expert", "shard", None),
        P("expert", None),
        P("expert", "shard", None),
        P("shard"),
        P("shard", None),
        P("shard", None),
        P("shard", None),
        P("shard"),
        P("shard"),
        P("shard", None),
        P("shard"),
        P("shard", None),
        P("expert", None, "shard"),
        P("expert", None, "shard"),
        P("expert", "shard", None),
        P("expert", "shard", None),
    )
    return jax.shard_map(
        on_device,
        mesh=mesh,
        in_specs=placed,
        out_specs=(
            P("expert", "shard", None),
            P("expert", "shard", None),
            P("shard"),
            P("shard", None),
            P("shard", None),
            P("shard", None),
            P("shard"),
            P("shard"),
            P("shard", None),
            P("shard"),
            P("shard", None),
            P("expert", None, "shard"),
            P("expert", None, "shard"),
            P("expert", "shard", None),
        ),
        check_vma=False,
    )
```

```python
import jax
import jax.numpy as jnp
from jax import lax
from jax.experimental import pallas as pl
from jax.experimental.pallas import tpu as pltpu
from jax.sharding import PartitionSpec as P

HEAD_DIM = 128
LANES = 128
EPSILON = 1e-05
SCORE_SCALE = HEAD_DIM ** (-0.5)
F32 = jnp.float32
BF16 = jnp.bfloat16
ORDER = (((0, 0), (0, 1)), ((0, 2), (0, 3)), ((1, 0), (1, 2)), ((1, 1), (1, 3)))


def dot(a, b):
    return jnp.dot(a, b, preferred_element_type=F32)


def dot_t(a, b):
    return lax.dot_general(a, b, (((1,), (1,)), ((), ())), preferred_element_type=F32)


def t_dot(a, b):
    return lax.dot_general(a, b, (((0,), (0,)), ((), ())), preferred_element_type=F32)


def flip_shard(values, bit):
    count = lax.axis_size("shard")
    return lax.ppermute(values, "shard", [(i, i ^ bit) for i in range(count)])


def swap_x(values):
    return flip_shard(values, 1)


def swap_y(values):
    return flip_shard(values, 2)


def swap_far(values):
    return flip_shard(values, 3)


def flip_expert(values, bit):
    count = lax.axis_size("expert")
    return lax.ppermute(values, "expert", [(i, i ^ bit) for i in range(count)])


def swap_core(values):
    return flip_expert(values, 1)


def ring_up(values):
    count = lax.axis_size("expert")
    return lax.ppermute(values, "expert", [(i, (i + 2) % count) for i in range(count)])


def after(values, *others):
    return lax.optimization_barrier((values, others))[0]


def spread_xy(first, second):
    pair_a = jnp.stack([first, swap_x(first)])
    pair_b = jnp.stack([second, swap_y(second)])
    return [pair_a, swap_y(pair_a), pair_b, swap_x(pair_b)]


def reduce_first(blocks, *others):
    keep_a, send_a, keep_b, send_b = blocks
    got_a, got_b = after((swap_y(send_a), swap_x(send_b)), *others)
    on_a = (keep_a[1].astype(F32) + got_a[1].astype(F32)).astype(BF16)
    on_b = (keep_b[1].astype(F32) + got_b[1].astype(F32)).astype(BF16)
    return ((keep_a[0], got_a[0]), (keep_b[0], got_b[0])), (on_a, on_b)


def reduce_last(kept, on):
    return kept[0] + (swap_x(on[0]),), kept[1] + (swap_y(on[1]),)


def reduce_xy(blocks, *others):
    return reduce_last(*reduce_first(blocks, *others))


def total_of(terms):
    total = terms[0].astype(F32)
    for term in terms[1:]:
        total = total + term.astype(F32)
    return total


def exchange_blocks(for_x, for_y, *others):
    got_x, got_y = after((swap_x(for_x), swap_y(for_y)), *others)
    depth = 2 * for_x.shape[0] // 3
    far = jnp.concatenate([swap_y(got_x[depth:]), swap_x(got_y[depth:])], axis=0)
    return [got_x[:depth], got_y[:depth], far]


def gather_parts(part):
    return [part, swap_x(part), swap_y(part), swap_far(part)]


def ring_gather(piece):
    pieces = [piece]
    for _ in range(lax.axis_size("expert") // 2 - 1):
        pieces.append(ring_up(pieces[-1]))
    return pieces


def ring_sum(total, pieces):
    for piece in pieces:
        total = (ring_up(total).astype(F32) + piece).astype(BF16)
    return total


def expert_spread(pieces, core, chip):
    chips = lax.axis_size("expert") // 2
    parts, rows, columns = pieces[0].shape
    spread = jnp.zeros((parts, chips, rows, columns), pieces[0].dtype)
    for j, got in enumerate(pieces):
        spread = lax.dynamic_update_slice_in_dim(
            spread, got[:, None], lax.rem(chip + chips - j, chips), 1
        )
    half = spread.reshape(parts, 1, chips * rows, columns)
    other = swap_core(half)
    first = jnp.where(core == 0, half, other)
    second = jnp.where(core == 0, other, half)
    return jnp.concatenate([first, second], axis=1).reshape(parts, 2 * chips * rows, columns)


def rms_scale(values):
    return lax.rsqrt(jnp.mean(values * values, axis=-1, keepdims=True) + EPSILON)


def norm_back(grad_out, source, scale_now, gain_now):
    weighted = grad_out * gain_now
    inner_mean = jnp.mean(weighted * source, axis=-1, keepdims=True)
    grad_source = scale_now * (weighted - source * scale_now * scale_now * inner_mean)
    grad_gain = jnp.sum(grad_out * source * scale_now, axis=0, keepdims=True)
    return (grad_source, grad_gain)


def whole(shape):
    return pl.BlockSpec(shape, lambda *_: (0,) * len(shape))


def scalars():
    return pl.BlockSpec(memory_space=pltpu.SMEM)


def call(kernel, name, args, outs, flops, smem=(), transcendentals=0):
    moved = sum(a.size * a.dtype.itemsize for a in args) + sum(
        o.size * o.dtype.itemsize for o in outs
    )
    return pl.pallas_call(
        kernel,
        in_specs=[scalars() if n in smem else whole(a.shape) for n, a in enumerate(args)],
        out_specs=[whole(o.shape) for o in outs],
        out_shape=outs,
        cost_estimate=pl.CostEstimate(
            flops=flops, bytes_accessed=moved, transcendentals=transcendentals
        ),
        name=name,
    )(*args)


def out(shape, dtype):
    return jax.ShapeDtypeStruct(shape, dtype)


def pack_stats(first, second):
    rows = first.shape[0]
    lane = lax.broadcasted_iota(jnp.int32, (rows, LANES), 1)
    spread = jnp.where(lane == 0, first, jnp.where(lane == 1, second, 0.0))
    return [spread[n : n + LANES].T[:8] for n in range(0, rows, LANES)]


def sum_stats(mine, from_x, from_y, far):
    def turn(values):
        return pltpu.roll(values, LANES // 2, 1)

    totals = [
        mine[0] + turn(from_x[0]) + from_y[1] + turn(far[1]),
        mine[1] + turn(from_x[1]) + from_y[0] + turn(far[0]),
        mine[2] + from_x[3] + turn(from_y[2]) + turn(far[3]),
        mine[3] + from_x[2] + turn(from_y[3]) + turn(far[2]),
    ]
    pad = jnp.zeros((LANES - 8, LANES), F32)
    return jnp.concatenate([jnp.concatenate([t, pad], axis=0).T for t in totals], axis=0)


def project_kernel(
    at_ref, r0, r1, r2, r3, gain_ref, *refs
):
    weight_refs, (normed_ref, proj_ref, stats_ref, scale_ref) = refs[:8], refs[8:]
    part = proj_ref.shape[1] // 3
    for n, ref in enumerate((r0, r1, r2, r3)):
        source = ref[...].reshape(LANES, ref.shape[2]).astype(F32)
        scale = rms_scale(source)
        rows = slice(n * LANES, (n + 1) * LANES)
        normed_ref[rows, :] = (source * scale * gain_ref[...]).astype(BF16)
        scale_ref[rows, :] = jnp.broadcast_to(scale, (LANES, LANES))
    depth = weight_refs[0].shape[0]
    for third in range(3):
        cols = slice(third * part, (third + 1) * part)
        total = None
        for n, ref in enumerate(weight_refs):
            rows = pl.ds(pl.multiple_of(at_ref[n] * depth, depth), depth)
            more = dot(normed_ref[:, rows], ref[:, cols])
            total = more if total is None else total + more
        proj_ref[:, cols] = total
    q_proj, k_proj = proj_ref[:, :part], proj_ref[:, part : 2 * part]
    packed = pack_stats(
        jnp.sum(q_proj * q_proj, axis=-1, keepdims=True),
        jnp.sum(k_proj * k_proj, axis=-1, keepdims=True),
    )
    for n, stats in enumerate(packed):
        stats_ref[n] = stats


def attend_kernel(
    width, proj_ref, s0, s1, s2, s3, gain_q_ref, gain_k_ref, cos_ref, sin_ref, bias_ref, w_ref, *refs
):
    q_ref, k_ref, v_ref, lse_ref, scales_ref, attended_ref = refs[:6]
    part_refs = refs[6:]
    part = w_ref.shape[0]
    rows = proj_ref.shape[0]
    sums = sum_stats(s0, s1, s2, s3)
    scales = lax.rsqrt(sums / width + EPSILON)
    scales_ref[...] = scales
    lane = lax.broadcasted_iota(jnp.int32, (rows, LANES), 1)
    q_scale, k_scale = scales[:, 0:1], scales[:, 1:2]
    cosine, sine_part = cos_ref[...], sin_ref[...]
    lse_all = jnp.zeros((rows, LANES), F32)
    for h in range(part // HEAD_DIM):
        cols = slice(h * HEAD_DIM, (h + 1) * HEAD_DIM)
        k_cols = slice(part + h * HEAD_DIM, part + (h + 1) * HEAD_DIM)
        v_cols = slice(2 * part + h * HEAD_DIM, 2 * part + (h + 1) * HEAD_DIM)
        query = proj_ref[:, cols] * q_scale * gain_q_ref[:, cols]
        key = proj_ref[:, k_cols] * k_scale * gain_k_ref[:, cols]
        query = (query * cosine + pltpu.roll(query, HEAD_DIM // 2, 1) * sine_part).astype(BF16)
        key = (key * cosine + pltpu.roll(key, HEAD_DIM // 2, 1) * sine_part).astype(BF16)
        value = proj_ref[:, v_cols].astype(BF16)
        q_ref[:, cols] = query
        k_ref[:, cols] = key
        v_ref[:, cols] = value
        scores = dot_t(query, key) * SCORE_SCALE + bias_ref[...]
        top = jnp.max(scores, axis=-1, keepdims=True)
        powers = jnp.exp(scores - top)
        total = jnp.sum(powers, axis=-1, keepdims=True)
        lse_all = jnp.where(lane == h, top + jnp.log(total), lse_all)
        attended_ref[:, cols] = dot((powers / total).astype(BF16), value).astype(BF16)
    lse_ref[...] = lse_all
    step = 512
    for c in range(w_ref.shape[1] // step):
        cols = slice(c * step, (c + 1) * step)
        for n, ref in enumerate(part_refs):
            got = dot(attended_ref[n * LANES : (n + 1) * LANES, :], w_ref[:, cols])
            ref[:, :, cols] = got.astype(BF16).reshape(2, LANES // 2, step)


def settle_kernel(x_ref, a0, a1, a2, b0, b1, b2, gain_ref, residual_ref, mixed_ref):
    for n, refs in enumerate(((a0, a1, a2), (b0, b1, b2))):
        residual = x_ref[n].astype(F32) + total_of([r[...] for r in refs])
        residual_ref[n] = residual
        mixed_ref[n] = (residual * rms_scale(residual) * gain_ref[...]).astype(BF16)


def flip_kernel(gate_ref, up_ref, down_ref, gate_up_t_ref, down_t_ref):
    unit_part = gate_ref.shape[2]
    for e in range(2):
        low = e * unit_part
        gate_up_t_ref[low : low + unit_part, :] = gate_ref[e].T
        gate_up_t_ref[2 * unit_part + low : 2 * unit_part + low + unit_part, :] = up_ref[e].T
        down_t_ref[:, low : low + unit_part] = down_ref[e].T


def flip_call(w_gate, w_up, w_down):
    two, width, unit_part = w_gate.shape
    step = 512
    tall = pl.BlockSpec((two, step, unit_part), lambda i: (0, i, 0))
    return pl.pallas_call(
        flip_kernel,
        grid=(width // step,),
        in_specs=[tall, tall, pl.BlockSpec((two, unit_part, step), lambda i: (0, 0, i))],
        out_specs=[
            pl.BlockSpec((4 * unit_part, step), lambda i: (0, i)),
            pl.BlockSpec((step, 2 * unit_part), lambda i: (i, 0)),
        ],
        out_shape=[out((4 * unit_part, width), BF16), out((width, 2 * unit_part), BF16)],
        cost_estimate=pl.CostEstimate(flops=0, bytes_accessed=12 * w_gate.size, transcendentals=0),
        name="flip",
    )(w_gate, w_up, w_down)


def lead_kernel(cot_ref, down_t_ref, lead_ref):
    width = down_t_ref.shape[0]
    cot = cot_ref[...].reshape(-1, cot_ref.shape[5])[:, :width]
    lead_ref[0, 0] = dot(cot, down_t_ref[...]).reshape(lead_ref.shape[2:])


def lead_call(cot, down_t):
    shards, chips, cores, two, rows, columns = cot.shape
    width, units = down_t.shape
    count = shards * two * rows
    return pl.pallas_call(
        lead_kernel,
        grid=(chips, cores),
        in_specs=[
            pl.BlockSpec((shards, 1, 1, two, rows, columns), lambda i, c: (0, i, c, 0, 0, 0)),
            whole(down_t.shape),
        ],
        out_specs=pl.BlockSpec((1, 1, shards * two, rows, units), lambda i, c: (i, c, 0, 0, 0)),
        out_shape=out((chips, cores, shards * two, rows, units), F32),
        cost_estimate=pl.CostEstimate(
            flops=2 * chips * cores * count * down_t.size,
            bytes_accessed=2 * cot.size + 4 * chips * cores * count * units,
            transcendentals=0,
        ),
        name="lead",
    )(cot, down_t)


def join_kernel(a_ref, b_ref, c_ref, d_ref, out_ref):
    for n, ref in enumerate((a_ref, b_ref, c_ref, d_ref)):
        out_ref[2 * n : 2 * n + 2] = ref[:, 0]


def join_call(parts, j):
    two, _, rows, width = parts[0].shape
    step = rows // 2
    return pl.pallas_call(
        join_kernel,
        grid=(2,),
        in_specs=[pl.BlockSpec((two, 1, step, width), lambda i: (0, j, i, 0))] * 4,
        out_specs=pl.BlockSpec((4 * two, step, width), lambda i: (0, i, 0)),
        out_shape=out((4 * two, rows, width), BF16),
        cost_estimate=pl.CostEstimate(
            flops=0, bytes_accessed=16 * two * rows * width, transcendentals=0
        ),
        name="join",
    )(*parts)


def expert_kernel(experts_all, at_ref, *refs):
    row_refs, routed_ref, lead_ref = refs[:2], refs[2], refs[3]
    gate_ref, up_ref, gate_up_t_ref, router_ref = refs[4:8]
    own_refs, other_ref, grads_ref, scaled_out, scaled_ref = (
        refs[8:12],
        refs[12],
        refs[13],
        refs[14],
        refs[15],
    )
    rows_ref, mask_ref, lead_here_ref = refs[16:]
    width = router_ref.shape[0]
    units = lead_here_ref.shape[1]
    unit_part = units // 2
    half = LANES // 2
    me = at_ref[1]
    now = pl.program_id(0)
    blocks = [block for pair in ORDER for block in pair]
    for side in range(2):

        @pl.when(now == side)
        def _():
            rows_ref[...] = row_refs[side][...].reshape(rows_ref.shape)

    for n, (part, d) in enumerate(blocks):
        to = slice(n * half, (n + 1) * half)
        mask_ref[to, :] = routed_ref[me ^ d, 0, 0, part]
        lead_here_ref[to, :] = lead_ref[0, 0, 2 * (me ^ d) + part]
    rows = rows_ref[...]
    count = rows.shape[0]
    lane = lax.broadcasted_iota(jnp.int32, (count, LANES), 1)
    routed = mask_ref[...].astype(F32)
    powers = jnp.where(lane < experts_all, jnp.exp(dot(rows, router_ref[...])), 0.0)
    weights = powers * routed / jnp.sum(powers, axis=-1, keepdims=True)
    spot = jnp.zeros((count, LANES), F32)
    for e in range(2):
        here = (lane == at_ref[0] * 2 + e).astype(F32)
        chosen = jnp.sum(weights * here, axis=-1, keepdims=True)
        low = e * unit_part
        gate_pre = dot(rows, gate_ref[e])
        up_pre = dot(rows, up_ref[e])
        lead = lead_here_ref[:, low : low + unit_part]
        sigmoid_gate = 1.0 / (1.0 + jnp.exp(-gate_pre))
        silu_gate = gate_pre * sigmoid_gate
        hidden = (silu_gate * up_pre).astype(BF16).astype(F32)
        spot = spot + jnp.sum(hidden * lead, axis=-1, keepdims=True) * (here * routed)
        grad_hidden = lead * chosen
        gate_grad = grad_hidden * up_pre * sigmoid_gate * (1.0 + gate_pre * (1.0 - sigmoid_gate))
        grads_ref[0, :, low : low + unit_part] = gate_grad.astype(BF16)
        grads_ref[0, :, units + low : units + low + unit_part] = (grad_hidden * silu_gate).astype(
            BF16
        )
        scaled_ref[0, :, low : low + unit_part] = (hidden * chosen).astype(BF16)
    for n, (part, d) in enumerate(blocks):
        scaled_out[0, 2 * (me ^ d) + part] = scaled_ref[0, n * half : (n + 1) * half, :]
    mask_ref[...] = spot.astype(BF16)
    step = 512

    @pl.when(now == 0)
    def _():
        for n, ref in enumerate(own_refs):
            at = slice(n * LANES, (n + 1) * LANES)
            ref[:, 0, :, width:] = mask_ref[at, :].reshape(2, half, LANES)
        for c in range(width // step):
            cols = slice(c * step, (c + 1) * step)
            part = dot(grads_ref[0], gate_up_t_ref[:, cols]).astype(BF16)
            for n, ref in enumerate(own_refs):
                at = slice(n * LANES, (n + 1) * LANES)
                ref[:, 0, :, cols] = part[at].reshape(2, half, step)

    @pl.when(now == 1)
    def _():
        for n in range(4):
            at = slice(n * LANES, (n + 1) * LANES)
            other_ref[n, :, 0, :, width:] = mask_ref[at, :].reshape(2, half, LANES)
        for c in range(width // step):
            cols = slice(c * step, (c + 1) * step)
            part = dot(grads_ref[0], gate_up_t_ref[:, cols]).astype(BF16)
            for n in range(4):
                at = slice(n * LANES, (n + 1) * LANES)
                other_ref[n, :, 0, :, cols] = part[at].reshape(2, half, step)


def expert_call(at, rows, cot, lead, w_gate, w_up, gate_up_t, router, experts_all):
    eight, half, width = rows[0].shape
    shards, units = cot.shape[0], lead.shape[4]
    count = eight * half
    own_shape = (2, 1, half, width + LANES)

    def core_of(i, at):
        return lax.rem(at[3] + i, 2)

    return pl.pallas_call(
        lambda *refs: expert_kernel(experts_all, *refs),
        grid_spec=pltpu.PrefetchScalarGridSpec(
            num_scalar_prefetch=1,
            grid=(2,),
            in_specs=[
                pl.BlockSpec(r.shape, lambda i, _: (0, 0, 0), pipeline_mode=pl.Buffered(1))
                for r in rows
            ]
            + [
                pl.BlockSpec(
                    (shards, 1, 1, 2, half, LANES),
                    lambda i, at: (0, at[2], core_of(i, at), 0, 0, width // LANES),
                ),
                pl.BlockSpec(
                    (1, 1, eight, half, units), lambda i, at: (at[2], core_of(i, at), 0, 0, 0)
                ),
            ]
            + [
                pl.BlockSpec(
                    w.shape, lambda i, _, n=w.ndim: (0,) * n, pipeline_mode=pl.Buffered(1)
                )
                for w in (w_gate, w_up, gate_up_t, router)
            ],
            out_specs=[whole(own_shape) for _ in range(4)]
            + [
                whole((4,) + own_shape),
                pl.BlockSpec((1, count, 2 * units), lambda i, _: (i, 0, 0)),
                pl.BlockSpec((1, eight, half, units), lambda i, _: (i, 0, 0, 0)),
                pl.BlockSpec((1, count, units), lambda i, _: (i, 0, 0)),
            ],
            scratch_shapes=[
                pltpu.VMEM((count, width), BF16),
                pltpu.VMEM((count, LANES), BF16),
                pltpu.VMEM((count, units), F32),
            ],
        ),
        out_shape=[out(own_shape, BF16)] * 4
        + [
            out((4,) + own_shape, BF16),
            out((2, count, 2 * units), BF16),
            out((2, eight, half, units), BF16),
            out((2, count, units), BF16),
        ],
        compiler_params=pltpu.CompilerParams(vmem_limit_bytes=38 << 20),
        cost_estimate=pl.CostEstimate(
            flops=8 * count * gate_up_t.size,
            bytes_accessed=8 * count * width + 4 * gate_up_t.size + 20 * count * units,
            transcendentals=2 * count * units,
        ),
        name="experts",
    )(at, *rows, cot, lead, w_gate, w_up, gate_up_t, router)


def mix_kernel(scaled_ref, down_ref, *refs):
    width = down_ref.shape[1]
    half = LANES // 2
    step = 512
    for c in range(width // step):
        cols = slice(c * step, (c + 1) * step)
        part = dot(scaled_ref[0], down_ref[:, cols])
        for n in range(4):
            some = part[n * LANES : (n + 1) * LANES].reshape(2, half, step)
            if len(refs) == 1:
                refs[0][n, :, 0, :, cols] = some.astype(BF16)
            else:
                more = refs[0][n, :, 0, :, cols].astype(F32)
                refs[1 + n][:, 0, :, cols] = (some + more).astype(BF16)


def mix_call(scaled, down, *others):
    chips, count, units = scaled.shape
    width = down.shape[1]
    shape = (2, chips, LANES // 2, width)
    quad = pl.BlockSpec((2, 1, LANES // 2, width), lambda i: (0, i, 0, 0))
    quads = pl.BlockSpec((4, 2, 1, LANES // 2, width), lambda i: (0, 0, i, 0, 0))
    return pl.pallas_call(
        mix_kernel,
        grid=(chips,),
        in_specs=[
            pl.BlockSpec((1, count, units), lambda i: (i, 0, 0)),
            whole(down.shape),
        ]
        + [quads] * len(others),
        out_specs=[quad] * 4 if others else quads,
        out_shape=[out(shape, BF16)] * 4 if others else out((4,) + shape, BF16),
        cost_estimate=pl.CostEstimate(
            flops=2 * scaled.size * width,
            bytes_accessed=2 * scaled.size + 2 * down.size + 4 * chips * count * width,
            transcendentals=0,
        ),
        name="mix",
    )(scaled, down, *others)


def row_grad_kernel(count, *refs):
    rows_refs, grads_refs, out_ref = refs[:count], refs[count:-1], refs[-1]
    _, step, unit_part = out_ref.shape
    total = jnp.zeros((step, 2 * unit_part), F32)
    for n, ref in enumerate(rows_refs):
        total = total + t_dot(ref[...].reshape(-1, step), grads_refs[n // 2][n % 2])
    for e in range(2):
        out_ref[e] = total[:, e * unit_part : (e + 1) * unit_part]


def row_grad_call(groups, which):
    step = 256
    rows = [r for pair, _ in groups for r in pair]
    eight, half, width = rows[0].shape
    _, count, four = groups[0][1].shape
    units = four // 2
    held = pl.BlockSpec((2, count, units), lambda i: (0, 0, which), pipeline_mode=pl.Buffered(1))
    return pl.pallas_call(
        lambda *refs: row_grad_kernel(len(rows), *refs),
        grid=(width // step,),
        in_specs=[pl.BlockSpec((eight, half, step), lambda i: (0, 0, i))] * len(rows)
        + [held] * len(groups),
        out_specs=pl.BlockSpec((2, step, units // 2), lambda i: (0, i, 0)),
        out_shape=out((2, width, units // 2), F32),
        cost_estimate=pl.CostEstimate(
            flops=2 * len(rows) * count * width * units,
            bytes_accessed=2 * len(rows) * count * (width + units) + 4 * width * units,
            transcendentals=0,
        ),
        name="row_grads",
    )(*rows, *[g for _, g in groups])


def down_grad_kernel(count, at_ref, *refs):
    scaled_refs, cot_refs, out_ref = refs[:count], refs[count:-1], refs[-1]
    _, unit_part, step = out_ref.shape
    total = jnp.zeros((2 * unit_part, step), F32)
    for n, scaled_ref in enumerate(scaled_refs):
        for side in range(2):
            cot = cot_refs[2 * n + side][...].reshape(-1, step)
            total = total + t_dot(scaled_ref[side].reshape(-1, 2 * unit_part), cot)
    for e in range(2):
        out_ref[e] = total[e * unit_part : (e + 1) * unit_part]


def down_grad_call(at, scaled, cot):
    step = 256
    shards, _, _, two, half, columns = cot.shape
    _, eight, _, units = scaled[0].shape
    width = (columns // step) * step
    count = len(scaled)

    def tile(n, side):
        return pl.BlockSpec(
            (shards, 1, 1, two, half, step),
            lambda i, at: (0, at[1 + n], lax.rem(at[0] + side, 2), 0, 0, i),
        )

    return pl.pallas_call(
        lambda *refs: down_grad_kernel(count, *refs),
        grid_spec=pltpu.PrefetchScalarGridSpec(
            num_scalar_prefetch=1,
            grid=(width // step,),
            in_specs=[
                pl.BlockSpec(
                    s.shape, lambda i, _: (0, 0, 0, 0), pipeline_mode=pl.Buffered(1)
                )
                for s in scaled
            ]
            + [tile(n, side) for n in range(count) for side in range(2)],
            out_specs=pl.BlockSpec((2, units // 2, step), lambda i, _: (0, 0, i)),
        ),
        out_shape=out((2, units // 2, width), F32),
        cost_estimate=pl.CostEstimate(
            flops=4 * count * eight * half * width * units,
            bytes_accessed=4 * count * eight * half * (width + units) + 4 * width * units,
            transcendentals=0,
        ),
        name="down_grads",
    )(at, *scaled, *([cot] * (2 * count)))


def add_up(parts):
    total = parts[0]
    for part in parts[1:]:
        total = total + part
    return total


def turn_kernel(
    experts_all,
    ring_ref,
    a0,
    a1,
    a2,
    b0,
    b1,
    b2,
    residual_ref,
    cot_ref,
    mixed_ref,
    router_ref,
    router_rows_ref,
    gain_ref,
    grad_ref,
    grad_b_ref,
    gain_grad_ref,
    router_grad_ref,
):
    width = residual_ref.shape[2]
    half = residual_ref.shape[1]
    lane = lax.broadcasted_iota(jnp.int32, (half, LANES), 1)
    gain_grad, router_grad = None, None
    for n, refs in enumerate(((a0, a1, a2), (b0, b1, b2))):
        back = ring_ref[n].astype(F32) + total_of([r[...] for r in refs])
        mixed = mixed_ref[n]
        powers = jnp.where(lane < experts_all, jnp.exp(dot(mixed, router_ref[...])), 0.0)
        probs = powers / jnp.sum(powers, axis=-1, keepdims=True)
        prob_grad = back[:, width:]
        logit_grad = (
            probs * (prob_grad - jnp.sum(probs * prob_grad, axis=-1, keepdims=True))
        ).astype(BF16)
        mixed_grad = back[:, :width] + dot(logit_grad, router_rows_ref[...])
        residual = residual_ref[n]
        norm_grad, gain_now = norm_back(mixed_grad, residual, rms_scale(residual), gain_ref[...])
        total = cot_ref[n] + norm_grad
        grad_ref[n] = total
        grad_b_ref[n] = total.astype(BF16)
        router_now = t_dot(logit_grad, mixed)
        gain_grad = gain_now if gain_grad is None else gain_grad + gain_now
        router_grad = router_now if router_grad is None else router_grad + router_now
    gain_grad_ref[...] = jnp.broadcast_to(gain_grad, gain_grad_ref.shape)
    router_grad_ref[...] = router_grad[: router_grad_ref.shape[0]]


def output_grad_kernel(core_ref, g0, g1, g2, g3, attended_ref, own_ref, other_ref):
    blocks, half, step = own_ref.shape
    own_cols = pl.ds(pl.multiple_of(core_ref[0] * half, half), half)
    other_cols = pl.ds(pl.multiple_of((1 - core_ref[0]) * half, half), half)
    for c in range(blocks):
        cols = slice(c * step, (c + 1) * step)
        grads = jnp.concatenate(
            [g[:, :, cols].reshape(LANES, step) for g in (g0, g1, g2, g3)], axis=0
        )
        own_ref[c] = t_dot(attended_ref[:, own_cols], grads)
        other_ref[c] = t_dot(attended_ref[:, other_cols], grads).astype(BF16)


def attend_back_kernel(
    g0,
    g1,
    g2,
    g3,
    w_ref,
    attended_ref,
    q_ref,
    k_ref,
    v_ref,
    lse_ref,
    scales_ref,
    bias_ref,
    cos_ref,
    sin_ref,
    gain_q_ref,
    gain_k_ref,
    proj_ref,
    query_ref,
    key_ref,
    value_ref,
    stats_ref,
    gains_ref,
    grad_ref,
):
    part, width = w_ref.shape
    rows = proj_ref.shape[0]
    grad_ref[...] = jnp.concatenate(
        [g[...].reshape(LANES, width) for g in (g0, g1, g2, g3)], axis=0
    )
    q_scale, k_scale = scales_ref[:, 0:1], scales_ref[:, 1:2]
    cosine, sine_part = cos_ref[...], sin_ref[...]
    q_inner = jnp.zeros((rows, 1), F32)
    k_inner = jnp.zeros((rows, 1), F32)
    for h in range(part // HEAD_DIM):
        cols = slice(h * HEAD_DIM, (h + 1) * HEAD_DIM)
        k_cols = slice(part + h * HEAD_DIM, part + (h + 1) * HEAD_DIM)
        attended_grad = dot_t(grad_ref[...], w_ref[cols, :]).astype(BF16)
        query, key, value = q_ref[:, cols], k_ref[:, cols], v_ref[:, cols]
        probs = jnp.exp(
            dot_t(query, key) * SCORE_SCALE + bias_ref[...] - lse_ref[:, h : h + 1]
        )
        delta = jnp.sum(
            attended_grad.astype(F32) * attended_ref[:, cols].astype(F32), axis=-1, keepdims=True
        )
        score_grad = (probs * (dot_t(attended_grad, value) - delta)).astype(BF16)
        value_ref[:, cols] = t_dot(probs.astype(BF16), attended_grad).astype(BF16)
        query_grad = dot(score_grad, key) * SCORE_SCALE
        key_grad = t_dot(score_grad, query) * SCORE_SCALE
        query_pre = query_grad * cosine + pltpu.roll(query_grad * sine_part, HEAD_DIM // 2, 1)
        key_pre = key_grad * cosine + pltpu.roll(key_grad * sine_part, HEAD_DIM // 2, 1)
        q_proj, k_proj = proj_ref[:, cols], proj_ref[:, k_cols]
        gains_ref[0:1, cols] = jnp.sum(query_pre * q_proj * q_scale, axis=0, keepdims=True)
        gains_ref[1:2, cols] = jnp.sum(key_pre * k_proj * k_scale, axis=0, keepdims=True)
        query_pre = query_pre * gain_q_ref[:, cols]
        key_pre = key_pre * gain_k_ref[:, cols]
        query_ref[:, cols] = query_pre
        key_ref[:, cols] = key_pre
        q_inner = q_inner + jnp.sum(query_pre * q_proj, axis=-1, keepdims=True)
        k_inner = k_inner + jnp.sum(key_pre * k_proj, axis=-1, keepdims=True)
    for n, stats in enumerate(pack_stats(q_inner, k_inner)):
        stats_ref[n] = stats


def project_back_kernel(
    at_ref, s0, s1, s2, s3, query_ref, key_ref, value_ref, proj_ref, scales_ref, normed_ref, *refs
):
    weight_refs = refs[:8]
    part_refs, pair_ref, all_ref = refs[8:12], refs[12], refs[13]
    width = normed_ref.shape[1]
    part = query_ref.shape[1]
    inner = sum_stats(s0, s1, s2, s3) / width
    for n, (grad_ref, low) in enumerate(((query_ref, 0), (key_ref, part))):
        scale = scales_ref[:, n : n + 1]
        factor = scale * scale * inner[:, n : n + 1]
        all_ref[:, low : low + part] = (
            scale * (grad_ref[...] - proj_ref[:, low : low + part] * factor)
        ).astype(BF16)
    all_ref[:, 2 * part :] = value_ref[...]
    depth = weight_refs[0].shape[0]
    for n, ref in enumerate(weight_refs):
        at = pl.ds(pl.multiple_of(at_ref[n] * depth, depth), depth)
        got = dot_t(all_ref[...], ref[...]).astype(BF16)
        for k, part_ref in enumerate(part_refs):
            part_ref[:, :, at] = got[k * LANES : (k + 1) * LANES].reshape(2, LANES // 2, depth)
    members, parts, rows, _ = pair_ref.shape
    for p in range(parts):
        for third in range(2):
            cols = slice(third * part, (third + 1) * part)
            got = t_dot(normed_ref[:, p * part : (p + 1) * part], all_ref[:, cols]).astype(BF16)
            for e in range(members):
                pair_ref[e, p, :, cols] = got[e * rows : (e + 1) * rows]


def value_back_kernel(core_ref, value_ref, normed_ref, own_ref, other_ref):
    parts, depth, _ = own_ref.shape
    for p in range(parts):
        for ref, side in ((own_ref, core_ref[0]), (other_ref, 1 - core_ref[0])):
            at = pl.ds(pl.multiple_of((2 * p + side) * depth, depth), depth)
            ref[p] = t_dot(normed_ref[:, at], value_ref[...]).astype(ref.dtype)


def finish_kernel(a0, a1, a2, b0, b1, b2, x_ref, grad_ref, gain_ref, out_ref, gain_grad_ref):
    gain_grad = None
    for n, refs in enumerate(((a0, a1, a2), (b0, b1, b2))):
        source = x_ref[n].astype(F32)
        normed_grad = total_of([r[...] for r in refs])
        norm_grad, gain_now = norm_back(normed_grad, source, rms_scale(source), gain_ref[...])
        out_ref[n] = grad_ref[n] + norm_grad
        gain_grad = gain_now if gain_grad is None else gain_grad + gain_now
    gain_grad_ref[...] = jnp.broadcast_to(gain_grad, gain_grad_ref.shape)


def cut_kernel(at_ref, *refs):
    sources, (own_ref, spare_ref, x_ref, y_ref) = refs[:15], refs[15:]
    depth, part = sources[0].shape
    rows = depth // 2
    for w in range(3):
        cols = slice(w * part, (w + 1) * part)
        own_ref[:, cols] = sources[w][...]
        x_ref[:depth, cols] = sources[3 + w][...]
        y_ref[:depth, cols] = sources[6 + w][...]
        x_ref[depth:, cols] = sources[9 + w][:rows, :]
        y_ref[depth:, cols] = sources[9 + w][rows:, :]
        spare_ref[:, cols] = sources[12 + w][...]


def cut_call(at, w_query, w_key, w_value):
    rows, width = w_query.shape
    part = width // 4
    depth = rows // 2

    def block(member, core):
        return pl.BlockSpec((depth, part), lambda i, at: (at[core], at[member]))

    full, more = (depth, 3 * part), (3 * depth // 2, 3 * part)
    fulls = [full, full, more, more]
    return pl.pallas_call(
        cut_kernel,
        grid_spec=pltpu.PrefetchScalarGridSpec(
            num_scalar_prefetch=1,
            grid=(1,),
            in_specs=[block(d, 4) for d in range(4) for _ in range(3)]
            + [block(0, 5) for _ in range(3)],
            out_specs=[whole(s) for s in fulls],
        ),
        out_shape=[out(s, BF16) for s in fulls],
        name="cut",
    )(at, *([w_query, w_key, w_value] * 5))


def on_device(
    block_input,
    segment_ids,
    expert_routes,
    attn_gain,
    w_query,
    w_key,
    w_value,
    query_gain,
    key_gain,
    w_output,
    moe_gain,
    w_router,
    w_gate,
    w_up,
    w_down,
    out_cotangent,
):
    expert_count = lax.axis_size("expert")
    shard_count = lax.axis_size("shard")
    chips = expert_count // 2
    me = lax.axis_index("shard")
    place = lax.axis_index("expert")
    core = lax.rem(place, 2)
    chip = place // 2
    tok_count = block_input.shape[1]
    half = tok_count // 2
    group_count = segment_ids.shape[1]
    width = block_input.shape[2]
    part = width // shard_count
    local_experts = w_gate.shape[0]
    experts_all = local_experts * expert_count
    unit_part = w_gate.shape[2]
    units = local_experts * unit_part
    core_at = jnp.reshape(core, (1,))

    own_input = block_input.reshape(2, half, width)
    group_input = [b.reshape(2, half, width) for b in spread_xy(own_input[:1], own_input[1:])]

    small = jnp.concatenate([attn_gain[None], moe_gain[None], w_router.T], axis=0)
    small = jnp.pad(small, ((0, (-small.shape[0]) % 32), (0, 0)))
    small_all = jnp.zeros((small.shape[0], width), BF16)
    small_parts = gather_parts(small)
    for d, got in enumerate(small_parts):
        small_all = lax.dynamic_update_slice_in_dim(small_all, got, (me ^ d) * part, 1)
    gain_one = small_all[0:1].astype(F32)
    gain_two = small_all[1:2].astype(F32)
    router = small_all[2 : 2 + experts_all]
    router = jnp.pad(router, ((0, LANES - experts_all), (0, 0)))
    router_t = router.T

    depth = part // 2
    at = jnp.stack([me, me ^ 1, me ^ 2, me ^ 3, core, 1 - core])
    cuts = cut_call(at, w_query, w_key, w_value)
    gate_up_t, down_t = flip_call(w_gate, w_up, w_down)
    direct = exchange_blocks(
        *after(cuts[2:], group_input[0], group_input[2], small_parts), group_input, gate_up_t
    )
    passed = [swap_core(block) for block in direct]
    weight_blocks = list(cuts[:2]) + direct + passed
    weight_at = jnp.stack(
        [2 * me + core, 2 * me + 1 - core]
        + [2 * (me ^ d) + core for d in (1, 2, 3)]
        + [2 * (me ^ d) + 1 - core for d in (1, 2, 3)]
    )

    routes = expert_routes[0]
    routed = jnp.sum(
        (routes[:, :, None] == jnp.arange(experts_all)[None, None, :]).astype(F32), axis=1
    )
    cotangent = out_cotangent[0]
    cot_block = (
        jnp.concatenate(
            [cotangent, routed, jnp.zeros((tok_count, LANES - experts_all), F32)], axis=1
        )
        .astype(BF16)
    )
    cot = lax.all_gather(cot_block, ("shard", "expert"), axis=0, tiled=True)

    down_w = w_down.reshape(units, width)

    starts = [(me ^ d) * tok_count + side * half for pair in ORDER for side, d in pair]
    position = jnp.concatenate([p + jnp.arange(half) for p in starts])
    seg_all = segment_ids[0]
    seg_here = jnp.concatenate([lax.dynamic_slice_in_dim(seg_all, p, half) for p in starts])
    allowed = (seg_here[:, None] == seg_here[None, :]) & (position[None, :] <= position[:, None])
    bias = jnp.where(allowed, 0.0, -1e30).astype(F32)
    half_dim = HEAD_DIM // 2
    inverse = 10000.0 ** (-(jnp.arange(half_dim).astype(F32) * 2.0) / HEAD_DIM)
    angles = position.astype(F32)[:, None] * inverse[None, :]
    cosine = jnp.concatenate([jnp.cos(angles), jnp.cos(angles)], axis=-1)
    sine_part = jnp.concatenate([-jnp.sin(angles), jnp.sin(angles)], axis=-1)
    gain_query = query_gain.astype(F32)[None]
    gain_key = key_gain.astype(F32)[None]
    normed, proj, squares, scale_one = call(
        project_kernel,
        "project",
        [weight_at] + group_input + [gain_one] + weight_blocks,
        [
            out((group_count, width), BF16),
            out((group_count, 3 * part), F32),
            out((4, 8, LANES), F32),
            out((group_count, LANES), F32),
        ],
        2 * group_count * width * 3 * part,
        smem=(0,),
    )
    quad = out((2, half, width), BF16)
    square_parts = out((group_count, part), BF16)
    heads = call(
        lambda *refs: attend_kernel(width, *refs),
        "attend",
        [proj] + gather_parts(squares) + [gain_query, gain_key, cosine, sine_part, bias, w_output],
        [square_parts] * 3
        + [out((group_count, LANES), F32)] * 2
        + [square_parts]
        + [quad] * 4,
        4 * group_count * group_count * part + 2 * group_count * part * width,
    )
    q_heads, k_heads, v_heads, log_total, scales, attended = heads[:6]
    terms_a, terms_b = reduce_xy([b.reshape(2, 1, half, width) for b in heads[6:]])
    residual, mixed_in = call(
        settle_kernel,
        "settle",
        [own_input]
        + [t.reshape(half, width) for t in terms_a + terms_b]
        + [gain_two],
        [out((2, half, width), F32), out((2, half, width), BF16)],
        tok_count * width,
    )

    pieces = [mixed_in, ring_up(mixed_in)]
    cot = after(cot, mixed_in).reshape(shard_count, chips, 2, 2, half, width + LANES)
    lead = lead_call(cot, down_t)
    pieces[1] = after(pieces[1], lead)
    while len(pieces) < chips:
        pieces.append(ring_up(pieces[-1]))
    chip_at = [lax.rem(chip + chips - j, chips) for j in range(chips)]
    lows, low = [0, 1], 2
    while low < chips:
        lows.append(low)
        low *= 2
    lows.append(chips)
    all_rows, firsts = [], []
    for low, high in zip(lows[:-1], lows[1:]):
        sides = [jnp.stack([p[s] for p in pieces[low:high]]) for s in range(2)]
        pair_a = jnp.stack([sides[0], swap_x(sides[0])])
        pair_b = jnp.stack([sides[1], swap_y(sides[1])])
        firsts.append((pair_a, pair_b))
        if low > 1:
            pair_a, pair_b = after((pair_a, pair_b), all_rows[1][0])
        parts = [pair_a, swap_y(pair_a), pair_b, swap_x(pair_b)]
        for j in range(high - low):
            own = join_call(parts, j)
            all_rows.append((own, swap_core(own)))
    groups, totals_all = [], []
    for j in range(chips):
        at = jnp.stack([place, me, chip_at[j], core])
        at = after(at, totals_all[j - 2] if j > 1 else firsts[:3])
        got = expert_call(
            at, all_rows[j], cot, lead, w_gate, w_up, gate_up_t, router_t, experts_all
        )
        groups.append((all_rows[j], got[5], got[6], got[7]))
        if 0 < j < chips - 1:
            passed_back = swap_core(after(got[4], all_rows[j + 1][1]))
        else:
            passed_back = swap_core(got[4])
        totals_all.append(
            [
                (a.astype(F32) + passed_back[n].astype(F32)).astype(BF16)
                for n, a in enumerate(got[:4])
            ]
        )
    back_terms = [None] * chips

    def back_piece(j):
        return jnp.stack([total_of(terms) for terms in back_terms[j]])

    back_pieces, arrived = [], []
    for j in list(range(1, chips)) + [0]:
        totals = totals_all[j]
        if j == 0:
            totals = after(totals, totals_all[-1], arrived[0])
        back_terms[j] = [
            [t[0] for t in terms]
            for terms in reduce_xy(
                after(totals, [r[0] for r in all_rows]),
                totals_all[-1] if j != 1 else (),
                back_pieces[-1:],
                arrived[-1:],
            )
        ]
        if j:
            back_pieces.append(back_piece(j))
        if j == 1:
            ring_total = back_pieces[0].astype(BF16)
        elif j:
            arrived.append(ring_up(ring_total))
            ring_total = (arrived[-1].astype(F32) + back_pieces[-1]).astype(BF16)
    scaled_sides = [
        jnp.concatenate([g[3][side : side + 1] for g in groups]) for side in range(2)
    ]
    mix_passed = swap_core(mix_call(after(scaled_sides[1], arrived[0], back_pieces[1]), down_w))

    ring_total = ring_up(ring_total)
    grad_res, grad_res_b, grad_gain_two, grad_router = call(
        lambda *refs: turn_kernel(experts_all, *refs),
        "turn",
        [ring_total]
        + back_terms[0][0]
        + back_terms[0][1]
        + [residual, cotangent.reshape(2, half, width), mixed_in, router_t, router]
        + [gain_two],
        [
            out((2, half, width), F32),
            out((2, half, width), BF16),
            out((8, width), F32),
            out((experts_all, width), F32),
        ],
        8 * tok_count * width * LANES,
    )

    group_grad = [b.reshape(2, half, width) for b in spread_xy(grad_res_b[:1], grad_res_b[1:])]
    out_totals = mix_call(
        after(scaled_sides[0], group_grad[0], group_grad[2]), down_w, mix_passed
    )
    output_own, output_other = call(
        output_grad_kernel,
        "output_grad",
        [core_at] + after(group_grad, out_totals) + [attended],
        [out((4, part // 2, width // 4), F32), out((4, part // 2, width // 4), BF16)],
        2 * group_count * part * width,
        smem=(0,),
    )
    query_pre, key_pre, value_grad, inner, gain_grads, _ = call(
        attend_back_kernel,
        "attend_back",
        after(group_grad, output_other)
        + [w_output, attended, q_heads, k_heads, v_heads, log_total, scales, bias]
        + [cosine, sine_part, gain_query, gain_key, proj],
        [
            out((group_count, part), F32),
            out((group_count, part), F32),
            square_parts,
            out((4, 8, LANES), F32),
            out((8, part), F32),
            out((group_count, width), BF16),
        ],
        10 * group_count * group_count * part + 2 * group_count * part * width,
    )
    def split_rows(own):
        parts, rows, columns = own.shape
        split = own.reshape(parts, chips, rows // chips, columns)
        return [lax.dynamic_index_in_dim(split, at, 1, keepdims=False) for at in chip_at]

    inner_parts = gather_parts(inner)
    keep_a, send_a, keep_b, send_b = after(out_totals, inner_parts)
    got_a, got_b = swap_y(send_a), swap_x(send_b)
    out_far = (
        (keep_a[1].astype(F32) + got_a[1].astype(F32)).astype(BF16),
        (keep_b[1].astype(F32) + got_b[1].astype(F32)).astype(BF16),
    )
    out_terms = (
        (keep_a[0], got_a[0], swap_x(out_far[0])),
        (keep_b[0], got_b[0], swap_y(out_far[1])),
    )

    def out_piece(j):
        return jnp.stack([total_of([t[j] for t in side]) for side in out_terms])

    def ring_add(total, pieces, *others):
        moved = after(ring_up(total), *others)
        return (moved.astype(F32) + pieces.pop(0)).astype(BF16)

    output_passed = after(swap_core(output_other), query_pre)
    output_pieces = split_rows(output_own + output_passed.astype(F32))
    output_pieces = output_pieces[1:] + output_pieces[:1]
    output_total = output_pieces.pop(0).astype(BF16)
    value_own, value_other = call(
        value_back_kernel,
        "value_back",
        [core_at] + after([value_grad], inner, output_total) + [normed],
        [out((4, depth, part), F32), out((4, depth, part), BF16)],
        2 * group_count * width * part,
        smem=(0,),
    )
    value_passed = swap_core(value_other)
    output_total = ring_add(output_total, output_pieces, value_other)
    got = call(
        project_back_kernel,
        "project_back",
        [weight_at]
        + inner_parts
        + after([query_pre, key_pre, value_grad, proj, scales, normed], output_total)
        + weight_blocks,
        [quad] * 4
        + [
            out((expert_count, 4, part // expert_count, 2 * part), BF16),
            out((group_count, 3 * part), BF16),
        ],
        4 * group_count * width * 3 * part,
        smem=(0,),
    )
    def exchange_grads(piece):
        sent = [lax.dynamic_index_in_dim(piece, me ^ d, 0, keepdims=False) for d in range(4)]
        low = sent[3].shape[0] // 2
        arrived = exchange_blocks(
            jnp.concatenate([sent[1], sent[3][:low]], axis=0),
            jnp.concatenate([sent[2], sent[3][low:]], axis=0),
        )
        return jnp.stack([sent[0]] + arrived)

    def whole_grads(rows):
        shares = [lax.dynamic_index_in_dim(rows, me ^ p, 0, keepdims=False) for p in range(4)]
        return [
            jnp.concatenate(
                [share[:, n * part : (n + 1) * part] for share in shares], axis=1
            ).astype(F32)
            for n in range(rows.shape[2] // part)
        ]

    pair_sums = lax.psum_scatter(got[4], "expert", scatter_dimension=0, tiled=True)[0]

    span = min(chips, 4)
    starts = range(0, chips, span)

    def row_grads(which, *others):
        late = after([g[1] for g in groups], *others)
        return add_up(
            [
                row_grad_call([(g[0], v) for g, v in zip(groups, late)][low : low + span], which)
                for low in starts
            ]
        )

    def down_grads(*others):
        late = after([g[2] for g in groups], *others)
        return add_up(
            [
                down_grad_call(
                    jnp.stack([core] + chip_at[low : low + span]), late[low : low + span], cot
                )
                for low in starts
            ]
        )

    expert_grads = [down_grads(got[0])]
    output_total = ring_add(output_total, output_pieces, expert_grads[0])
    value_pieces = split_rows(
        value_own + after(value_passed, expert_grads[0]).astype(F32)
    )
    value_pieces = value_pieces[1:] + value_pieces[:1]
    total = value_pieces.pop(0).astype(BF16)
    expert_grads.append(row_grads(0, total, output_total))
    total = ring_add(total, value_pieces, expert_grads[1])
    output_total = ring_add(output_total, output_pieces, expert_grads[1])
    first_kept, first_on = reduce_first(
        [b.reshape(2, 1, half, width) for b in got[:4]], total, output_total
    )
    expert_grads.append(row_grads(1, total, output_total, first_on, out_far))
    while output_pieces:
        output_total = ring_add(output_total, output_pieces, expert_grads[2])
    out_spread = [output_total]
    while len(value_pieces) > 1:
        total = ring_add(total, value_pieces, expert_grads[2])
    terms_a, terms_b = reduce_last(first_kept, first_on)
    grad_input, grad_gain_one = call(
        finish_kernel,
        "finish",
        [t.reshape(half, width) for t in terms_a + terms_b]
        + [own_input, grad_res, after(gain_one, total)],
        [out((2, half, width), F32), out((8, width), F32)],
        tok_count * width,
    )
    out_now = after(out_piece(1), total).astype(BF16)
    pair_mine = exchange_grads(after(pair_sums, grad_gain_one, out_now))
    pair_rows = lax.all_gather(pair_mine, "expert", axis=0)
    total = ring_add(total, value_pieces, pair_mine)
    spread = [exchange_grads(total)]
    grad_w_down, grad_w_gate, grad_w_up = expert_grads
    for j in range(1, chips):
        moved = after(ring_up(out_now), spread[0])
        if j + 1 < chips:
            out_now = (moved.astype(F32) + out_piece(j + 1)).astype(BF16)
        spread.append(after(ring_up(spread[-1]), out_now if j + 1 < chips else moved))
        if len(out_spread) < chips:
            out_spread.append(after(ring_up(out_spread[-1]), spread[-1]))
    while len(out_spread) < chips:
        out_spread.append(ring_up(out_spread[-1]))
    block_output = residual + (moved.astype(F32) + out_piece(0))
    early_rows = expert_spread(out_spread, core, chip)
    grad_w_output = jnp.concatenate([early_rows[c] for c in range(4)], axis=1).astype(F32)
    (grad_w_value,) = whole_grads(expert_spread(spread, core, chip))
    pair_rows = jnp.transpose(pair_rows, (1, 0, 2, 3)).reshape(4, part, 2 * part)
    grad_w_query, grad_w_key = whole_grads(pair_rows)

    grad_gain_one = after(grad_gain_one, spread[0])
    packed = jnp.concatenate([grad_gain_one[:1], grad_gain_two[:1], grad_router], axis=0)
    rows_used = packed.shape[0]
    packed = jnp.pad(packed, ((0, (-rows_used) % 16), (0, 0)))
    quarters = jnp.stack(
        [lax.dynamic_slice_in_dim(packed, (me ^ d) * part, part, 1) for d in range(4)]
    )
    quarters = quarters[:2] + swap_y(quarters[2:])
    packed = (quarters[0] + swap_x(quarters[1]))[:rows_used]
    packed = after(jnp.concatenate([packed, gain_grads[:2]], axis=0), spread[-1])
    bit = 1
    while bit < expert_count:
        packed = packed + flip_expert(packed, bit)
        bit *= 2
    return (
        block_output.reshape(1, tok_count, width),
        grad_input.reshape(1, tok_count, width),
        packed[0],
        grad_w_query,
        grad_w_key,
        grad_w_value,
        packed[rows_used],
        packed[rows_used + 1],
        grad_w_output,
        packed[1],
        packed[2 : 2 + experts_all].T,
        grad_w_gate,
        grad_w_up,
        grad_w_down,
    )


def solution(mesh):
    placed = (
        P("expert", "shard", None),
        P("expert", None),
        P("expert", "shard", None),
        P("shard"),
        P("shard", None),
        P("shard", None),
        P("shard", None),
        P("shard"),
        P("shard"),
        P("shard", None),
        P("shard"),
        P("shard", None),
        P("expert", None, "shard"),
        P("expert", None, "shard"),
        P("expert", "shard", None),
        P("expert", "shard", None),
    )
    return jax.shard_map(
        on_device,
        mesh=mesh,
        in_specs=placed,
        out_specs=(
            P("expert", "shard", None),
            P("expert", "shard", None),
            P("shard"),
            P("shard", None),
            P("shard", None),
            P("shard", None),
            P("shard"),
            P("shard"),
            P("shard", None),
            P("shard"),
            P("shard", None),
            P("expert", None, "shard"),
            P("expert", None, "shard"),
            P("expert", "shard", None),
        ),
        check_vma=False,
    )
```

```python
import jax
import jax.numpy as jnp
from jax import lax
from jax.experimental import pallas as pl
from jax.experimental.pallas import tpu as pltpu
from jax.sharding import PartitionSpec as P

HEAD_DIM = 128
LANES = 128
EPSILON = 1e-05
SCORE_SCALE = HEAD_DIM ** (-0.5)
F32 = jnp.float32
BF16 = jnp.bfloat16
ORDER = (((0, 0), (0, 1)), ((0, 2), (0, 3)), ((1, 0), (1, 2)), ((1, 1), (1, 3)))


def dot(a, b):
    return jnp.dot(a, b, preferred_element_type=F32)


def dot_t(a, b):
    return lax.dot_general(a, b, (((1,), (1,)), ((), ())), preferred_element_type=F32)


def t_dot(a, b):
    return lax.dot_general(a, b, (((0,), (0,)), ((), ())), preferred_element_type=F32)


def flip_shard(values, bit):
    count = lax.axis_size("shard")
    return lax.ppermute(values, "shard", [(i, i ^ bit) for i in range(count)])


def swap_x(values):
    return flip_shard(values, 1)


def swap_y(values):
    return flip_shard(values, 2)


def swap_far(values):
    return flip_shard(values, 3)


def flip_expert(values, bit):
    count = lax.axis_size("expert")
    return lax.ppermute(values, "expert", [(i, i ^ bit) for i in range(count)])


def swap_core(values):
    return flip_expert(values, 1)


def ring_up(values):
    count = lax.axis_size("expert")
    return lax.ppermute(values, "expert", [(i, (i + 2) % count) for i in range(count)])


def after(values, *others):
    return lax.optimization_barrier((values, others))[0]


def spread_xy(first, second):
    pair_a = jnp.stack([first, swap_x(first)])
    pair_b = jnp.stack([second, swap_y(second)])
    return [pair_a, swap_y(pair_a), pair_b, swap_x(pair_b)]


def reduce_first(blocks, *others):
    keep_a, send_a, keep_b, send_b = blocks
    got_a, got_b = after((swap_y(send_a), swap_x(send_b)), *others)
    on_a = (keep_a[1].astype(F32) + got_a[1].astype(F32)).astype(BF16)
    on_b = (keep_b[1].astype(F32) + got_b[1].astype(F32)).astype(BF16)
    return ((keep_a[0], got_a[0]), (keep_b[0], got_b[0])), (on_a, on_b)


def reduce_last(kept, on):
    return kept[0] + (swap_x(on[0]),), kept[1] + (swap_y(on[1]),)


def reduce_xy(blocks, *others):
    return reduce_last(*reduce_first(blocks, *others))


def total_of(terms):
    total = terms[0].astype(F32)
    for term in terms[1:]:
        total = total + term.astype(F32)
    return total


def exchange_blocks(for_x, for_y, *others):
    got_x, got_y = after((swap_x(for_x), swap_y(for_y)), *others)
    depth = 2 * for_x.shape[0] // 3
    far = jnp.concatenate([swap_y(got_x[depth:]), swap_x(got_y[depth:])], axis=0)
    return [got_x[:depth], got_y[:depth], far]


def gather_parts(part):
    return [part, swap_x(part), swap_y(part), swap_far(part)]


def ring_gather(piece):
    pieces = [piece]
    for _ in range(lax.axis_size("expert") // 2 - 1):
        pieces.append(ring_up(pieces[-1]))
    return pieces


def ring_sum(total, pieces):
    for piece in pieces:
        total = (ring_up(total).astype(F32) + piece).astype(BF16)
    return total


def expert_spread(pieces, core, chip):
    chips = lax.axis_size("expert") // 2
    parts, rows, columns = pieces[0].shape
    spread = jnp.zeros((parts, chips, rows, columns), pieces[0].dtype)
    for j, got in enumerate(pieces):
        spread = lax.dynamic_update_slice_in_dim(
            spread, got[:, None], lax.rem(chip + chips - j, chips), 1
        )
    half = spread.reshape(parts, 1, chips * rows, columns)
    other = swap_core(half)
    first = jnp.where(core == 0, half, other)
    second = jnp.where(core == 0, other, half)
    return jnp.concatenate([first, second], axis=1).reshape(parts, 2 * chips * rows, columns)


def rms_scale(values):
    return lax.rsqrt(jnp.mean(values * values, axis=-1, keepdims=True) + EPSILON)


def norm_back(grad_out, source, scale_now, gain_now):
    weighted = grad_out * gain_now
    inner_mean = jnp.mean(weighted * source, axis=-1, keepdims=True)
    grad_source = scale_now * (weighted - source * scale_now * scale_now * inner_mean)
    grad_gain = jnp.sum(grad_out * source * scale_now, axis=0, keepdims=True)
    return (grad_source, grad_gain)


def whole(shape):
    return pl.BlockSpec(shape, lambda *_: (0,) * len(shape))


def scalars():
    return pl.BlockSpec(memory_space=pltpu.SMEM)


def call(kernel, name, args, outs, flops, smem=(), transcendentals=0):
    moved = sum(a.size * a.dtype.itemsize for a in args) + sum(
        o.size * o.dtype.itemsize for o in outs
    )
    return pl.pallas_call(
        kernel,
        in_specs=[scalars() if n in smem else whole(a.shape) for n, a in enumerate(args)],
        out_specs=[whole(o.shape) for o in outs],
        out_shape=outs,
        cost_estimate=pl.CostEstimate(
            flops=flops, bytes_accessed=moved, transcendentals=transcendentals
        ),
        name=name,
    )(*args)


def out(shape, dtype):
    return jax.ShapeDtypeStruct(shape, dtype)


def pack_stats(first, second):
    rows = first.shape[0]
    lane = lax.broadcasted_iota(jnp.int32, (rows, LANES), 1)
    spread = jnp.where(lane == 0, first, jnp.where(lane == 1, second, 0.0))
    return [spread[n : n + LANES].T[:8] for n in range(0, rows, LANES)]


def sum_stats(mine, from_x, from_y, far):
    def turn(values):
        return pltpu.roll(values, LANES // 2, 1)

    totals = [
        mine[0] + turn(from_x[0]) + from_y[1] + turn(far[1]),
        mine[1] + turn(from_x[1]) + from_y[0] + turn(far[0]),
        mine[2] + from_x[3] + turn(from_y[2]) + turn(far[3]),
        mine[3] + from_x[2] + turn(from_y[3]) + turn(far[2]),
    ]
    pad = jnp.zeros((LANES - 8, LANES), F32)
    return jnp.concatenate([jnp.concatenate([t, pad], axis=0).T for t in totals], axis=0)


def project_kernel(
    at_ref, r0, r1, r2, r3, gain_ref, *refs
):
    weight_refs, (normed_ref, proj_ref, stats_ref, scale_ref) = refs[:8], refs[8:]
    part = proj_ref.shape[1] // 3
    for n, ref in enumerate((r0, r1, r2, r3)):
        source = ref[...].reshape(LANES, ref.shape[2]).astype(F32)
        scale = rms_scale(source)
        rows = slice(n * LANES, (n + 1) * LANES)
        normed_ref[rows, :] = (source * scale * gain_ref[...]).astype(BF16)
        scale_ref[rows, :] = jnp.broadcast_to(scale, (LANES, LANES))
    depth = weight_refs[0].shape[0]
    for third in range(3):
        cols = slice(third * part, (third + 1) * part)
        total = None
        for n, ref in enumerate(weight_refs):
            rows = pl.ds(pl.multiple_of(at_ref[n] * depth, depth), depth)
            more = dot(normed_ref[:, rows], ref[:, cols])
            total = more if total is None else total + more
        proj_ref[:, cols] = total
    q_proj, k_proj = proj_ref[:, :part], proj_ref[:, part : 2 * part]
    packed = pack_stats(
        jnp.sum(q_proj * q_proj, axis=-1, keepdims=True),
        jnp.sum(k_proj * k_proj, axis=-1, keepdims=True),
    )
    for n, stats in enumerate(packed):
        stats_ref[n] = stats


def attend_kernel(
    width, proj_ref, s0, s1, s2, s3, gain_q_ref, gain_k_ref, cos_ref, sin_ref, bias_ref, w_ref, *refs
):
    q_ref, k_ref, v_ref, lse_ref, scales_ref, attended_ref = refs[:6]
    part_refs = refs[6:]
    part = w_ref.shape[0]
    rows = proj_ref.shape[0]
    sums = sum_stats(s0, s1, s2, s3)
    scales = lax.rsqrt(sums / width + EPSILON)
    scales_ref[...] = scales
    lane = lax.broadcasted_iota(jnp.int32, (rows, LANES), 1)
    q_scale, k_scale = scales[:, 0:1], scales[:, 1:2]
    cosine, sine_part = cos_ref[...], sin_ref[...]
    lse_all = jnp.zeros((rows, LANES), F32)
    for h in range(part // HEAD_DIM):
        cols = slice(h * HEAD_DIM, (h + 1) * HEAD_DIM)
        k_cols = slice(part + h * HEAD_DIM, part + (h + 1) * HEAD_DIM)
        v_cols = slice(2 * part + h * HEAD_DIM, 2 * part + (h + 1) * HEAD_DIM)
        query = proj_ref[:, cols] * q_scale * gain_q_ref[:, cols]
        key = proj_ref[:, k_cols] * k_scale * gain_k_ref[:, cols]
        query = (query * cosine + pltpu.roll(query, HEAD_DIM // 2, 1) * sine_part).astype(BF16)
        key = (key * cosine + pltpu.roll(key, HEAD_DIM // 2, 1) * sine_part).astype(BF16)
        value = proj_ref[:, v_cols].astype(BF16)
        q_ref[:, cols] = query
        k_ref[:, cols] = key
        v_ref[:, cols] = value
        scores = dot_t(query, key) * SCORE_SCALE + bias_ref[...]
        top = jnp.max(scores, axis=-1, keepdims=True)
        powers = jnp.exp(scores - top)
        total = jnp.sum(powers, axis=-1, keepdims=True)
        lse_all = jnp.where(lane == h, top + jnp.log(total), lse_all)
        attended_ref[:, cols] = dot((powers / total).astype(BF16), value).astype(BF16)
    lse_ref[...] = lse_all
    step = 512
    for c in range(w_ref.shape[1] // step):
        cols = slice(c * step, (c + 1) * step)
        for n, ref in enumerate(part_refs):
            got = dot(attended_ref[n * LANES : (n + 1) * LANES, :], w_ref[:, cols])
            ref[:, :, cols] = got.astype(BF16).reshape(2, LANES // 2, step)


def settle_kernel(x_ref, a0, a1, a2, b0, b1, b2, gain_ref, residual_ref, mixed_ref):
    for n, refs in enumerate(((a0, a1, a2), (b0, b1, b2))):
        residual = x_ref[n].astype(F32) + total_of([r[...] for r in refs])
        residual_ref[n] = residual
        mixed_ref[n] = (residual * rms_scale(residual) * gain_ref[...]).astype(BF16)


def flip_kernel(gate_ref, up_ref, down_ref, gate_up_t_ref, down_t_ref):
    unit_part = gate_ref.shape[2]
    for e in range(2):
        low = e * unit_part
        gate_up_t_ref[low : low + unit_part, :] = gate_ref[e].T
        gate_up_t_ref[2 * unit_part + low : 2 * unit_part + low + unit_part, :] = up_ref[e].T
        down_t_ref[:, low : low + unit_part] = down_ref[e].T


def flip_call(w_gate, w_up, w_down):
    two, width, unit_part = w_gate.shape
    step = 512
    tall = pl.BlockSpec((two, step, unit_part), lambda i: (0, i, 0))
    return pl.pallas_call(
        flip_kernel,
        grid=(width // step,),
        in_specs=[tall, tall, pl.BlockSpec((two, unit_part, step), lambda i: (0, 0, i))],
        out_specs=[
            pl.BlockSpec((4 * unit_part, step), lambda i: (0, i)),
            pl.BlockSpec((step, 2 * unit_part), lambda i: (i, 0)),
        ],
        out_shape=[out((4 * unit_part, width), BF16), out((width, 2 * unit_part), BF16)],
        cost_estimate=pl.CostEstimate(flops=0, bytes_accessed=12 * w_gate.size, transcendentals=0),
        name="flip",
    )(w_gate, w_up, w_down)


def lead_kernel(cot_ref, down_t_ref, lead_ref):
    width = down_t_ref.shape[0]
    cot = cot_ref[...].reshape(-1, cot_ref.shape[5])[:, :width]
    lead_ref[0, 0] = dot(cot, down_t_ref[...]).reshape(lead_ref.shape[2:])


def lead_call(cot, down_t):
    shards, chips, cores, two, rows, columns = cot.shape
    width, units = down_t.shape
    count = shards * two * rows
    return pl.pallas_call(
        lead_kernel,
        grid=(chips, cores),
        in_specs=[
            pl.BlockSpec((shards, 1, 1, two, rows, columns), lambda i, c: (0, i, c, 0, 0, 0)),
            whole(down_t.shape),
        ],
        out_specs=pl.BlockSpec((1, 1, shards * two, rows, units), lambda i, c: (i, c, 0, 0, 0)),
        out_shape=out((chips, cores, shards * two, rows, units), F32),
        cost_estimate=pl.CostEstimate(
            flops=2 * chips * cores * count * down_t.size,
            bytes_accessed=2 * cot.size + 4 * chips * cores * count * units,
            transcendentals=0,
        ),
        name="lead",
    )(cot, down_t)


def join_kernel(a_ref, b_ref, c_ref, d_ref, out_ref):
    for n, ref in enumerate((a_ref, b_ref, c_ref, d_ref)):
        out_ref[2 * n : 2 * n + 2] = ref[:, 0]


def join_call(parts, j):
    two, _, rows, width = parts[0].shape
    step = rows // 2
    return pl.pallas_call(
        join_kernel,
        grid=(2,),
        in_specs=[pl.BlockSpec((two, 1, step, width), lambda i: (0, j, i, 0))] * 4,
        out_specs=pl.BlockSpec((4 * two, step, width), lambda i: (0, i, 0)),
        out_shape=out((4 * two, rows, width), BF16),
        cost_estimate=pl.CostEstimate(
            flops=0, bytes_accessed=16 * two * rows * width, transcendentals=0
        ),
        name="join",
    )(*parts)


def expert_kernel(experts_all, at_ref, *refs):
    row_refs, routed_ref, lead_ref = refs[:2], refs[2], refs[3]
    gate_ref, up_ref, gate_up_t_ref, router_ref = refs[4:8]
    own_refs, other_ref, grads_ref, scaled_out, scaled_ref = (
        refs[8:12],
        refs[12],
        refs[13],
        refs[14],
        refs[15],
    )
    rows_ref, mask_ref, lead_here_ref = refs[16:]
    width = router_ref.shape[0]
    units = lead_here_ref.shape[1]
    unit_part = units // 2
    half = LANES // 2
    me = at_ref[1]
    now = pl.program_id(0)
    blocks = [block for pair in ORDER for block in pair]
    for side in range(2):

        @pl.when(now == side)
        def _():
            rows_ref[...] = row_refs[side][...].reshape(rows_ref.shape)

    for n, (part, d) in enumerate(blocks):
        to = slice(n * half, (n + 1) * half)
        mask_ref[to, :] = routed_ref[me ^ d, 0, 0, part]
        lead_here_ref[to, :] = lead_ref[0, 0, 2 * (me ^ d) + part]
    rows = rows_ref[...]
    count = rows.shape[0]
    lane = lax.broadcasted_iota(jnp.int32, (count, LANES), 1)
    routed = mask_ref[...].astype(F32)
    powers = jnp.where(lane < experts_all, jnp.exp(dot(rows, router_ref[...])), 0.0)
    weights = powers * routed / jnp.sum(powers, axis=-1, keepdims=True)
    spot = jnp.zeros((count, LANES), F32)
    for e in range(2):
        here = (lane == at_ref[0] * 2 + e).astype(F32)
        chosen = jnp.sum(weights * here, axis=-1, keepdims=True)
        low = e * unit_part
        gate_pre = dot(rows, gate_ref[e])
        up_pre = dot(rows, up_ref[e])
        lead = lead_here_ref[:, low : low + unit_part]
        sigmoid_gate = 1.0 / (1.0 + jnp.exp(-gate_pre))
        silu_gate = gate_pre * sigmoid_gate
        hidden = (silu_gate * up_pre).astype(BF16).astype(F32)
        spot = spot + jnp.sum(hidden * lead, axis=-1, keepdims=True) * (here * routed)
        grad_hidden = lead * chosen
        gate_grad = grad_hidden * up_pre * sigmoid_gate * (1.0 + gate_pre * (1.0 - sigmoid_gate))
        grads_ref[0, :, low : low + unit_part] = gate_grad.astype(BF16)
        grads_ref[0, :, units + low : units + low + unit_part] = (grad_hidden * silu_gate).astype(
            BF16
        )
        scaled_ref[0, :, low : low + unit_part] = (hidden * chosen).astype(BF16)
    for n, (part, d) in enumerate(blocks):
        scaled_out[0, 2 * (me ^ d) + part] = scaled_ref[0, n * half : (n + 1) * half, :]
    mask_ref[...] = spot.astype(BF16)
    step = 512

    @pl.when(now == 0)
    def _():
        for n, ref in enumerate(own_refs):
            at = slice(n * LANES, (n + 1) * LANES)
            ref[:, 0, :, width:] = mask_ref[at, :].reshape(2, half, LANES)
        for c in range(width // step):
            cols = slice(c * step, (c + 1) * step)
            part = dot(grads_ref[0], gate_up_t_ref[:, cols]).astype(BF16)
            for n, ref in enumerate(own_refs):
                at = slice(n * LANES, (n + 1) * LANES)
                ref[:, 0, :, cols] = part[at].reshape(2, half, step)

    @pl.when(now == 1)
    def _():
        for n in range(4):
            at = slice(n * LANES, (n + 1) * LANES)
            other_ref[n, :, 0, :, width:] = mask_ref[at, :].reshape(2, half, LANES)
        for c in range(width // step):
            cols = slice(c * step, (c + 1) * step)
            part = dot(grads_ref[0], gate_up_t_ref[:, cols]).astype(BF16)
            for n in range(4):
                at = slice(n * LANES, (n + 1) * LANES)
                other_ref[n, :, 0, :, cols] = part[at].reshape(2, half, step)


def expert_call(at, rows, cot, lead, w_gate, w_up, gate_up_t, router, experts_all):
    eight, half, width = rows[0].shape
    shards, units = cot.shape[0], lead.shape[4]
    count = eight * half
    own_shape = (2, 1, half, width + LANES)

    def core_of(i, at):
        return lax.rem(at[3] + i, 2)

    return pl.pallas_call(
        lambda *refs: expert_kernel(experts_all, *refs),
        grid_spec=pltpu.PrefetchScalarGridSpec(
            num_scalar_prefetch=1,
            grid=(2,),
            in_specs=[
                pl.BlockSpec(r.shape, lambda i, _: (0, 0, 0), pipeline_mode=pl.Buffered(1))
                for r in rows
            ]
            + [
                pl.BlockSpec(
                    (shards, 1, 1, 2, half, LANES),
                    lambda i, at: (0, at[2], core_of(i, at), 0, 0, width // LANES),
                ),
                pl.BlockSpec(
                    (1, 1, eight, half, units), lambda i, at: (at[2], core_of(i, at), 0, 0, 0)
                ),
            ]
            + [whole(w_gate.shape), whole(w_up.shape), whole(gate_up_t.shape), whole(router.shape)],
            out_specs=[whole(own_shape) for _ in range(4)]
            + [
                whole((4,) + own_shape),
                pl.BlockSpec((1, count, 2 * units), lambda i, _: (i, 0, 0)),
                pl.BlockSpec((1, eight, half, units), lambda i, _: (i, 0, 0, 0)),
                pl.BlockSpec((1, count, units), lambda i, _: (i, 0, 0)),
            ],
            scratch_shapes=[
                pltpu.VMEM((count, width), BF16),
                pltpu.VMEM((count, LANES), BF16),
                pltpu.VMEM((count, units), F32),
            ],
        ),
        out_shape=[out(own_shape, BF16)] * 4
        + [
            out((4,) + own_shape, BF16),
            out((2, count, 2 * units), BF16),
            out((2, eight, half, units), BF16),
            out((2, count, units), BF16),
        ],
        compiler_params=pltpu.CompilerParams(vmem_limit_bytes=48 << 20),
        cost_estimate=pl.CostEstimate(
            flops=8 * count * gate_up_t.size,
            bytes_accessed=8 * count * width + 4 * gate_up_t.size + 20 * count * units,
            transcendentals=2 * count * units,
        ),
        name="experts",
    )(at, *rows, cot, lead, w_gate, w_up, gate_up_t, router)


def mix_kernel(scaled_ref, down_ref, *refs):
    width = down_ref.shape[1]
    half = LANES // 2
    step = 512
    for c in range(width // step):
        cols = slice(c * step, (c + 1) * step)
        part = dot(scaled_ref[0], down_ref[:, cols])
        for n in range(4):
            some = part[n * LANES : (n + 1) * LANES].reshape(2, half, step)
            if len(refs) == 1:
                refs[0][n, :, 0, :, cols] = some.astype(BF16)
            else:
                more = refs[0][n, :, 0, :, cols].astype(F32)
                refs[1 + n][:, 0, :, cols] = (some + more).astype(BF16)


def mix_call(scaled, down, *others):
    chips, count, units = scaled.shape
    width = down.shape[1]
    shape = (2, chips, LANES // 2, width)
    quad = pl.BlockSpec((2, 1, LANES // 2, width), lambda i: (0, i, 0, 0))
    quads = pl.BlockSpec((4, 2, 1, LANES // 2, width), lambda i: (0, 0, i, 0, 0))
    return pl.pallas_call(
        mix_kernel,
        grid=(chips,),
        in_specs=[
            pl.BlockSpec((1, count, units), lambda i: (i, 0, 0)),
            whole(down.shape),
        ]
        + [quads] * len(others),
        out_specs=[quad] * 4 if others else quads,
        out_shape=[out(shape, BF16)] * 4 if others else out((4,) + shape, BF16),
        cost_estimate=pl.CostEstimate(
            flops=2 * scaled.size * width,
            bytes_accessed=2 * scaled.size + 2 * down.size + 4 * chips * count * width,
            transcendentals=0,
        ),
        name="mix",
    )(scaled, down, *others)


def row_grad_kernel(count, *refs):
    rows_refs, grads_refs, out_ref = refs[:count], refs[count:-1], refs[-1]
    _, step, unit_part = out_ref.shape
    total = jnp.zeros((step, 2 * unit_part), F32)
    for n, ref in enumerate(rows_refs):
        total = total + t_dot(ref[...].reshape(-1, step), grads_refs[n // 2][n % 2])
    for e in range(2):
        out_ref[e] = total[:, e * unit_part : (e + 1) * unit_part]


def row_grad_call(groups, which):
    step = 256
    rows = [r for pair, _ in groups for r in pair]
    eight, half, width = rows[0].shape
    _, count, four = groups[0][1].shape
    units = four // 2
    held = pl.BlockSpec((2, count, units), lambda i: (0, 0, which), pipeline_mode=pl.Buffered(1))
    return pl.pallas_call(
        lambda *refs: row_grad_kernel(len(rows), *refs),
        grid=(width // step,),
        in_specs=[pl.BlockSpec((eight, half, step), lambda i: (0, 0, i))] * len(rows)
        + [held] * len(groups),
        out_specs=pl.BlockSpec((2, step, units // 2), lambda i: (0, i, 0)),
        out_shape=out((2, width, units // 2), F32),
        cost_estimate=pl.CostEstimate(
            flops=2 * len(rows) * count * width * units,
            bytes_accessed=2 * len(rows) * count * (width + units) + 4 * width * units,
            transcendentals=0,
        ),
        name="row_grads",
    )(*rows, *[g for _, g in groups])


def down_grad_kernel(count, at_ref, *refs):
    scaled_refs, cot_refs, out_ref = refs[:count], refs[count:-1], refs[-1]
    _, unit_part, step = out_ref.shape
    total = jnp.zeros((2 * unit_part, step), F32)
    for n, scaled_ref in enumerate(scaled_refs):
        for side in range(2):
            cot = cot_refs[2 * n + side][...].reshape(-1, step)
            total = total + t_dot(scaled_ref[side].reshape(-1, 2 * unit_part), cot)
    for e in range(2):
        out_ref[e] = total[e * unit_part : (e + 1) * unit_part]


def down_grad_call(at, scaled, cot):
    step = 256
    shards, _, _, two, half, columns = cot.shape
    _, eight, _, units = scaled[0].shape
    width = (columns // step) * step
    count = len(scaled)

    def tile(n, side):
        return pl.BlockSpec(
            (shards, 1, 1, two, half, step),
            lambda i, at: (0, at[1 + n], lax.rem(at[0] + side, 2), 0, 0, i),
        )

    return pl.pallas_call(
        lambda *refs: down_grad_kernel(count, *refs),
        grid_spec=pltpu.PrefetchScalarGridSpec(
            num_scalar_prefetch=1,
            grid=(width // step,),
            in_specs=[
                pl.BlockSpec(
                    s.shape, lambda i, _: (0, 0, 0, 0), pipeline_mode=pl.Buffered(1)
                )
                for s in scaled
            ]
            + [tile(n, side) for n in range(count) for side in range(2)],
            out_specs=pl.BlockSpec((2, units // 2, step), lambda i, _: (0, 0, i)),
        ),
        out_shape=out((2, units // 2, width), F32),
        cost_estimate=pl.CostEstimate(
            flops=4 * count * eight * half * width * units,
            bytes_accessed=4 * count * eight * half * (width + units) + 4 * width * units,
            transcendentals=0,
        ),
        name="down_grads",
    )(at, *scaled, *([cot] * (2 * count)))


def add_up(parts):
    total = parts[0]
    for part in parts[1:]:
        total = total + part
    return total


def turn_kernel(
    experts_all,
    ring_ref,
    a0,
    a1,
    a2,
    b0,
    b1,
    b2,
    residual_ref,
    cot_ref,
    mixed_ref,
    router_ref,
    router_rows_ref,
    gain_ref,
    grad_ref,
    grad_b_ref,
    gain_grad_ref,
    router_grad_ref,
):
    width = residual_ref.shape[2]
    half = residual_ref.shape[1]
    lane = lax.broadcasted_iota(jnp.int32, (half, LANES), 1)
    gain_grad, router_grad = None, None
    for n, refs in enumerate(((a0, a1, a2), (b0, b1, b2))):
        back = ring_ref[n].astype(F32) + total_of([r[...] for r in refs])
        mixed = mixed_ref[n]
        powers = jnp.where(lane < experts_all, jnp.exp(dot(mixed, router_ref[...])), 0.0)
        probs = powers / jnp.sum(powers, axis=-1, keepdims=True)
        prob_grad = back[:, width:]
        logit_grad = (
            probs * (prob_grad - jnp.sum(probs * prob_grad, axis=-1, keepdims=True))
        ).astype(BF16)
        mixed_grad = back[:, :width] + dot(logit_grad, router_rows_ref[...])
        residual = residual_ref[n]
        norm_grad, gain_now = norm_back(mixed_grad, residual, rms_scale(residual), gain_ref[...])
        total = cot_ref[n] + norm_grad
        grad_ref[n] = total
        grad_b_ref[n] = total.astype(BF16)
        router_now = t_dot(logit_grad, mixed)
        gain_grad = gain_now if gain_grad is None else gain_grad + gain_now
        router_grad = router_now if router_grad is None else router_grad + router_now
    gain_grad_ref[...] = jnp.broadcast_to(gain_grad, gain_grad_ref.shape)
    router_grad_ref[...] = router_grad[: router_grad_ref.shape[0]]


def output_grad_kernel(core_ref, g0, g1, g2, g3, attended_ref, own_ref, other_ref):
    blocks, half, step = own_ref.shape
    own_cols = pl.ds(pl.multiple_of(core_ref[0] * half, half), half)
    other_cols = pl.ds(pl.multiple_of((1 - core_ref[0]) * half, half), half)
    for c in range(blocks):
        cols = slice(c * step, (c + 1) * step)
        grads = jnp.concatenate(
            [g[:, :, cols].reshape(LANES, step) for g in (g0, g1, g2, g3)], axis=0
        )
        own_ref[c] = t_dot(attended_ref[:, own_cols], grads)
        other_ref[c] = t_dot(attended_ref[:, other_cols], grads).astype(BF16)


def attend_back_kernel(
    g0,
    g1,
    g2,
    g3,
    w_ref,
    attended_ref,
    q_ref,
    k_ref,
    v_ref,
    lse_ref,
    scales_ref,
    bias_ref,
    cos_ref,
    sin_ref,
    gain_q_ref,
    gain_k_ref,
    proj_ref,
    query_ref,
    key_ref,
    value_ref,
    stats_ref,
    gains_ref,
    grad_ref,
):
    part, width = w_ref.shape
    rows = proj_ref.shape[0]
    grad_ref[...] = jnp.concatenate(
        [g[...].reshape(LANES, width) for g in (g0, g1, g2, g3)], axis=0
    )
    q_scale, k_scale = scales_ref[:, 0:1], scales_ref[:, 1:2]
    cosine, sine_part = cos_ref[...], sin_ref[...]
    q_inner = jnp.zeros((rows, 1), F32)
    k_inner = jnp.zeros((rows, 1), F32)
    for h in range(part // HEAD_DIM):
        cols = slice(h * HEAD_DIM, (h + 1) * HEAD_DIM)
        k_cols = slice(part + h * HEAD_DIM, part + (h + 1) * HEAD_DIM)
        attended_grad = dot_t(grad_ref[...], w_ref[cols, :]).astype(BF16)
        query, key, value = q_ref[:, cols], k_ref[:, cols], v_ref[:, cols]
        probs = jnp.exp(
            dot_t(query, key) * SCORE_SCALE + bias_ref[...] - lse_ref[:, h : h + 1]
        )
        delta = jnp.sum(
            attended_grad.astype(F32) * attended_ref[:, cols].astype(F32), axis=-1, keepdims=True
        )
        score_grad = (probs * (dot_t(attended_grad, value) - delta)).astype(BF16)
        value_ref[:, cols] = t_dot(probs.astype(BF16), attended_grad).astype(BF16)
        query_grad = dot(score_grad, key) * SCORE_SCALE
        key_grad = t_dot(score_grad, query) * SCORE_SCALE
        query_pre = query_grad * cosine + pltpu.roll(query_grad * sine_part, HEAD_DIM // 2, 1)
        key_pre = key_grad * cosine + pltpu.roll(key_grad * sine_part, HEAD_DIM // 2, 1)
        q_proj, k_proj = proj_ref[:, cols], proj_ref[:, k_cols]
        gains_ref[0:1, cols] = jnp.sum(query_pre * q_proj * q_scale, axis=0, keepdims=True)
        gains_ref[1:2, cols] = jnp.sum(key_pre * k_proj * k_scale, axis=0, keepdims=True)
        query_pre = query_pre * gain_q_ref[:, cols]
        key_pre = key_pre * gain_k_ref[:, cols]
        query_ref[:, cols] = query_pre
        key_ref[:, cols] = key_pre
        q_inner = q_inner + jnp.sum(query_pre * q_proj, axis=-1, keepdims=True)
        k_inner = k_inner + jnp.sum(key_pre * k_proj, axis=-1, keepdims=True)
    for n, stats in enumerate(pack_stats(q_inner, k_inner)):
        stats_ref[n] = stats


def project_back_kernel(
    at_ref, s0, s1, s2, s3, query_ref, key_ref, value_ref, proj_ref, scales_ref, normed_ref, *refs
):
    weight_refs = refs[:8]
    part_refs, pair_ref, all_ref = refs[8:12], refs[12], refs[13]
    width = normed_ref.shape[1]
    part = query_ref.shape[1]
    inner = sum_stats(s0, s1, s2, s3) / width
    for n, (grad_ref, low) in enumerate(((query_ref, 0), (key_ref, part))):
        scale = scales_ref[:, n : n + 1]
        factor = scale * scale * inner[:, n : n + 1]
        all_ref[:, low : low + part] = (
            scale * (grad_ref[...] - proj_ref[:, low : low + part] * factor)
        ).astype(BF16)
    all_ref[:, 2 * part :] = value_ref[...]
    depth = weight_refs[0].shape[0]
    for n, ref in enumerate(weight_refs):
        at = pl.ds(pl.multiple_of(at_ref[n] * depth, depth), depth)
        got = dot_t(all_ref[...], ref[...]).astype(BF16)
        for k, part_ref in enumerate(part_refs):
            part_ref[:, :, at] = got[k * LANES : (k + 1) * LANES].reshape(2, LANES // 2, depth)
    members, parts, rows, _ = pair_ref.shape
    for p in range(parts):
        for third in range(2):
            cols = slice(third * part, (third + 1) * part)
            got = t_dot(normed_ref[:, p * part : (p + 1) * part], all_ref[:, cols]).astype(BF16)
            for e in range(members):
                pair_ref[e, p, :, cols] = got[e * rows : (e + 1) * rows]


def value_back_kernel(core_ref, value_ref, normed_ref, own_ref, other_ref):
    parts, depth, _ = own_ref.shape
    for p in range(parts):
        for ref, side in ((own_ref, core_ref[0]), (other_ref, 1 - core_ref[0])):
            at = pl.ds(pl.multiple_of((2 * p + side) * depth, depth), depth)
            ref[p] = t_dot(normed_ref[:, at], value_ref[...]).astype(ref.dtype)


def finish_kernel(a0, a1, a2, b0, b1, b2, x_ref, grad_ref, gain_ref, out_ref, gain_grad_ref):
    gain_grad = None
    for n, refs in enumerate(((a0, a1, a2), (b0, b1, b2))):
        source = x_ref[n].astype(F32)
        normed_grad = total_of([r[...] for r in refs])
        norm_grad, gain_now = norm_back(normed_grad, source, rms_scale(source), gain_ref[...])
        out_ref[n] = grad_ref[n] + norm_grad
        gain_grad = gain_now if gain_grad is None else gain_grad + gain_now
    gain_grad_ref[...] = jnp.broadcast_to(gain_grad, gain_grad_ref.shape)


def cut_kernel(at_ref, *refs):
    sources, (own_ref, spare_ref, x_ref, y_ref) = refs[:15], refs[15:]
    depth, part = sources[0].shape
    rows = depth // 2
    for w in range(3):
        cols = slice(w * part, (w + 1) * part)
        own_ref[:, cols] = sources[w][...]
        x_ref[:depth, cols] = sources[3 + w][...]
        y_ref[:depth, cols] = sources[6 + w][...]
        x_ref[depth:, cols] = sources[9 + w][:rows, :]
        y_ref[depth:, cols] = sources[9 + w][rows:, :]
        spare_ref[:, cols] = sources[12 + w][...]


def cut_call(at, w_query, w_key, w_value):
    rows, width = w_query.shape
    part = width // 4
    depth = rows // 2

    def block(member, core):
        return pl.BlockSpec((depth, part), lambda i, at: (at[core], at[member]))

    full, more = (depth, 3 * part), (3 * depth // 2, 3 * part)
    fulls = [full, full, more, more]
    return pl.pallas_call(
        cut_kernel,
        grid_spec=pltpu.PrefetchScalarGridSpec(
            num_scalar_prefetch=1,
            grid=(1,),
            in_specs=[block(d, 4) for d in range(4) for _ in range(3)]
            + [block(0, 5) for _ in range(3)],
            out_specs=[whole(s) for s in fulls],
        ),
        out_shape=[out(s, BF16) for s in fulls],
        name="cut",
    )(at, *([w_query, w_key, w_value] * 5))


def on_device(
    block_input,
    segment_ids,
    expert_routes,
    attn_gain,
    w_query,
    w_key,
    w_value,
    query_gain,
    key_gain,
    w_output,
    moe_gain,
    w_router,
    w_gate,
    w_up,
    w_down,
    out_cotangent,
):
    expert_count = lax.axis_size("expert")
    shard_count = lax.axis_size("shard")
    chips = expert_count // 2
    me = lax.axis_index("shard")
    place = lax.axis_index("expert")
    core = lax.rem(place, 2)
    chip = place // 2
    tok_count = block_input.shape[1]
    half = tok_count // 2
    group_count = segment_ids.shape[1]
    width = block_input.shape[2]
    part = width // shard_count
    local_experts = w_gate.shape[0]
    experts_all = local_experts * expert_count
    unit_part = w_gate.shape[2]
    units = local_experts * unit_part
    core_at = jnp.reshape(core, (1,))

    own_input = block_input.reshape(2, half, width)
    group_input = [b.reshape(2, half, width) for b in spread_xy(own_input[:1], own_input[1:])]

    small = jnp.concatenate([attn_gain[None], moe_gain[None], w_router.T], axis=0)
    small = jnp.pad(small, ((0, (-small.shape[0]) % 32), (0, 0)))
    small_all = jnp.zeros((small.shape[0], width), BF16)
    small_parts = gather_parts(small)
    for d, got in enumerate(small_parts):
        small_all = lax.dynamic_update_slice_in_dim(small_all, got, (me ^ d) * part, 1)
    gain_one = small_all[0:1].astype(F32)
    gain_two = small_all[1:2].astype(F32)
    router = small_all[2 : 2 + experts_all]
    router = jnp.pad(router, ((0, LANES - experts_all), (0, 0)))
    router_t = router.T

    depth = part // 2
    at = jnp.stack([me, me ^ 1, me ^ 2, me ^ 3, core, 1 - core])
    cuts = cut_call(at, w_query, w_key, w_value)
    gate_up_t, down_t = flip_call(w_gate, w_up, w_down)
    direct = exchange_blocks(
        *after(cuts[2:], group_input[0], group_input[2], small_parts), group_input, gate_up_t
    )
    passed = [swap_core(block) for block in direct]
    weight_blocks = list(cuts[:2]) + direct + passed
    weight_at = jnp.stack(
        [2 * me + core, 2 * me + 1 - core]
        + [2 * (me ^ d) + core for d in (1, 2, 3)]
        + [2 * (me ^ d) + 1 - core for d in (1, 2, 3)]
    )

    routes = expert_routes[0]
    routed = jnp.sum(
        (routes[:, :, None] == jnp.arange(experts_all)[None, None, :]).astype(F32), axis=1
    )
    cotangent = out_cotangent[0]
    cot_block = (
        jnp.concatenate(
            [cotangent, routed, jnp.zeros((tok_count, LANES - experts_all), F32)], axis=1
        )
        .astype(BF16)
    )
    cot = lax.all_gather(cot_block, ("shard", "expert"), axis=0, tiled=True)

    down_w = w_down.reshape(units, width)

    starts = [(me ^ d) * tok_count + side * half for pair in ORDER for side, d in pair]
    position = jnp.concatenate([p + jnp.arange(half) for p in starts])
    seg_all = segment_ids[0]
    seg_here = jnp.concatenate([lax.dynamic_slice_in_dim(seg_all, p, half) for p in starts])
    allowed = (seg_here[:, None] == seg_here[None, :]) & (position[None, :] <= position[:, None])
    bias = jnp.where(allowed, 0.0, -1e30).astype(F32)
    half_dim = HEAD_DIM // 2
    inverse = 10000.0 ** (-(jnp.arange(half_dim).astype(F32) * 2.0) / HEAD_DIM)
    angles = position.astype(F32)[:, None] * inverse[None, :]
    cosine = jnp.concatenate([jnp.cos(angles), jnp.cos(angles)], axis=-1)
    sine_part = jnp.concatenate([-jnp.sin(angles), jnp.sin(angles)], axis=-1)
    gain_query = query_gain.astype(F32)[None]
    gain_key = key_gain.astype(F32)[None]
    normed, proj, squares, scale_one = call(
        project_kernel,
        "project",
        [weight_at] + group_input + [gain_one] + weight_blocks,
        [
            out((group_count, width), BF16),
            out((group_count, 3 * part), F32),
            out((4, 8, LANES), F32),
            out((group_count, LANES), F32),
        ],
        2 * group_count * width * 3 * part,
        smem=(0,),
    )
    quad = out((2, half, width), BF16)
    square_parts = out((group_count, part), BF16)
    heads = call(
        lambda *refs: attend_kernel(width, *refs),
        "attend",
        [proj] + gather_parts(squares) + [gain_query, gain_key, cosine, sine_part, bias, w_output],
        [square_parts] * 3
        + [out((group_count, LANES), F32)] * 2
        + [square_parts]
        + [quad] * 4,
        4 * group_count * group_count * part + 2 * group_count * part * width,
    )
    q_heads, k_heads, v_heads, log_total, scales, attended = heads[:6]
    terms_a, terms_b = reduce_xy([b.reshape(2, 1, half, width) for b in heads[6:]])
    residual, mixed_in = call(
        settle_kernel,
        "settle",
        [own_input]
        + [t.reshape(half, width) for t in terms_a + terms_b]
        + [gain_two],
        [out((2, half, width), F32), out((2, half, width), BF16)],
        tok_count * width,
    )

    pieces = [mixed_in, ring_up(mixed_in)]
    cot = after(cot, mixed_in).reshape(shard_count, chips, 2, 2, half, width + LANES)
    lead = lead_call(cot, down_t)
    pieces[1] = after(pieces[1], lead)
    while len(pieces) < chips:
        pieces.append(ring_up(pieces[-1]))
    chip_at = [lax.rem(chip + chips - j, chips) for j in range(chips)]
    lows, low = [0, 1], 2
    while low < chips:
        lows.append(low)
        low *= 2
    lows.append(chips)
    all_rows, firsts = [], []
    for low, high in zip(lows[:-1], lows[1:]):
        sides = [jnp.stack([p[s] for p in pieces[low:high]]) for s in range(2)]
        pair_a = jnp.stack([sides[0], swap_x(sides[0])])
        pair_b = jnp.stack([sides[1], swap_y(sides[1])])
        firsts.append((pair_a, pair_b))
        if low > 1:
            pair_a, pair_b = after((pair_a, pair_b), all_rows[1][0])
        parts = [pair_a, swap_y(pair_a), pair_b, swap_x(pair_b)]
        for j in range(high - low):
            own = join_call(parts, j)
            all_rows.append((own, swap_core(own)))
    groups, totals_all = [], []
    for j in range(chips):
        at = jnp.stack([place, me, chip_at[j], core])
        at = after(at, totals_all[j - 2] if j > 1 else firsts[:3])
        got = expert_call(
            at, all_rows[j], cot, lead, w_gate, w_up, gate_up_t, router_t, experts_all
        )
        groups.append((all_rows[j], got[5], got[6], got[7]))
        if 0 < j < chips - 1:
            passed_back = swap_core(after(got[4], all_rows[j + 1][1]))
        else:
            passed_back = swap_core(got[4])
        totals_all.append(
            [
                (a.astype(F32) + passed_back[n].astype(F32)).astype(BF16)
                for n, a in enumerate(got[:4])
            ]
        )
    back_terms = [None] * chips

    def back_piece(j):
        return jnp.stack([total_of(terms) for terms in back_terms[j]])

    back_pieces, arrived = [], []
    for j in list(range(1, chips)) + [0]:
        totals = totals_all[j]
        if j == 0:
            totals = after(totals, totals_all[-1], back_pieces[min(1, chips - 2)])
        back_terms[j] = [
            [t[0] for t in terms]
            for terms in reduce_xy(
                after(totals, [r[0] for r in all_rows]),
                totals_all[-1] if j != 1 else (),
                back_pieces[-1:],
                arrived[-1:],
            )
        ]
        if j:
            back_pieces.append(back_piece(j))
        if j == 1:
            ring_total = back_pieces[0].astype(BF16)
        elif j:
            arrived.append(ring_up(ring_total))
            ring_total = (arrived[-1].astype(F32) + back_pieces[-1]).astype(BF16)
    scaled_sides = [
        jnp.concatenate([g[3][side : side + 1] for g in groups]) for side in range(2)
    ]
    mix_passed = swap_core(mix_call(after(scaled_sides[1], arrived[0], back_pieces[1]), down_w))

    ring_total = ring_up(ring_total)
    grad_res, grad_res_b, grad_gain_two, grad_router = call(
        lambda *refs: turn_kernel(experts_all, *refs),
        "turn",
        [ring_total]
        + back_terms[0][0]
        + back_terms[0][1]
        + [residual, cotangent.reshape(2, half, width), mixed_in, router_t, router]
        + [gain_two],
        [
            out((2, half, width), F32),
            out((2, half, width), BF16),
            out((8, width), F32),
            out((experts_all, width), F32),
        ],
        8 * tok_count * width * LANES,
    )

    group_grad = [b.reshape(2, half, width) for b in spread_xy(grad_res_b[:1], grad_res_b[1:])]
    out_totals = mix_call(
        after(scaled_sides[0], group_grad[0], group_grad[2]), down_w, mix_passed
    )
    output_own, output_other = call(
        output_grad_kernel,
        "output_grad",
        [core_at] + after(group_grad, out_totals) + [attended],
        [out((4, part // 2, width // 4), F32), out((4, part // 2, width // 4), BF16)],
        2 * group_count * part * width,
        smem=(0,),
    )
    query_pre, key_pre, value_grad, inner, gain_grads, _ = call(
        attend_back_kernel,
        "attend_back",
        after(group_grad, output_other)
        + [w_output, attended, q_heads, k_heads, v_heads, log_total, scales, bias]
        + [cosine, sine_part, gain_query, gain_key, proj],
        [
            out((group_count, part), F32),
            out((group_count, part), F32),
            square_parts,
            out((4, 8, LANES), F32),
            out((8, part), F32),
            out((group_count, width), BF16),
        ],
        10 * group_count * group_count * part + 2 * group_count * part * width,
    )
    def split_rows(own):
        parts, rows, columns = own.shape
        split = own.reshape(parts, chips, rows // chips, columns)
        return [lax.dynamic_index_in_dim(split, at, 1, keepdims=False) for at in chip_at]

    inner_parts = gather_parts(inner)
    keep_a, send_a, keep_b, send_b = after(out_totals, inner_parts)
    got_a, got_b = swap_y(send_a), swap_x(send_b)
    out_far = (
        (keep_a[1].astype(F32) + got_a[1].astype(F32)).astype(BF16),
        (keep_b[1].astype(F32) + got_b[1].astype(F32)).astype(BF16),
    )
    out_terms = (
        (keep_a[0], got_a[0], swap_x(out_far[0])),
        (keep_b[0], got_b[0], swap_y(out_far[1])),
    )

    def out_piece(j):
        return jnp.stack([total_of([t[j] for t in side]) for side in out_terms])

    def ring_add(total, pieces, *others):
        moved = after(ring_up(total), *others)
        return (moved.astype(F32) + pieces.pop(0)).astype(BF16)

    output_passed = after(swap_core(output_other), query_pre)
    output_pieces = split_rows(output_own + output_passed.astype(F32))
    output_pieces = output_pieces[1:] + output_pieces[:1]
    output_total = output_pieces.pop(0).astype(BF16)
    value_own, value_other = call(
        value_back_kernel,
        "value_back",
        [core_at] + after([value_grad], inner, output_total) + [normed],
        [out((4, depth, part), F32), out((4, depth, part), BF16)],
        2 * group_count * width * part,
        smem=(0,),
    )
    value_passed = swap_core(value_other)
    output_total = ring_add(output_total, output_pieces, value_other)
    got = call(
        project_back_kernel,
        "project_back",
        [weight_at]
        + inner_parts
        + after([query_pre, key_pre, value_grad, proj, scales, normed], output_total)
        + weight_blocks,
        [quad] * 4
        + [
            out((expert_count, 4, part // expert_count, 2 * part), BF16),
            out((group_count, 3 * part), BF16),
        ],
        4 * group_count * width * 3 * part,
        smem=(0,),
    )
    def exchange_grads(piece):
        sent = [lax.dynamic_index_in_dim(piece, me ^ d, 0, keepdims=False) for d in range(4)]
        low = sent[3].shape[0] // 2
        arrived = exchange_blocks(
            jnp.concatenate([sent[1], sent[3][:low]], axis=0),
            jnp.concatenate([sent[2], sent[3][low:]], axis=0),
        )
        return jnp.stack([sent[0]] + arrived)

    def whole_grads(rows):
        shares = [lax.dynamic_index_in_dim(rows, me ^ p, 0, keepdims=False) for p in range(4)]
        return [
            jnp.concatenate(
                [share[:, n * part : (n + 1) * part] for share in shares], axis=1
            ).astype(F32)
            for n in range(rows.shape[2] // part)
        ]

    pair_sums = lax.psum_scatter(got[4], "expert", scatter_dimension=0, tiled=True)[0]

    span = min(chips, 4)
    starts = range(0, chips, span)

    def row_grads(which, *others):
        late = after([g[1] for g in groups], *others)
        return add_up(
            [
                row_grad_call([(g[0], v) for g, v in zip(groups, late)][low : low + span], which)
                for low in starts
            ]
        )

    def down_grads(*others):
        late = after([g[2] for g in groups], *others)
        return add_up(
            [
                down_grad_call(
                    jnp.stack([core] + chip_at[low : low + span]), late[low : low + span], cot
                )
                for low in starts
            ]
        )

    expert_grads = [down_grads(got[0])]
    output_total = ring_add(output_total, output_pieces, expert_grads[0])
    value_pieces = split_rows(
        value_own + after(value_passed, expert_grads[0]).astype(F32)
    )
    value_pieces = value_pieces[1:] + value_pieces[:1]
    total = value_pieces.pop(0).astype(BF16)
    expert_grads.append(row_grads(0, total, output_total))
    total = ring_add(total, value_pieces, expert_grads[1])
    output_total = ring_add(output_total, output_pieces, expert_grads[1])
    first_kept, first_on = reduce_first(
        [b.reshape(2, 1, half, width) for b in got[:4]], total, output_total
    )
    expert_grads.append(row_grads(1, total, output_total, first_on, out_far))
    while output_pieces:
        output_total = ring_add(output_total, output_pieces, expert_grads[2])
    out_spread = [output_total]
    while len(value_pieces) > 1:
        total = ring_add(total, value_pieces, expert_grads[2])
    out_spread.append(after(ring_up(out_spread[-1]), total))
    terms_a, terms_b = reduce_last(first_kept, first_on)
    grad_input, grad_gain_one = call(
        finish_kernel,
        "finish",
        [t.reshape(half, width) for t in terms_a + terms_b]
        + [own_input, grad_res, after(gain_one, out_spread[-1])],
        [out((2, half, width), F32), out((8, width), F32)],
        tok_count * width,
    )
    out_now = after(out_piece(1), total).astype(BF16)
    pair_mine = exchange_grads(after(pair_sums, grad_gain_one, out_now))
    pair_rows = lax.all_gather(pair_mine, "expert", axis=0)
    total = ring_add(total, value_pieces, pair_mine)
    spread = [exchange_grads(total)]
    grad_w_down, grad_w_gate, grad_w_up = expert_grads
    for j in range(1, chips):
        moved = after(ring_up(out_now), spread[0])
        if j + 1 < chips:
            out_now = (moved.astype(F32) + out_piece(j + 1)).astype(BF16)
        spread.append(after(ring_up(spread[-1]), out_now if j + 1 < chips else moved))
        if len(out_spread) < chips:
            out_spread.append(after(ring_up(out_spread[-1]), spread[-1]))
    while len(out_spread) < chips:
        out_spread.append(ring_up(out_spread[-1]))
    block_output = residual + (moved.astype(F32) + out_piece(0))
    early_rows = expert_spread(out_spread, core, chip)
    grad_w_output = jnp.concatenate([early_rows[c] for c in range(4)], axis=1).astype(F32)
    (grad_w_value,) = whole_grads(expert_spread(spread, core, chip))
    pair_rows = jnp.transpose(pair_rows, (1, 0, 2, 3)).reshape(4, part, 2 * part)
    grad_w_query, grad_w_key = whole_grads(pair_rows)

    grad_gain_one = after(grad_gain_one, spread[0])
    packed = jnp.concatenate([grad_gain_one[:1], grad_gain_two[:1], grad_router], axis=0)
    rows_used = packed.shape[0]
    packed = jnp.pad(packed, ((0, (-rows_used) % 16), (0, 0)))
    quarters = jnp.stack(
        [lax.dynamic_slice_in_dim(packed, (me ^ d) * part, part, 1) for d in range(4)]
    )
    quarters = quarters[:2] + swap_y(quarters[2:])
    packed = (quarters[0] + swap_x(quarters[1]))[:rows_used]
    packed = after(jnp.concatenate([packed, gain_grads[:2]], axis=0), spread[-1])
    bit = 1
    while bit < expert_count:
        packed = packed + flip_expert(packed, bit)
        bit *= 2
    return (
        block_output.reshape(1, tok_count, width),
        grad_input.reshape(1, tok_count, width),
        packed[0],
        grad_w_query,
        grad_w_key,
        grad_w_value,
        packed[rows_used],
        packed[rows_used + 1],
        grad_w_output,
        packed[1],
        packed[2 : 2 + experts_all].T,
        grad_w_gate,
        grad_w_up,
        grad_w_down,
    )


def solution(mesh):
    placed = (
        P("expert", "shard", None),
        P("expert", None),
        P("expert", "shard", None),
        P("shard"),
        P("shard", None),
        P("shard", None),
        P("shard", None),
        P("shard"),
        P("shard"),
        P("shard", None),
        P("shard"),
        P("shard", None),
        P("expert", None, "shard"),
        P("expert", None, "shard"),
        P("expert", "shard", None),
        P("expert", "shard", None),
    )
    return jax.shard_map(
        on_device,
        mesh=mesh,
        in_specs=placed,
        out_specs=(
            P("expert", "shard", None),
            P("expert", "shard", None),
            P("shard"),
            P("shard", None),
            P("shard", None),
            P("shard", None),
            P("shard"),
            P("shard"),
            P("shard", None),
            P("shard"),
            P("shard", None),
            P("expert", None, "shard"),
            P("expert", None, "shard"),
            P("expert", "shard", None),
        ),
        check_vma=False,
    )
```

```python
import jax
import jax.numpy as jnp
from jax import lax
from jax.experimental import pallas as pl
from jax.experimental.pallas import tpu as pltpu
from jax.sharding import PartitionSpec as P

HEAD_DIM = 128
LANES = 128
EPSILON = 1e-05
SCORE_SCALE = HEAD_DIM ** (-0.5)
F32 = jnp.float32
BF16 = jnp.bfloat16
ORDER = (((0, 0), (0, 1)), ((0, 2), (0, 3)), ((1, 0), (1, 2)), ((1, 1), (1, 3)))


def dot(a, b):
    return jnp.dot(a, b, preferred_element_type=F32)


def dot_t(a, b):
    return lax.dot_general(a, b, (((1,), (1,)), ((), ())), preferred_element_type=F32)


def t_dot(a, b):
    return lax.dot_general(a, b, (((0,), (0,)), ((), ())), preferred_element_type=F32)


def flip_shard(values, bit):
    count = lax.axis_size("shard")
    return lax.ppermute(values, "shard", [(i, i ^ bit) for i in range(count)])


def swap_x(values):
    return flip_shard(values, 1)


def swap_y(values):
    return flip_shard(values, 2)


def swap_far(values):
    return flip_shard(values, 3)


def flip_expert(values, bit):
    count = lax.axis_size("expert")
    return lax.ppermute(values, "expert", [(i, i ^ bit) for i in range(count)])


def swap_core(values):
    return flip_expert(values, 1)


def ring_up(values):
    count = lax.axis_size("expert")
    return lax.ppermute(values, "expert", [(i, (i + 2) % count) for i in range(count)])


def after(values, *others):
    return lax.optimization_barrier((values, others))[0]


def spread_xy(first, second):
    pair_a = jnp.stack([first, swap_x(first)])
    pair_b = jnp.stack([second, swap_y(second)])
    return [pair_a, swap_y(pair_a), pair_b, swap_x(pair_b)]


def reduce_first(blocks, *others):
    keep_a, send_a, keep_b, send_b = blocks
    got_a, got_b = after((swap_y(send_a), swap_x(send_b)), *others)
    on_a = (keep_a[1].astype(F32) + got_a[1].astype(F32)).astype(BF16)
    on_b = (keep_b[1].astype(F32) + got_b[1].astype(F32)).astype(BF16)
    return ((keep_a[0], got_a[0]), (keep_b[0], got_b[0])), (on_a, on_b)


def reduce_last(kept, on):
    return kept[0] + (swap_x(on[0]),), kept[1] + (swap_y(on[1]),)


def reduce_xy(blocks, *others):
    return reduce_last(*reduce_first(blocks, *others))


def reduce_late(gate, *args):
    return after(reduce_xy(*args), gate)


def total_of(terms):
    total = terms[0].astype(F32)
    for term in terms[1:]:
        total = total + term.astype(F32)
    return total


def exchange_blocks(for_x, for_y, *others):
    got_x, got_y = after((swap_x(for_x), swap_y(for_y)), *others)
    depth = 2 * for_x.shape[0] // 3
    far = jnp.concatenate([swap_y(got_x[depth:]), swap_x(got_y[depth:])], axis=0)
    return [got_x[:depth], got_y[:depth], far]


def gather_parts(part):
    return [part, swap_x(part), swap_y(part), swap_far(part)]


def ring_gather(piece):
    pieces = [piece]
    for _ in range(lax.axis_size("expert") // 2 - 1):
        pieces.append(ring_up(pieces[-1]))
    return pieces


def ring_sum(total, pieces):
    for piece in pieces:
        total = (ring_up(total).astype(F32) + piece).astype(BF16)
    return total


def expert_spread(pieces, core, chip):
    chips = lax.axis_size("expert") // 2
    parts, rows, columns = pieces[0].shape
    spread = jnp.zeros((parts, chips, rows, columns), pieces[0].dtype)
    for j, got in enumerate(pieces):
        spread = lax.dynamic_update_slice_in_dim(
            spread, got[:, None], lax.rem(chip + chips - j, chips), 1
        )
    half = spread.reshape(parts, 1, chips * rows, columns)
    other = swap_core(half)
    first = jnp.where(core == 0, half, other)
    second = jnp.where(core == 0, other, half)
    return jnp.concatenate([first, second], axis=1).reshape(parts, 2 * chips * rows, columns)


def rms_scale(values):
    return lax.rsqrt(jnp.mean(values * values, axis=-1, keepdims=True) + EPSILON)


def norm_back(grad_out, source, scale_now, gain_now):
    weighted = grad_out * gain_now
    inner_mean = jnp.mean(weighted * source, axis=-1, keepdims=True)
    grad_source = scale_now * (weighted - source * scale_now * scale_now * inner_mean)
    grad_gain = jnp.sum(grad_out * source * scale_now, axis=0, keepdims=True)
    return (grad_source, grad_gain)


def whole(shape):
    return pl.BlockSpec(shape, lambda *_: (0,) * len(shape))


def scalars():
    return pl.BlockSpec(memory_space=pltpu.SMEM)


def call(kernel, name, args, outs, flops, smem=(), transcendentals=0):
    moved = sum(a.size * a.dtype.itemsize for a in args) + sum(
        o.size * o.dtype.itemsize for o in outs
    )
    return pl.pallas_call(
        kernel,
        in_specs=[scalars() if n in smem else whole(a.shape) for n, a in enumerate(args)],
        out_specs=[whole(o.shape) for o in outs],
        out_shape=outs,
        cost_estimate=pl.CostEstimate(
            flops=flops, bytes_accessed=moved, transcendentals=transcendentals
        ),
        name=name,
    )(*args)


def out(shape, dtype):
    return jax.ShapeDtypeStruct(shape, dtype)


def pack_stats(first, second):
    rows = first.shape[0]
    lane = lax.broadcasted_iota(jnp.int32, (rows, LANES), 1)
    spread = jnp.where(lane == 0, first, jnp.where(lane == 1, second, 0.0))
    return [spread[n : n + LANES].T[:8] for n in range(0, rows, LANES)]


def sum_stats(mine, from_x, from_y, far):
    def turn(values):
        return pltpu.roll(values, LANES // 2, 1)

    totals = [
        mine[0] + turn(from_x[0]) + from_y[1] + turn(far[1]),
        mine[1] + turn(from_x[1]) + from_y[0] + turn(far[0]),
        mine[2] + from_x[3] + turn(from_y[2]) + turn(far[3]),
        mine[3] + from_x[2] + turn(from_y[3]) + turn(far[2]),
    ]
    pad = jnp.zeros((LANES - 8, LANES), F32)
    return jnp.concatenate([jnp.concatenate([t, pad], axis=0).T for t in totals], axis=0)


def project_kernel(
    at_ref, r0, r1, r2, r3, gain_ref, *refs
):
    weight_refs, (normed_ref, proj_ref, stats_ref, scale_ref) = refs[:8], refs[8:]
    part = proj_ref.shape[1] // 3
    for n, ref in enumerate((r0, r1, r2, r3)):
        source = ref[...].reshape(LANES, ref.shape[2]).astype(F32)
        scale = rms_scale(source)
        rows = slice(n * LANES, (n + 1) * LANES)
        normed_ref[rows, :] = (source * scale * gain_ref[...]).astype(BF16)
        scale_ref[rows, :] = jnp.broadcast_to(scale, (LANES, LANES))
    depth = weight_refs[0].shape[0]
    for third in range(3):
        cols = slice(third * part, (third + 1) * part)
        total = None
        for n, ref in enumerate(weight_refs):
            rows = pl.ds(pl.multiple_of(at_ref[n] * depth, depth), depth)
            more = dot(normed_ref[:, rows], ref[:, cols])
            total = more if total is None else total + more
        proj_ref[:, cols] = total
    q_proj, k_proj = proj_ref[:, :part], proj_ref[:, part : 2 * part]
    packed = pack_stats(
        jnp.sum(q_proj * q_proj, axis=-1, keepdims=True),
        jnp.sum(k_proj * k_proj, axis=-1, keepdims=True),
    )
    for n, stats in enumerate(packed):
        stats_ref[n] = stats


def attend_kernel(
    width, proj_ref, s0, s1, s2, s3, gain_q_ref, gain_k_ref, cos_ref, sin_ref, bias_ref, w_ref, *refs
):
    q_ref, k_ref, v_ref, lse_ref, scales_ref, attended_ref = refs[:6]
    part_refs = refs[6:]
    part = w_ref.shape[0]
    rows = proj_ref.shape[0]
    sums = sum_stats(s0, s1, s2, s3)
    scales = lax.rsqrt(sums / width + EPSILON)
    scales_ref[...] = scales
    lane = lax.broadcasted_iota(jnp.int32, (rows, LANES), 1)
    q_scale, k_scale = scales[:, 0:1], scales[:, 1:2]
    cosine, sine_part = cos_ref[...], sin_ref[...]
    lse_all = jnp.zeros((rows, LANES), F32)
    for h in range(part // HEAD_DIM):
        cols = slice(h * HEAD_DIM, (h + 1) * HEAD_DIM)
        k_cols = slice(part + h * HEAD_DIM, part + (h + 1) * HEAD_DIM)
        v_cols = slice(2 * part + h * HEAD_DIM, 2 * part + (h + 1) * HEAD_DIM)
        query = proj_ref[:, cols] * q_scale * gain_q_ref[:, cols]
        key = proj_ref[:, k_cols] * k_scale * gain_k_ref[:, cols]
        query = (query * cosine + pltpu.roll(query, HEAD_DIM // 2, 1) * sine_part).astype(BF16)
        key = (key * cosine + pltpu.roll(key, HEAD_DIM // 2, 1) * sine_part).astype(BF16)
        value = proj_ref[:, v_cols].astype(BF16)
        q_ref[:, cols] = query
        k_ref[:, cols] = key
        v_ref[:, cols] = value
        scores = dot_t(query, key) * SCORE_SCALE + bias_ref[...]
        top = jnp.max(scores, axis=-1, keepdims=True)
        powers = jnp.exp(scores - top)
        total = jnp.sum(powers, axis=-1, keepdims=True)
        lse_all = jnp.where(lane == h, top + jnp.log(total), lse_all)
        attended_ref[:, cols] = dot((powers / total).astype(BF16), value).astype(BF16)
    lse_ref[...] = lse_all
    step = 512
    for c in range(w_ref.shape[1] // step):
        cols = slice(c * step, (c + 1) * step)
        for n, ref in enumerate(part_refs):
            got = dot(attended_ref[n * LANES : (n + 1) * LANES, :], w_ref[:, cols])
            ref[:, :, cols] = got.astype(BF16).reshape(2, LANES // 2, step)


def settle_kernel(x_ref, a0, a1, a2, b0, b1, b2, gain_ref, residual_ref, mixed_ref):
    for n, refs in enumerate(((a0, a1, a2), (b0, b1, b2))):
        residual = x_ref[n].astype(F32) + total_of([r[...] for r in refs])
        residual_ref[n] = residual
        mixed_ref[n] = (residual * rms_scale(residual) * gain_ref[...]).astype(BF16)


def flip_kernel(gate_ref, up_ref, down_ref, gate_up_t_ref, down_t_ref):
    unit_part = gate_ref.shape[2]
    for e in range(2):
        low = e * unit_part
        gate_up_t_ref[low : low + unit_part, :] = gate_ref[e].T
        gate_up_t_ref[2 * unit_part + low : 2 * unit_part + low + unit_part, :] = up_ref[e].T
        down_t_ref[:, low : low + unit_part] = down_ref[e].T


def flip_call(w_gate, w_up, w_down):
    two, width, unit_part = w_gate.shape
    step = 512
    tall = pl.BlockSpec((two, step, unit_part), lambda i: (0, i, 0))
    return pl.pallas_call(
        flip_kernel,
        grid=(width // step,),
        in_specs=[tall, tall, pl.BlockSpec((two, unit_part, step), lambda i: (0, 0, i))],
        out_specs=[
            pl.BlockSpec((4 * unit_part, step), lambda i: (0, i)),
            pl.BlockSpec((step, 2 * unit_part), lambda i: (i, 0)),
        ],
        out_shape=[out((4 * unit_part, width), BF16), out((width, 2 * unit_part), BF16)],
        cost_estimate=pl.CostEstimate(flops=0, bytes_accessed=12 * w_gate.size, transcendentals=0),
        name="flip",
    )(w_gate, w_up, w_down)


def lead_kernel(cot_ref, down_t_ref, lead_ref):
    width = down_t_ref.shape[0]
    cot = cot_ref[...].reshape(-1, cot_ref.shape[5])[:, :width]
    lead_ref[0, 0] = dot(cot, down_t_ref[...]).reshape(lead_ref.shape[2:])


def lead_call(cot, down_t):
    shards, chips, cores, two, rows, columns = cot.shape
    width, units = down_t.shape
    count = shards * two * rows
    return pl.pallas_call(
        lead_kernel,
        grid=(chips, cores),
        in_specs=[
            pl.BlockSpec((shards, 1, 1, two, rows, columns), lambda i, c: (0, i, c, 0, 0, 0)),
            whole(down_t.shape),
        ],
        out_specs=pl.BlockSpec((1, 1, shards * two, rows, units), lambda i, c: (i, c, 0, 0, 0)),
        out_shape=out((chips, cores, shards * two, rows, units), F32),
        cost_estimate=pl.CostEstimate(
            flops=2 * chips * cores * count * down_t.size,
            bytes_accessed=2 * cot.size + 4 * chips * cores * count * units,
            transcendentals=0,
        ),
        name="lead",
    )(cot, down_t)


def join_kernel(a_ref, b_ref, c_ref, d_ref, out_ref):
    for n, ref in enumerate((a_ref, b_ref, c_ref, d_ref)):
        out_ref[2 * n : 2 * n + 2] = ref[:, 0]


def join_call(parts, j):
    two, _, rows, width = parts[0].shape
    step = rows // 2
    return pl.pallas_call(
        join_kernel,
        grid=(2,),
        in_specs=[pl.BlockSpec((two, 1, step, width), lambda i: (0, j, i, 0))] * 4,
        out_specs=pl.BlockSpec((4 * two, step, width), lambda i: (0, i, 0)),
        out_shape=out((4 * two, rows, width), BF16),
        cost_estimate=pl.CostEstimate(
            flops=0, bytes_accessed=16 * two * rows * width, transcendentals=0
        ),
        name="join",
    )(*parts)


def expert_kernel(experts_all, at_ref, *refs):
    row_refs, routed_ref, lead_ref = refs[:2], refs[2], refs[3]
    gate_ref, up_ref, gate_up_t_ref, router_ref = refs[4:8]
    own_refs, other_ref, grads_ref, scaled_out, scaled_ref = (
        refs[8:12],
        refs[12],
        refs[13],
        refs[14],
        refs[15],
    )
    rows_ref, mask_ref, lead_here_ref = refs[16:]
    width = router_ref.shape[0]
    units = lead_here_ref.shape[1]
    unit_part = units // 2
    half = LANES // 2
    me = at_ref[1]
    now = pl.program_id(0)
    blocks = [block for pair in ORDER for block in pair]
    for side in range(2):

        @pl.when(now == side)
        def _():
            rows_ref[...] = row_refs[side][...].reshape(rows_ref.shape)

    for n, (part, d) in enumerate(blocks):
        to = slice(n * half, (n + 1) * half)
        mask_ref[to, :] = routed_ref[me ^ d, 0, 0, part]
        lead_here_ref[to, :] = lead_ref[0, 0, 2 * (me ^ d) + part]
    rows = rows_ref[...]
    count = rows.shape[0]
    lane = lax.broadcasted_iota(jnp.int32, (count, LANES), 1)
    routed = mask_ref[...].astype(F32)
    powers = jnp.where(lane < experts_all, jnp.exp(dot(rows, router_ref[...])), 0.0)
    weights = powers * routed / jnp.sum(powers, axis=-1, keepdims=True)
    spot = jnp.zeros((count, LANES), F32)
    for e in range(2):
        here = (lane == at_ref[0] * 2 + e).astype(F32)
        chosen = jnp.sum(weights * here, axis=-1, keepdims=True)
        low = e * unit_part
        gate_pre = dot(rows, gate_ref[e])
        up_pre = dot(rows, up_ref[e])
        lead = lead_here_ref[:, low : low + unit_part]
        sigmoid_gate = 1.0 / (1.0 + jnp.exp(-gate_pre))
        silu_gate = gate_pre * sigmoid_gate
        hidden = (silu_gate * up_pre).astype(BF16).astype(F32)
        spot = spot + jnp.sum(hidden * lead, axis=-1, keepdims=True) * (here * routed)
        grad_hidden = lead * chosen
        gate_grad = grad_hidden * up_pre * sigmoid_gate * (1.0 + gate_pre * (1.0 - sigmoid_gate))
        grads_ref[0, :, low : low + unit_part] = gate_grad.astype(BF16)
        grads_ref[0, :, units + low : units + low + unit_part] = (grad_hidden * silu_gate).astype(
            BF16
        )
        scaled_ref[0, :, low : low + unit_part] = (hidden * chosen).astype(BF16)
    for n, (part, d) in enumerate(blocks):
        scaled_out[0, 2 * (me ^ d) + part] = scaled_ref[0, n * half : (n + 1) * half, :]
    mask_ref[...] = spot.astype(BF16)
    step = 512

    @pl.when(now == 0)
    def _():
        for n, ref in enumerate(own_refs):
            at = slice(n * LANES, (n + 1) * LANES)
            ref[:, 0, :, width:] = mask_ref[at, :].reshape(2, half, LANES)
        for c in range(width // step):
            cols = slice(c * step, (c + 1) * step)
            part = dot(grads_ref[0], gate_up_t_ref[:, cols]).astype(BF16)
            for n, ref in enumerate(own_refs):
                at = slice(n * LANES, (n + 1) * LANES)
                ref[:, 0, :, cols] = part[at].reshape(2, half, step)

    @pl.when(now == 1)
    def _():
        for n in range(4):
            at = slice(n * LANES, (n + 1) * LANES)
            other_ref[n, :, 0, :, width:] = mask_ref[at, :].reshape(2, half, LANES)
        for c in range(width // step):
            cols = slice(c * step, (c + 1) * step)
            part = dot(grads_ref[0], gate_up_t_ref[:, cols]).astype(BF16)
            for n in range(4):
                at = slice(n * LANES, (n + 1) * LANES)
                other_ref[n, :, 0, :, cols] = part[at].reshape(2, half, step)


def expert_call(at, rows, cot, lead, w_gate, w_up, gate_up_t, router, experts_all):
    eight, half, width = rows[0].shape
    shards, units = cot.shape[0], lead.shape[4]
    count = eight * half
    own_shape = (2, 1, half, width + LANES)

    def core_of(i, at):
        return lax.rem(at[3] + i, 2)

    return pl.pallas_call(
        lambda *refs: expert_kernel(experts_all, *refs),
        grid_spec=pltpu.PrefetchScalarGridSpec(
            num_scalar_prefetch=1,
            grid=(2,),
            in_specs=[
                pl.BlockSpec(r.shape, lambda i, _: (0, 0, 0), pipeline_mode=pl.Buffered(1))
                for r in rows
            ]
            + [
                pl.BlockSpec(
                    (shards, 1, 1, 2, half, LANES),
                    lambda i, at: (0, at[2], core_of(i, at), 0, 0, width // LANES),
                ),
                pl.BlockSpec(
                    (1, 1, eight, half, units), lambda i, at: (at[2], core_of(i, at), 0, 0, 0)
                ),
            ]
            + [whole(w_gate.shape), whole(w_up.shape), whole(gate_up_t.shape), whole(router.shape)],
            out_specs=[whole(own_shape) for _ in range(4)]
            + [
                whole((4,) + own_shape),
                pl.BlockSpec((1, count, 2 * units), lambda i, _: (i, 0, 0)),
                pl.BlockSpec((1, eight, half, units), lambda i, _: (i, 0, 0, 0)),
                pl.BlockSpec((1, count, units), lambda i, _: (i, 0, 0)),
            ],
            scratch_shapes=[
                pltpu.VMEM((count, width), BF16),
                pltpu.VMEM((count, LANES), BF16),
                pltpu.VMEM((count, units), F32),
            ],
        ),
        out_shape=[out(own_shape, BF16)] * 4
        + [
            out((4,) + own_shape, BF16),
            out((2, count, 2 * units), BF16),
            out((2, eight, half, units), BF16),
            out((2, count, units), BF16),
        ],
        compiler_params=pltpu.CompilerParams(vmem_limit_bytes=48 << 20),
        cost_estimate=pl.CostEstimate(
            flops=8 * count * gate_up_t.size,
            bytes_accessed=8 * count * width + 4 * gate_up_t.size + 20 * count * units,
            transcendentals=2 * count * units,
        ),
        name="experts",
    )(at, *rows, cot, lead, w_gate, w_up, gate_up_t, router)


def mix_kernel(scaled_ref, down_ref, *refs):
    width = down_ref.shape[1]
    half = LANES // 2
    step = 512
    for c in range(width // step):
        cols = slice(c * step, (c + 1) * step)
        part = dot(scaled_ref[0], down_ref[:, cols])
        for n in range(4):
            some = part[n * LANES : (n + 1) * LANES].reshape(2, half, step)
            if len(refs) == 1:
                refs[0][n, :, 0, :, cols] = some.astype(BF16)
            else:
                more = refs[0][n, :, 0, :, cols].astype(F32)
                refs[1 + n][:, 0, :, cols] = (some + more).astype(BF16)


def mix_call(scaled, down, *others):
    chips, count, units = scaled.shape
    width = down.shape[1]
    shape = (2, chips, LANES // 2, width)
    quad = pl.BlockSpec((2, 1, LANES // 2, width), lambda i: (0, i, 0, 0))
    quads = pl.BlockSpec((4, 2, 1, LANES // 2, width), lambda i: (0, 0, i, 0, 0))
    return pl.pallas_call(
        mix_kernel,
        grid=(chips,),
        in_specs=[
            pl.BlockSpec((1, count, units), lambda i: (i, 0, 0)),
            whole(down.shape),
        ]
        + [quads] * len(others),
        out_specs=[quad] * 4 if others else quads,
        out_shape=[out(shape, BF16)] * 4 if others else out((4,) + shape, BF16),
        cost_estimate=pl.CostEstimate(
            flops=2 * scaled.size * width,
            bytes_accessed=2 * scaled.size + 2 * down.size + 4 * chips * count * width,
            transcendentals=0,
        ),
        name="mix",
    )(scaled, down, *others)


def row_grad_kernel(count, *refs):
    rows_refs, grads_refs, out_ref = refs[:count], refs[count:-1], refs[-1]
    _, step, unit_part = out_ref.shape
    total = jnp.zeros((step, 2 * unit_part), F32)
    for n, ref in enumerate(rows_refs):
        total = total + t_dot(ref[...].reshape(-1, step), grads_refs[n // 2][n % 2])
    for e in range(2):
        out_ref[e] = total[:, e * unit_part : (e + 1) * unit_part]


def row_grad_call(groups, which):
    step = 256
    rows = [r for pair, _ in groups for r in pair]
    eight, half, width = rows[0].shape
    _, count, four = groups[0][1].shape
    units = four // 2
    held = pl.BlockSpec((2, count, units), lambda i: (0, 0, which), pipeline_mode=pl.Buffered(1))
    return pl.pallas_call(
        lambda *refs: row_grad_kernel(len(rows), *refs),
        grid=(width // step,),
        in_specs=[pl.BlockSpec((eight, half, step), lambda i: (0, 0, i))] * len(rows)
        + [held] * len(groups),
        out_specs=pl.BlockSpec((2, step, units // 2), lambda i: (0, i, 0)),
        out_shape=out((2, width, units // 2), F32),
        cost_estimate=pl.CostEstimate(
            flops=2 * len(rows) * count * width * units,
            bytes_accessed=2 * len(rows) * count * (width + units) + 4 * width * units,
            transcendentals=0,
        ),
        name="row_grads",
    )(*rows, *[g for _, g in groups])


def down_grad_kernel(count, at_ref, *refs):
    scaled_refs, cot_refs, out_ref = refs[:count], refs[count:-1], refs[-1]
    _, unit_part, step = out_ref.shape
    total = jnp.zeros((2 * unit_part, step), F32)
    for n, scaled_ref in enumerate(scaled_refs):
        for side in range(2):
            cot = cot_refs[2 * n + side][...].reshape(-1, step)
            total = total + t_dot(scaled_ref[side].reshape(-1, 2 * unit_part), cot)
    for e in range(2):
        out_ref[e] = total[e * unit_part : (e + 1) * unit_part]


def down_grad_call(at, scaled, cot):
    step = 256
    shards, _, _, two, half, columns = cot.shape
    _, eight, _, units = scaled[0].shape
    width = (columns // step) * step
    count = len(scaled)

    def tile(n, side):
        return pl.BlockSpec(
            (shards, 1, 1, two, half, step),
            lambda i, at: (0, at[1 + n], lax.rem(at[0] + side, 2), 0, 0, i),
        )

    return pl.pallas_call(
        lambda *refs: down_grad_kernel(count, *refs),
        grid_spec=pltpu.PrefetchScalarGridSpec(
            num_scalar_prefetch=1,
            grid=(width // step,),
            in_specs=[
                pl.BlockSpec(
                    s.shape, lambda i, _: (0, 0, 0, 0), pipeline_mode=pl.Buffered(1)
                )
                for s in scaled
            ]
            + [tile(n, side) for n in range(count) for side in range(2)],
            out_specs=pl.BlockSpec((2, units // 2, step), lambda i, _: (0, 0, i)),
        ),
        out_shape=out((2, units // 2, width), F32),
        cost_estimate=pl.CostEstimate(
            flops=4 * count * eight * half * width * units,
            bytes_accessed=4 * count * eight * half * (width + units) + 4 * width * units,
            transcendentals=0,
        ),
        name="down_grads",
    )(at, *scaled, *([cot] * (2 * count)))


def add_up(parts):
    total = parts[0]
    for part in parts[1:]:
        total = total + part
    return total


def turn_kernel(
    experts_all,
    ring_ref,
    a0,
    a1,
    a2,
    b0,
    b1,
    b2,
    residual_ref,
    cot_ref,
    mixed_ref,
    router_ref,
    router_rows_ref,
    gain_ref,
    grad_ref,
    grad_b_ref,
    gain_grad_ref,
    router_grad_ref,
):
    width = residual_ref.shape[2]
    half = residual_ref.shape[1]
    lane = lax.broadcasted_iota(jnp.int32, (half, LANES), 1)
    gain_grad, router_grad = None, None
    for n, refs in enumerate(((a0, a1, a2), (b0, b1, b2))):
        back = ring_ref[n].astype(F32) + total_of([r[...] for r in refs])
        mixed = mixed_ref[n]
        powers = jnp.where(lane < experts_all, jnp.exp(dot(mixed, router_ref[...])), 0.0)
        probs = powers / jnp.sum(powers, axis=-1, keepdims=True)
        prob_grad = back[:, width:]
        logit_grad = (
            probs * (prob_grad - jnp.sum(probs * prob_grad, axis=-1, keepdims=True))
        ).astype(BF16)
        mixed_grad = back[:, :width] + dot(logit_grad, router_rows_ref[...])
        residual = residual_ref[n]
        norm_grad, gain_now = norm_back(mixed_grad, residual, rms_scale(residual), gain_ref[...])
        total = cot_ref[n] + norm_grad
        grad_ref[n] = total
        grad_b_ref[n] = total.astype(BF16)
        router_now = t_dot(logit_grad, mixed)
        gain_grad = gain_now if gain_grad is None else gain_grad + gain_now
        router_grad = router_now if router_grad is None else router_grad + router_now
    gain_grad_ref[...] = jnp.broadcast_to(gain_grad, gain_grad_ref.shape)
    router_grad_ref[...] = router_grad[: router_grad_ref.shape[0]]


def output_grad_kernel(core_ref, g0, g1, g2, g3, attended_ref, own_ref, other_ref):
    blocks, half, step = own_ref.shape
    own_cols = pl.ds(pl.multiple_of(core_ref[0] * half, half), half)
    other_cols = pl.ds(pl.multiple_of((1 - core_ref[0]) * half, half), half)
    for c in range(blocks):
        cols = slice(c * step, (c + 1) * step)
        grads = jnp.concatenate(
            [g[:, :, cols].reshape(LANES, step) for g in (g0, g1, g2, g3)], axis=0
        )
        own_ref[c] = t_dot(attended_ref[:, own_cols], grads)
        other_ref[c] = t_dot(attended_ref[:, other_cols], grads).astype(BF16)


def attend_back_kernel(
    g0,
    g1,
    g2,
    g3,
    w_ref,
    attended_ref,
    q_ref,
    k_ref,
    v_ref,
    lse_ref,
    scales_ref,
    bias_ref,
    cos_ref,
    sin_ref,
    gain_q_ref,
    gain_k_ref,
    proj_ref,
    query_ref,
    key_ref,
    value_ref,
    stats_ref,
    gains_ref,
    grad_ref,
):
    part, width = w_ref.shape
    rows = proj_ref.shape[0]
    grad_ref[...] = jnp.concatenate(
        [g[...].reshape(LANES, width) for g in (g0, g1, g2, g3)], axis=0
    )
    q_scale, k_scale = scales_ref[:, 0:1], scales_ref[:, 1:2]
    cosine, sine_part = cos_ref[...], sin_ref[...]
    q_inner = jnp.zeros((rows, 1), F32)
    k_inner = jnp.zeros((rows, 1), F32)
    for h in range(part // HEAD_DIM):
        cols = slice(h * HEAD_DIM, (h + 1) * HEAD_DIM)
        k_cols = slice(part + h * HEAD_DIM, part + (h + 1) * HEAD_DIM)
        attended_grad = dot_t(grad_ref[...], w_ref[cols, :]).astype(BF16)
        query, key, value = q_ref[:, cols], k_ref[:, cols], v_ref[:, cols]
        probs = jnp.exp(
            dot_t(query, key) * SCORE_SCALE + bias_ref[...] - lse_ref[:, h : h + 1]
        )
        delta = jnp.sum(
            attended_grad.astype(F32) * attended_ref[:, cols].astype(F32), axis=-1, keepdims=True
        )
        score_grad = (probs * (dot_t(attended_grad, value) - delta)).astype(BF16)
        value_ref[:, cols] = t_dot(probs.astype(BF16), attended_grad).astype(BF16)
        query_grad = dot(score_grad, key) * SCORE_SCALE
        key_grad = t_dot(score_grad, query) * SCORE_SCALE
        query_pre = query_grad * cosine + pltpu.roll(query_grad * sine_part, HEAD_DIM // 2, 1)
        key_pre = key_grad * cosine + pltpu.roll(key_grad * sine_part, HEAD_DIM // 2, 1)
        q_proj, k_proj = proj_ref[:, cols], proj_ref[:, k_cols]
        gains_ref[0:1, cols] = jnp.sum(query_pre * q_proj * q_scale, axis=0, keepdims=True)
        gains_ref[1:2, cols] = jnp.sum(key_pre * k_proj * k_scale, axis=0, keepdims=True)
        query_pre = query_pre * gain_q_ref[:, cols]
        key_pre = key_pre * gain_k_ref[:, cols]
        query_ref[:, cols] = query_pre
        key_ref[:, cols] = key_pre
        q_inner = q_inner + jnp.sum(query_pre * q_proj, axis=-1, keepdims=True)
        k_inner = k_inner + jnp.sum(key_pre * k_proj, axis=-1, keepdims=True)
    for n, stats in enumerate(pack_stats(q_inner, k_inner)):
        stats_ref[n] = stats


def project_back_kernel(
    at_ref, s0, s1, s2, s3, query_ref, key_ref, value_ref, proj_ref, scales_ref, normed_ref, *refs
):
    weight_refs = refs[:8]
    part_refs, pair_ref, all_ref = refs[8:12], refs[12], refs[13]
    width = normed_ref.shape[1]
    part = query_ref.shape[1]
    inner = sum_stats(s0, s1, s2, s3) / width
    for n, (grad_ref, low) in enumerate(((query_ref, 0), (key_ref, part))):
        scale = scales_ref[:, n : n + 1]
        factor = scale * scale * inner[:, n : n + 1]
        all_ref[:, low : low + part] = (
            scale * (grad_ref[...] - proj_ref[:, low : low + part] * factor)
        ).astype(BF16)
    all_ref[:, 2 * part :] = value_ref[...]
    depth = weight_refs[0].shape[0]
    for n, ref in enumerate(weight_refs):
        at = pl.ds(pl.multiple_of(at_ref[n] * depth, depth), depth)
        got = dot_t(all_ref[...], ref[...]).astype(BF16)
        for k, part_ref in enumerate(part_refs):
            part_ref[:, :, at] = got[k * LANES : (k + 1) * LANES].reshape(2, LANES // 2, depth)
    members, parts, rows, _ = pair_ref.shape
    for p in range(parts):
        for third in range(2):
            cols = slice(third * part, (third + 1) * part)
            got = t_dot(normed_ref[:, p * part : (p + 1) * part], all_ref[:, cols]).astype(BF16)
            for e in range(members):
                pair_ref[e, p, :, cols] = got[e * rows : (e + 1) * rows]


def value_back_kernel(core_ref, value_ref, normed_ref, own_ref, other_ref):
    parts, depth, _ = own_ref.shape
    for p in range(parts):
        for ref, side in ((own_ref, core_ref[0]), (other_ref, 1 - core_ref[0])):
            at = pl.ds(pl.multiple_of((2 * p + side) * depth, depth), depth)
            ref[p] = t_dot(normed_ref[:, at], value_ref[...]).astype(ref.dtype)


def finish_kernel(a0, a1, a2, b0, b1, b2, x_ref, grad_ref, gain_ref, out_ref, gain_grad_ref):
    gain_grad = None
    for n, refs in enumerate(((a0, a1, a2), (b0, b1, b2))):
        source = x_ref[n].astype(F32)
        normed_grad = total_of([r[...] for r in refs])
        norm_grad, gain_now = norm_back(normed_grad, source, rms_scale(source), gain_ref[...])
        out_ref[n] = grad_ref[n] + norm_grad
        gain_grad = gain_now if gain_grad is None else gain_grad + gain_now
    gain_grad_ref[...] = jnp.broadcast_to(gain_grad, gain_grad_ref.shape)


def cut_kernel(at_ref, *refs):
    sources, (own_ref, spare_ref, x_ref, y_ref) = refs[:15], refs[15:]
    depth, part = sources[0].shape
    rows = depth // 2
    for w in range(3):
        cols = slice(w * part, (w + 1) * part)
        own_ref[:, cols] = sources[w][...]
        x_ref[:depth, cols] = sources[3 + w][...]
        y_ref[:depth, cols] = sources[6 + w][...]
        x_ref[depth:, cols] = sources[9 + w][:rows, :]
        y_ref[depth:, cols] = sources[9 + w][rows:, :]
        spare_ref[:, cols] = sources[12 + w][...]


def cut_call(at, w_query, w_key, w_value):
    rows, width = w_query.shape
    part = width // 4
    depth = rows // 2

    def block(member, core):
        return pl.BlockSpec((depth, part), lambda i, at: (at[core], at[member]))

    full, more = (depth, 3 * part), (3 * depth // 2, 3 * part)
    fulls = [full, full, more, more]
    return pl.pallas_call(
        cut_kernel,
        grid_spec=pltpu.PrefetchScalarGridSpec(
            num_scalar_prefetch=1,
            grid=(1,),
            in_specs=[block(d, 4) for d in range(4) for _ in range(3)]
            + [block(0, 5) for _ in range(3)],
            out_specs=[whole(s) for s in fulls],
        ),
        out_shape=[out(s, BF16) for s in fulls],
        name="cut",
    )(at, *([w_query, w_key, w_value] * 5))


def on_device(
    block_input,
    segment_ids,
    expert_routes,
    attn_gain,
    w_query,
    w_key,
    w_value,
    query_gain,
    key_gain,
    w_output,
    moe_gain,
    w_router,
    w_gate,
    w_up,
    w_down,
    out_cotangent,
):
    expert_count = lax.axis_size("expert")
    shard_count = lax.axis_size("shard")
    chips = expert_count // 2
    me = lax.axis_index("shard")
    place = lax.axis_index("expert")
    core = lax.rem(place, 2)
    chip = place // 2
    tok_count = block_input.shape[1]
    half = tok_count // 2
    group_count = segment_ids.shape[1]
    width = block_input.shape[2]
    part = width // shard_count
    local_experts = w_gate.shape[0]
    experts_all = local_experts * expert_count
    unit_part = w_gate.shape[2]
    units = local_experts * unit_part
    core_at = jnp.reshape(core, (1,))

    own_input = block_input.reshape(2, half, width)
    group_input = [b.reshape(2, half, width) for b in spread_xy(own_input[:1], own_input[1:])]

    small = jnp.concatenate([attn_gain[None], moe_gain[None], w_router.T], axis=0)
    small = jnp.pad(small, ((0, (-small.shape[0]) % 32), (0, 0)))
    small_all = jnp.zeros((small.shape[0], width), BF16)
    small_parts = gather_parts(small)
    for d, got in enumerate(small_parts):
        small_all = lax.dynamic_update_slice_in_dim(small_all, got, (me ^ d) * part, 1)
    gain_one = small_all[0:1].astype(F32)
    gain_two = small_all[1:2].astype(F32)
    router = small_all[2 : 2 + experts_all]
    router = jnp.pad(router, ((0, LANES - experts_all), (0, 0)))
    router_t = router.T

    depth = part // 2
    at = jnp.stack([me, me ^ 1, me ^ 2, me ^ 3, core, 1 - core])
    cuts = cut_call(at, w_query, w_key, w_value)
    gate_up_t, down_t = flip_call(w_gate, w_up, w_down)
    direct = exchange_blocks(
        *after(cuts[2:], group_input[0], group_input[2], small_parts), group_input, gate_up_t
    )
    passed = [swap_core(block) for block in direct]
    weight_blocks = list(cuts[:2]) + direct + passed
    weight_at = jnp.stack(
        [2 * me + core, 2 * me + 1 - core]
        + [2 * (me ^ d) + core for d in (1, 2, 3)]
        + [2 * (me ^ d) + 1 - core for d in (1, 2, 3)]
    )

    routes = expert_routes[0]
    routed = jnp.sum(
        (routes[:, :, None] == jnp.arange(experts_all)[None, None, :]).astype(F32), axis=1
    )
    cotangent = out_cotangent[0]
    cot_block = (
        jnp.concatenate(
            [cotangent, routed, jnp.zeros((tok_count, LANES - experts_all), F32)], axis=1
        )
        .astype(BF16)
    )
    cot = lax.all_gather(cot_block, ("shard", "expert"), axis=0, tiled=True)

    down_w = w_down.reshape(units, width)

    starts = [(me ^ d) * tok_count + side * half for pair in ORDER for side, d in pair]
    position = jnp.concatenate([p + jnp.arange(half) for p in starts])
    seg_all = segment_ids[0]
    seg_here = jnp.concatenate([lax.dynamic_slice_in_dim(seg_all, p, half) for p in starts])
    allowed = (seg_here[:, None] == seg_here[None, :]) & (position[None, :] <= position[:, None])
    bias = jnp.where(allowed, 0.0, -1e30).astype(F32)
    half_dim = HEAD_DIM // 2
    inverse = 10000.0 ** (-(jnp.arange(half_dim).astype(F32) * 2.0) / HEAD_DIM)
    angles = position.astype(F32)[:, None] * inverse[None, :]
    cosine = jnp.concatenate([jnp.cos(angles), jnp.cos(angles)], axis=-1)
    sine_part = jnp.concatenate([-jnp.sin(angles), jnp.sin(angles)], axis=-1)
    gain_query = query_gain.astype(F32)[None]
    gain_key = key_gain.astype(F32)[None]
    normed, proj, squares, scale_one = call(
        project_kernel,
        "project",
        [weight_at] + group_input + [gain_one] + weight_blocks,
        [
            out((group_count, width), BF16),
            out((group_count, 3 * part), F32),
            out((4, 8, LANES), F32),
            out((group_count, LANES), F32),
        ],
        2 * group_count * width * 3 * part,
        smem=(0,),
    )
    quad = out((2, half, width), BF16)
    square_parts = out((group_count, part), BF16)
    heads = call(
        lambda *refs: attend_kernel(width, *refs),
        "attend",
        [proj] + gather_parts(squares) + [gain_query, gain_key, cosine, sine_part, bias, w_output],
        [square_parts] * 3
        + [out((group_count, LANES), F32)] * 2
        + [square_parts]
        + [quad] * 4,
        4 * group_count * group_count * part + 2 * group_count * part * width,
    )
    q_heads, k_heads, v_heads, log_total, scales, attended = heads[:6]
    terms_a, terms_b = reduce_xy([b.reshape(2, 1, half, width) for b in heads[6:]])
    residual, mixed_in = call(
        settle_kernel,
        "settle",
        [own_input]
        + [t.reshape(half, width) for t in terms_a + terms_b]
        + [gain_two],
        [out((2, half, width), F32), out((2, half, width), BF16)],
        tok_count * width,
    )

    pieces = [mixed_in, ring_up(mixed_in)]
    cot = after(cot, mixed_in).reshape(shard_count, chips, 2, 2, half, width + LANES)
    lead = lead_call(cot, down_t)
    pieces[1] = after(pieces[1], lead)
    while len(pieces) < chips:
        pieces.append(ring_up(pieces[-1]))
    chip_at = [lax.rem(chip + chips - j, chips) for j in range(chips)]
    lows, low = [0, 1], 2
    while low < chips:
        lows.append(low)
        low *= 2
    lows.append(chips)
    all_rows, firsts = [], []
    for low, high in zip(lows[:-1], lows[1:]):
        sides = [jnp.stack([p[s] for p in pieces[low:high]]) for s in range(2)]
        pair_a = jnp.stack([sides[0], swap_x(sides[0])])
        pair_b = jnp.stack([sides[1], swap_y(sides[1])])
        firsts.append((pair_a, pair_b))
        if low > 1:
            pair_a, pair_b = after((pair_a, pair_b), all_rows[1][0])
        parts = [pair_a, swap_y(pair_a), pair_b, swap_x(pair_b)]
        for j in range(high - low):
            own = join_call(parts, j)
            all_rows.append((own, swap_core(own)))
    groups, totals_all = [], []
    for j in range(chips):
        at = jnp.stack([place, me, chip_at[j], core])
        at = after(at, totals_all[j - 2] if j > 1 else firsts[:3])
        got = expert_call(
            at, all_rows[j], cot, lead, w_gate, w_up, gate_up_t, router_t, experts_all
        )
        groups.append((all_rows[j], got[5], got[6], got[7]))
        if 0 < j < chips - 1:
            passed_back = swap_core(after(got[4], all_rows[j + 1][1]))
        else:
            passed_back = swap_core(got[4])
        totals_all.append(
            [
                (a.astype(F32) + passed_back[n].astype(F32)).astype(BF16)
                for n, a in enumerate(got[:4])
            ]
        )
    back_terms = [None] * chips

    def back_piece(j):
        return jnp.stack([total_of(terms) for terms in back_terms[j]])

    back_pieces, arrived = [], []
    for j in list(range(1, chips)) + [0]:
        totals = totals_all[j]
        if j == 0:
            totals = after(totals, totals_all[-1], back_pieces[min(1, chips - 2)])
        back_terms[j] = [
            [t[0] for t in terms]
            for terms in reduce_late(
                totals_all[-1] if j == 1 else (),
                after(totals, [r[0] for r in all_rows]),
                totals_all[-1] if j != 1 else (),
                back_pieces[-1:],
                arrived[-1:],
            )
        ]
        if j:
            back_pieces.append(back_piece(j))
        if j == 1:
            ring_total = back_pieces[0].astype(BF16)
        elif j:
            arrived.append(ring_up(ring_total))
            ring_total = (arrived[-1].astype(F32) + back_pieces[-1]).astype(BF16)
    scaled_sides = [
        jnp.concatenate([g[3][side : side + 1] for g in groups]) for side in range(2)
    ]
    mix_passed = swap_core(mix_call(after(scaled_sides[1], ring_total), down_w))

    ring_total = ring_up(ring_total)
    grad_res, grad_res_b, grad_gain_two, grad_router = call(
        lambda *refs: turn_kernel(experts_all, *refs),
        "turn",
        [ring_total]
        + back_terms[0][0]
        + back_terms[0][1]
        + [residual, cotangent.reshape(2, half, width), mixed_in, router_t, router]
        + [gain_two],
        [
            out((2, half, width), F32),
            out((2, half, width), BF16),
            out((8, width), F32),
            out((experts_all, width), F32),
        ],
        8 * tok_count * width * LANES,
    )

    group_grad = [b.reshape(2, half, width) for b in spread_xy(grad_res_b[:1], grad_res_b[1:])]
    out_totals = mix_call(
        after(scaled_sides[0], group_grad[0], group_grad[2]), down_w, mix_passed
    )
    output_own, output_other = call(
        output_grad_kernel,
        "output_grad",
        [core_at] + after(group_grad, out_totals) + [attended],
        [out((4, part // 2, width // 4), F32), out((4, part // 2, width // 4), BF16)],
        2 * group_count * part * width,
        smem=(0,),
    )
    query_pre, key_pre, value_grad, inner, gain_grads, _ = call(
        attend_back_kernel,
        "attend_back",
        after(group_grad, output_other)
        + [w_output, attended, q_heads, k_heads, v_heads, log_total, scales, bias]
        + [cosine, sine_part, gain_query, gain_key, proj],
        [
            out((group_count, part), F32),
            out((group_count, part), F32),
            square_parts,
            out((4, 8, LANES), F32),
            out((8, part), F32),
            out((group_count, width), BF16),
        ],
        10 * group_count * group_count * part + 2 * group_count * part * width,
    )
    def split_rows(own):
        parts, rows, columns = own.shape
        split = own.reshape(parts, chips, rows // chips, columns)
        return [lax.dynamic_index_in_dim(split, at, 1, keepdims=False) for at in chip_at]

    inner_parts = gather_parts(inner)
    keep_a, send_a, keep_b, send_b = after(out_totals, inner_parts)
    got_a, got_b = swap_y(send_a), swap_x(send_b)
    out_far = (
        (keep_a[1].astype(F32) + got_a[1].astype(F32)).astype(BF16),
        (keep_b[1].astype(F32) + got_b[1].astype(F32)).astype(BF16),
    )
    out_terms = (
        (keep_a[0], got_a[0], swap_x(out_far[0])),
        (keep_b[0], got_b[0], swap_y(out_far[1])),
    )

    def out_piece(j):
        return jnp.stack([total_of([t[j] for t in side]) for side in out_terms])

    def ring_add(total, pieces, *others):
        moved = after(ring_up(total), *others)
        return (moved.astype(F32) + pieces.pop(0)).astype(BF16)

    output_passed = after(swap_core(output_other), query_pre)
    output_pieces = split_rows(output_own + output_passed.astype(F32))
    output_pieces = output_pieces[1:] + output_pieces[:1]
    output_total = output_pieces.pop(0).astype(BF16)
    value_own, value_other = call(
        value_back_kernel,
        "value_back",
        [core_at] + after([value_grad], inner, output_total) + [normed],
        [out((4, depth, part), F32), out((4, depth, part), BF16)],
        2 * group_count * width * part,
        smem=(0,),
    )
    value_passed = swap_core(value_other)
    output_total = ring_add(output_total, output_pieces, value_other)
    got = call(
        project_back_kernel,
        "project_back",
        [weight_at]
        + inner_parts
        + after([query_pre, key_pre, value_grad, proj, scales, normed], output_total)
        + weight_blocks,
        [quad] * 4
        + [
            out((expert_count, 4, part // expert_count, 2 * part), BF16),
            out((group_count, 3 * part), BF16),
        ],
        4 * group_count * width * 3 * part,
        smem=(0,),
    )
    def exchange_grads(piece):
        sent = [lax.dynamic_index_in_dim(piece, me ^ d, 0, keepdims=False) for d in range(4)]
        low = sent[3].shape[0] // 2
        arrived = exchange_blocks(
            jnp.concatenate([sent[1], sent[3][:low]], axis=0),
            jnp.concatenate([sent[2], sent[3][low:]], axis=0),
        )
        return jnp.stack([sent[0]] + arrived)

    def whole_grads(rows):
        shares = [lax.dynamic_index_in_dim(rows, me ^ p, 0, keepdims=False) for p in range(4)]
        return [
            jnp.concatenate(
                [share[:, n * part : (n + 1) * part] for share in shares], axis=1
            ).astype(F32)
            for n in range(rows.shape[2] // part)
        ]

    pair_sums = lax.psum_scatter(got[4], "expert", scatter_dimension=0, tiled=True)[0]

    span = min(chips, 4)
    starts = range(0, chips, span)

    def row_grads(which, *others):
        late = after([g[1] for g in groups], *others)
        return add_up(
            [
                row_grad_call([(g[0], v) for g, v in zip(groups, late)][low : low + span], which)
                for low in starts
            ]
        )

    def down_grads(*others):
        late = after([g[2] for g in groups], *others)
        return add_up(
            [
                down_grad_call(
                    jnp.stack([core] + chip_at[low : low + span]), late[low : low + span], cot
                )
                for low in starts
            ]
        )

    expert_grads = [down_grads(got[0])]
    output_total = ring_add(output_total, output_pieces, expert_grads[0])
    value_pieces = split_rows(
        value_own + after(value_passed, expert_grads[0]).astype(F32)
    )
    value_pieces = value_pieces[1:] + value_pieces[:1]
    total = value_pieces.pop(0).astype(BF16)
    expert_grads.append(row_grads(0, total, output_total))
    total = ring_add(total, value_pieces, expert_grads[1])
    output_total = ring_add(output_total, output_pieces, expert_grads[1])
    first_kept, first_on = reduce_first(
        [b.reshape(2, 1, half, width) for b in got[:4]], total, output_total
    )
    expert_grads.append(row_grads(1, total, output_total, first_on, out_far))
    while output_pieces:
        output_total = ring_add(output_total, output_pieces, expert_grads[2])
    out_spread = [output_total]
    while len(value_pieces) > 1:
        total = ring_add(total, value_pieces, expert_grads[2])
    out_spread.append(after(ring_up(out_spread[-1]), total))
    terms_a, terms_b = reduce_last(first_kept, first_on)
    grad_input, grad_gain_one = call(
        finish_kernel,
        "finish",
        [t.reshape(half, width) for t in terms_a + terms_b]
        + [own_input, grad_res, after(gain_one, out_spread[-1])],
        [out((2, half, width), F32), out((8, width), F32)],
        tok_count * width,
    )
    out_now = after(out_piece(1), total).astype(BF16)
    pair_mine = exchange_grads(after(pair_sums, grad_gain_one, out_now))
    pair_rows = lax.all_gather(pair_mine, "expert", axis=0)
    total = ring_add(total, value_pieces, pair_mine)
    spread = [exchange_grads(total)]
    grad_w_down, grad_w_gate, grad_w_up = expert_grads
    for j in range(1, chips):
        moved = after(ring_up(out_now), spread[0])
        if j + 1 < chips:
            out_now = (moved.astype(F32) + out_piece(j + 1)).astype(BF16)
        spread.append(after(ring_up(spread[-1]), out_now if j + 1 < chips else moved))
        if len(out_spread) < chips:
            out_spread.append(after(ring_up(out_spread[-1]), spread[-1]))
    while len(out_spread) < chips:
        out_spread.append(ring_up(out_spread[-1]))
    block_output = residual + (moved.astype(F32) + out_piece(0))
    early_rows = expert_spread(out_spread, core, chip)
    grad_w_output = jnp.concatenate([early_rows[c] for c in range(4)], axis=1).astype(F32)
    (grad_w_value,) = whole_grads(expert_spread(spread, core, chip))
    pair_rows = jnp.transpose(pair_rows, (1, 0, 2, 3)).reshape(4, part, 2 * part)
    grad_w_query, grad_w_key = whole_grads(pair_rows)

    grad_gain_one = after(grad_gain_one, spread[0])
    packed = jnp.concatenate([grad_gain_one[:1], grad_gain_two[:1], grad_router], axis=0)
    rows_used = packed.shape[0]
    packed = jnp.pad(packed, ((0, (-rows_used) % 16), (0, 0)))
    quarters = jnp.stack(
        [lax.dynamic_slice_in_dim(packed, (me ^ d) * part, part, 1) for d in range(4)]
    )
    quarters = quarters[:2] + swap_y(quarters[2:])
    packed = (quarters[0] + swap_x(quarters[1]))[:rows_used]
    packed = after(jnp.concatenate([packed, gain_grads[:2]], axis=0), spread[-1])
    bit = 1
    while bit < expert_count:
        packed = packed + flip_expert(packed, bit)
        bit *= 2
    return (
        block_output.reshape(1, tok_count, width),
        grad_input.reshape(1, tok_count, width),
        packed[0],
        grad_w_query,
        grad_w_key,
        grad_w_value,
        packed[rows_used],
        packed[rows_used + 1],
        grad_w_output,
        packed[1],
        packed[2 : 2 + experts_all].T,
        grad_w_gate,
        grad_w_up,
        grad_w_down,
    )


def solution(mesh):
    placed = (
        P("expert", "shard", None),
        P("expert", None),
        P("expert", "shard", None),
        P("shard"),
        P("shard", None),
        P("shard", None),
        P("shard", None),
        P("shard"),
        P("shard"),
        P("shard", None),
        P("shard"),
        P("shard", None),
        P("expert", None, "shard"),
        P("expert", None, "shard"),
        P("expert", "shard", None),
        P("expert", "shard", None),
    )
    return jax.shard_map(
        on_device,
        mesh=mesh,
        in_specs=placed,
        out_specs=(
            P("expert", "shard", None),
            P("expert", "shard", None),
            P("shard"),
            P("shard", None),
            P("shard", None),
            P("shard", None),
            P("shard"),
            P("shard"),
            P("shard", None),
            P("shard"),
            P("shard", None),
            P("expert", None, "shard"),
            P("expert", None, "shard"),
            P("expert", "shard", None),
        ),
        check_vma=False,
    )
```

```python
import jax
import jax.numpy as jnp
from jax import lax
from jax.experimental import pallas as pl
from jax.experimental.pallas import tpu as pltpu
from jax.sharding import PartitionSpec as P

HEAD_DIM = 128
LANES = 128
EPSILON = 1e-05
SCORE_SCALE = HEAD_DIM ** (-0.5)
F32 = jnp.float32
BF16 = jnp.bfloat16
ORDER = (((0, 0), (0, 1)), ((0, 2), (0, 3)), ((1, 0), (1, 2)), ((1, 1), (1, 3)))


def dot(a, b):
    return jnp.dot(a, b, preferred_element_type=F32)


def dot_t(a, b):
    return lax.dot_general(a, b, (((1,), (1,)), ((), ())), preferred_element_type=F32)


def t_dot(a, b):
    return lax.dot_general(a, b, (((0,), (0,)), ((), ())), preferred_element_type=F32)


def flip_shard(values, bit):
    count = lax.axis_size("shard")
    return lax.ppermute(values, "shard", [(i, i ^ bit) for i in range(count)])


def swap_x(values):
    return flip_shard(values, 1)


def swap_y(values):
    return flip_shard(values, 2)


def swap_far(values):
    return flip_shard(values, 3)


def flip_expert(values, bit):
    count = lax.axis_size("expert")
    return lax.ppermute(values, "expert", [(i, i ^ bit) for i in range(count)])


def swap_core(values):
    return flip_expert(values, 1)


def ring_up(values):
    count = lax.axis_size("expert")
    return lax.ppermute(values, "expert", [(i, (i + 2) % count) for i in range(count)])


def after(values, *others):
    return lax.optimization_barrier((values, others))[0]


def spread_xy(first, second):
    pair_a = jnp.stack([first, swap_x(first)])
    pair_b = jnp.stack([second, swap_y(second)])
    return [pair_a, swap_y(pair_a), pair_b, swap_x(pair_b)]


def reduce_first(blocks, *others):
    keep_a, send_a, keep_b, send_b = blocks
    got_a, got_b = after((swap_y(send_a), swap_x(send_b)), *others)
    on_a = (keep_a[1].astype(F32) + got_a[1].astype(F32)).astype(BF16)
    on_b = (keep_b[1].astype(F32) + got_b[1].astype(F32)).astype(BF16)
    return ((keep_a[0], got_a[0]), (keep_b[0], got_b[0])), (on_a, on_b)


def reduce_last(kept, on):
    return kept[0] + (swap_x(on[0]),), kept[1] + (swap_y(on[1]),)


def reduce_xy(blocks, *others):
    return reduce_last(*reduce_first(blocks, *others))


def reduce_late(gate, *args):
    return after(reduce_xy(*args), gate)


def total_of(terms):
    total = terms[0].astype(F32)
    for term in terms[1:]:
        total = total + term.astype(F32)
    return total


def exchange_blocks(for_x, for_y, *others):
    got_x, got_y = after((swap_x(for_x), swap_y(for_y)), *others)
    depth = 2 * for_x.shape[0] // 3
    far = jnp.concatenate([swap_y(got_x[depth:]), swap_x(got_y[depth:])], axis=0)
    return [got_x[:depth], got_y[:depth], far]


def gather_parts(part):
    return [part, swap_x(part), swap_y(part), swap_far(part)]


def ring_gather(piece):
    pieces = [piece]
    for _ in range(lax.axis_size("expert") // 2 - 1):
        pieces.append(ring_up(pieces[-1]))
    return pieces


def ring_sum(total, pieces):
    for piece in pieces:
        total = (ring_up(total).astype(F32) + piece).astype(BF16)
    return total


def expert_spread(pieces, core, chip):
    chips = lax.axis_size("expert") // 2
    parts, rows, columns = pieces[0].shape
    spread = jnp.zeros((parts, chips, rows, columns), pieces[0].dtype)
    for j, got in enumerate(pieces):
        spread = lax.dynamic_update_slice_in_dim(
            spread, got[:, None], lax.rem(chip + chips - j, chips), 1
        )
    half = spread.reshape(parts, 1, chips * rows, columns)
    other = swap_core(half)
    first = jnp.where(core == 0, half, other)
    second = jnp.where(core == 0, other, half)
    return jnp.concatenate([first, second], axis=1).reshape(parts, 2 * chips * rows, columns)


def rms_scale(values):
    return lax.rsqrt(jnp.mean(values * values, axis=-1, keepdims=True) + EPSILON)


def norm_back(grad_out, source, scale_now, gain_now):
    weighted = grad_out * gain_now
    inner_mean = jnp.mean(weighted * source, axis=-1, keepdims=True)
    grad_source = scale_now * (weighted - source * scale_now * scale_now * inner_mean)
    grad_gain = jnp.sum(grad_out * source * scale_now, axis=0, keepdims=True)
    return (grad_source, grad_gain)


def whole(shape):
    return pl.BlockSpec(shape, lambda *_: (0,) * len(shape))


def scalars():
    return pl.BlockSpec(memory_space=pltpu.SMEM)


def call(kernel, name, args, outs, flops, smem=(), transcendentals=0):
    moved = sum(a.size * a.dtype.itemsize for a in args) + sum(
        o.size * o.dtype.itemsize for o in outs
    )
    return pl.pallas_call(
        kernel,
        in_specs=[scalars() if n in smem else whole(a.shape) for n, a in enumerate(args)],
        out_specs=[whole(o.shape) for o in outs],
        out_shape=outs,
        cost_estimate=pl.CostEstimate(
            flops=flops, bytes_accessed=moved, transcendentals=transcendentals
        ),
        name=name,
    )(*args)


def out(shape, dtype):
    return jax.ShapeDtypeStruct(shape, dtype)


def pack_stats(first, second):
    rows = first.shape[0]
    lane = lax.broadcasted_iota(jnp.int32, (rows, LANES), 1)
    spread = jnp.where(lane == 0, first, jnp.where(lane == 1, second, 0.0))
    return [spread[n : n + LANES].T[:8] for n in range(0, rows, LANES)]


def sum_stats(mine, from_x, from_y, far):
    def turn(values):
        return pltpu.roll(values, LANES // 2, 1)

    totals = [
        mine[0] + turn(from_x[0]) + from_y[1] + turn(far[1]),
        mine[1] + turn(from_x[1]) + from_y[0] + turn(far[0]),
        mine[2] + from_x[3] + turn(from_y[2]) + turn(far[3]),
        mine[3] + from_x[2] + turn(from_y[3]) + turn(far[2]),
    ]
    pad = jnp.zeros((LANES - 8, LANES), F32)
    return jnp.concatenate([jnp.concatenate([t, pad], axis=0).T for t in totals], axis=0)


def project_kernel(
    at_ref, r0, r1, r2, r3, gain_ref, *refs
):
    weight_refs, (normed_ref, proj_ref, stats_ref, scale_ref) = refs[:8], refs[8:]
    part = proj_ref.shape[1] // 3
    for n, ref in enumerate((r0, r1, r2, r3)):
        source = ref[...].reshape(LANES, ref.shape[2]).astype(F32)
        scale = rms_scale(source)
        rows = slice(n * LANES, (n + 1) * LANES)
        normed_ref[rows, :] = (source * scale * gain_ref[...]).astype(BF16)
        scale_ref[rows, :] = jnp.broadcast_to(scale, (LANES, LANES))
    depth = weight_refs[0].shape[0]
    for third in range(3):
        cols = slice(third * part, (third + 1) * part)
        total = None
        for n, ref in enumerate(weight_refs):
            rows = pl.ds(pl.multiple_of(at_ref[n] * depth, depth), depth)
            more = dot(normed_ref[:, rows], ref[:, cols])
            total = more if total is None else total + more
        proj_ref[:, cols] = total
    q_proj, k_proj = proj_ref[:, :part], proj_ref[:, part : 2 * part]
    packed = pack_stats(
        jnp.sum(q_proj * q_proj, axis=-1, keepdims=True),
        jnp.sum(k_proj * k_proj, axis=-1, keepdims=True),
    )
    for n, stats in enumerate(packed):
        stats_ref[n] = stats


def attend_kernel(
    width, proj_ref, s0, s1, s2, s3, gain_q_ref, gain_k_ref, cos_ref, sin_ref, bias_ref, w_ref, *refs
):
    q_ref, k_ref, v_ref, lse_ref, scales_ref, attended_ref = refs[:6]
    part_refs = refs[6:]
    part = w_ref.shape[0]
    rows = proj_ref.shape[0]
    sums = sum_stats(s0, s1, s2, s3)
    scales = lax.rsqrt(sums / width + EPSILON)
    scales_ref[...] = scales
    lane = lax.broadcasted_iota(jnp.int32, (rows, LANES), 1)
    q_scale, k_scale = scales[:, 0:1], scales[:, 1:2]
    cosine, sine_part = cos_ref[...], sin_ref[...]
    lse_all = jnp.zeros((rows, LANES), F32)
    for h in range(part // HEAD_DIM):
        cols = slice(h * HEAD_DIM, (h + 1) * HEAD_DIM)
        k_cols = slice(part + h * HEAD_DIM, part + (h + 1) * HEAD_DIM)
        v_cols = slice(2 * part + h * HEAD_DIM, 2 * part + (h + 1) * HEAD_DIM)
        query = proj_ref[:, cols] * q_scale * gain_q_ref[:, cols]
        key = proj_ref[:, k_cols] * k_scale * gain_k_ref[:, cols]
        query = (query * cosine + pltpu.roll(query, HEAD_DIM // 2, 1) * sine_part).astype(BF16)
        key = (key * cosine + pltpu.roll(key, HEAD_DIM // 2, 1) * sine_part).astype(BF16)
        value = proj_ref[:, v_cols].astype(BF16)
        q_ref[:, cols] = query
        k_ref[:, cols] = key
        v_ref[:, cols] = value
        scores = dot_t(query, key) * SCORE_SCALE + bias_ref[...]
        top = jnp.max(scores, axis=-1, keepdims=True)
        powers = jnp.exp(scores - top)
        total = jnp.sum(powers, axis=-1, keepdims=True)
        lse_all = jnp.where(lane == h, top + jnp.log(total), lse_all)
        attended_ref[:, cols] = dot((powers / total).astype(BF16), value).astype(BF16)
    lse_ref[...] = lse_all
    step = 512
    for c in range(w_ref.shape[1] // step):
        cols = slice(c * step, (c + 1) * step)
        for n, ref in enumerate(part_refs):
            got = dot(attended_ref[n * LANES : (n + 1) * LANES, :], w_ref[:, cols])
            ref[:, :, cols] = got.astype(BF16).reshape(2, LANES // 2, step)


def settle_kernel(x_ref, a0, a1, a2, b0, b1, b2, gain_ref, residual_ref, mixed_ref):
    for n, refs in enumerate(((a0, a1, a2), (b0, b1, b2))):
        residual = x_ref[n].astype(F32) + total_of([r[...] for r in refs])
        residual_ref[n] = residual
        mixed_ref[n] = (residual * rms_scale(residual) * gain_ref[...]).astype(BF16)


def flip_kernel(gate_ref, up_ref, down_ref, gate_up_t_ref, down_t_ref):
    unit_part = gate_ref.shape[2]
    for e in range(2):
        low = e * unit_part
        gate_up_t_ref[low : low + unit_part, :] = gate_ref[e].T
        gate_up_t_ref[2 * unit_part + low : 2 * unit_part + low + unit_part, :] = up_ref[e].T
        down_t_ref[:, low : low + unit_part] = down_ref[e].T


def flip_call(w_gate, w_up, w_down):
    two, width, unit_part = w_gate.shape
    step = 512
    tall = pl.BlockSpec((two, step, unit_part), lambda i: (0, i, 0))
    return pl.pallas_call(
        flip_kernel,
        grid=(width // step,),
        in_specs=[tall, tall, pl.BlockSpec((two, unit_part, step), lambda i: (0, 0, i))],
        out_specs=[
            pl.BlockSpec((4 * unit_part, step), lambda i: (0, i)),
            pl.BlockSpec((step, 2 * unit_part), lambda i: (i, 0)),
        ],
        out_shape=[out((4 * unit_part, width), BF16), out((width, 2 * unit_part), BF16)],
        cost_estimate=pl.CostEstimate(flops=0, bytes_accessed=12 * w_gate.size, transcendentals=0),
        name="flip",
    )(w_gate, w_up, w_down)


def lead_kernel(cot_ref, down_t_ref, lead_ref):
    width = down_t_ref.shape[0]
    cot = cot_ref[...].reshape(-1, cot_ref.shape[5])[:, :width]
    lead_ref[0, 0] = dot(cot, down_t_ref[...]).reshape(lead_ref.shape[2:])


def lead_call(cot, down_t):
    shards, chips, cores, two, rows, columns = cot.shape
    width, units = down_t.shape
    count = shards * two * rows
    return pl.pallas_call(
        lead_kernel,
        grid=(chips, cores),
        in_specs=[
            pl.BlockSpec((shards, 1, 1, two, rows, columns), lambda i, c: (0, i, c, 0, 0, 0)),
            whole(down_t.shape),
        ],
        out_specs=pl.BlockSpec((1, 1, shards * two, rows, units), lambda i, c: (i, c, 0, 0, 0)),
        out_shape=out((chips, cores, shards * two, rows, units), F32),
        cost_estimate=pl.CostEstimate(
            flops=2 * chips * cores * count * down_t.size,
            bytes_accessed=2 * cot.size + 4 * chips * cores * count * units,
            transcendentals=0,
        ),
        name="lead",
    )(cot, down_t)


def join_kernel(a_ref, b_ref, c_ref, d_ref, out_ref):
    for n, ref in enumerate((a_ref, b_ref, c_ref, d_ref)):
        out_ref[2 * n : 2 * n + 2] = ref[:, 0]


def join_call(parts, j):
    two, _, rows, width = parts[0].shape
    step = rows // 2
    return pl.pallas_call(
        join_kernel,
        grid=(2,),
        in_specs=[pl.BlockSpec((two, 1, step, width), lambda i: (0, j, i, 0))] * 4,
        out_specs=pl.BlockSpec((4 * two, step, width), lambda i: (0, i, 0)),
        out_shape=out((4 * two, rows, width), BF16),
        cost_estimate=pl.CostEstimate(
            flops=0, bytes_accessed=16 * two * rows * width, transcendentals=0
        ),
        name="join",
    )(*parts)


def expert_kernel(experts_all, at_ref, *refs):
    row_refs, routed_ref, lead_ref = refs[:2], refs[2], refs[3]
    gate_ref, up_ref, gate_up_t_ref, router_ref = refs[4:8]
    own_refs, other_ref, grads_ref, scaled_out, scaled_ref = (
        refs[8:12],
        refs[12],
        refs[13],
        refs[14],
        refs[15],
    )
    rows_ref, mask_ref, lead_here_ref = refs[16:]
    width = router_ref.shape[0]
    units = lead_here_ref.shape[1]
    unit_part = units // 2
    half = LANES // 2
    me = at_ref[1]
    now = pl.program_id(0)
    blocks = [block for pair in ORDER for block in pair]
    for side in range(2):

        @pl.when(now == side)
        def _():
            rows_ref[...] = row_refs[side][...].reshape(rows_ref.shape)

    for n, (part, d) in enumerate(blocks):
        to = slice(n * half, (n + 1) * half)
        mask_ref[to, :] = routed_ref[me ^ d, 0, 0, part]
        lead_here_ref[to, :] = lead_ref[0, 0, 2 * (me ^ d) + part]
    rows = rows_ref[...]
    count = rows.shape[0]
    lane = lax.broadcasted_iota(jnp.int32, (count, LANES), 1)
    routed = mask_ref[...].astype(F32)
    powers = jnp.where(lane < experts_all, jnp.exp(dot(rows, router_ref[...])), 0.0)
    weights = powers * routed / jnp.sum(powers, axis=-1, keepdims=True)
    spot = jnp.zeros((count, LANES), F32)
    for e in range(2):
        here = (lane == at_ref[0] * 2 + e).astype(F32)
        chosen = jnp.sum(weights * here, axis=-1, keepdims=True)
        low = e * unit_part
        gate_pre = dot(rows, gate_ref[e])
        up_pre = dot(rows, up_ref[e])
        lead = lead_here_ref[:, low : low + unit_part]
        sigmoid_gate = 1.0 / (1.0 + jnp.exp(-gate_pre))
        silu_gate = gate_pre * sigmoid_gate
        hidden = (silu_gate * up_pre).astype(BF16).astype(F32)
        spot = spot + jnp.sum(hidden * lead, axis=-1, keepdims=True) * (here * routed)
        grad_hidden = lead * chosen
        gate_grad = grad_hidden * up_pre * sigmoid_gate * (1.0 + gate_pre * (1.0 - sigmoid_gate))
        grads_ref[0, :, low : low + unit_part] = gate_grad.astype(BF16)
        grads_ref[0, :, units + low : units + low + unit_part] = (grad_hidden * silu_gate).astype(
            BF16
        )
        scaled_ref[0, :, low : low + unit_part] = (hidden * chosen).astype(BF16)
    for n, (part, d) in enumerate(blocks):
        scaled_out[0, 2 * (me ^ d) + part] = scaled_ref[0, n * half : (n + 1) * half, :]
    mask_ref[...] = spot.astype(BF16)
    step = 512

    @pl.when(now == 0)
    def _():
        for n, ref in enumerate(own_refs):
            at = slice(n * LANES, (n + 1) * LANES)
            ref[:, 0, :, width:] = mask_ref[at, :].reshape(2, half, LANES)
        for c in range(width // step):
            cols = slice(c * step, (c + 1) * step)
            part = dot(grads_ref[0], gate_up_t_ref[:, cols]).astype(BF16)
            for n, ref in enumerate(own_refs):
                at = slice(n * LANES, (n + 1) * LANES)
                ref[:, 0, :, cols] = part[at].reshape(2, half, step)

    @pl.when(now == 1)
    def _():
        for n in range(4):
            at = slice(n * LANES, (n + 1) * LANES)
            other_ref[n, :, 0, :, width:] = mask_ref[at, :].reshape(2, half, LANES)
        for c in range(width // step):
            cols = slice(c * step, (c + 1) * step)
            part = dot(grads_ref[0], gate_up_t_ref[:, cols]).astype(BF16)
            for n in range(4):
                at = slice(n * LANES, (n + 1) * LANES)
                other_ref[n, :, 0, :, cols] = part[at].reshape(2, half, step)


def expert_call(at, rows, cot, lead, w_gate, w_up, gate_up_t, router, experts_all):
    eight, half, width = rows[0].shape
    shards, units = cot.shape[0], lead.shape[4]
    count = eight * half
    own_shape = (2, 1, half, width + LANES)

    def core_of(i, at):
        return lax.rem(at[3] + i, 2)

    return pl.pallas_call(
        lambda *refs: expert_kernel(experts_all, *refs),
        grid_spec=pltpu.PrefetchScalarGridSpec(
            num_scalar_prefetch=1,
            grid=(2,),
            in_specs=[
                pl.BlockSpec(r.shape, lambda i, _: (0, 0, 0), pipeline_mode=pl.Buffered(1))
                for r in rows
            ]
            + [
                pl.BlockSpec(
                    (shards, 1, 1, 2, half, LANES),
                    lambda i, at: (0, at[2], core_of(i, at), 0, 0, width // LANES),
                ),
                pl.BlockSpec(
                    (1, 1, eight, half, units), lambda i, at: (at[2], core_of(i, at), 0, 0, 0)
                ),
            ]
            + [whole(w_gate.shape), whole(w_up.shape), whole(gate_up_t.shape), whole(router.shape)],
            out_specs=[whole(own_shape) for _ in range(4)]
            + [
                whole((4,) + own_shape),
                pl.BlockSpec((1, count, 2 * units), lambda i, _: (i, 0, 0)),
                pl.BlockSpec((1, eight, half, units), lambda i, _: (i, 0, 0, 0)),
                pl.BlockSpec((1, count, units), lambda i, _: (i, 0, 0)),
            ],
            scratch_shapes=[
                pltpu.VMEM((count, width), BF16),
                pltpu.VMEM((count, LANES), BF16),
                pltpu.VMEM((count, units), F32),
            ],
        ),
        out_shape=[out(own_shape, BF16)] * 4
        + [
            out((4,) + own_shape, BF16),
            out((2, count, 2 * units), BF16),
            out((2, eight, half, units), BF16),
            out((2, count, units), BF16),
        ],
        compiler_params=pltpu.CompilerParams(vmem_limit_bytes=48 << 20),
        cost_estimate=pl.CostEstimate(
            flops=8 * count * gate_up_t.size,
            bytes_accessed=8 * count * width + 4 * gate_up_t.size + 20 * count * units,
            transcendentals=2 * count * units,
        ),
        name="experts",
    )(at, *rows, cot, lead, w_gate, w_up, gate_up_t, router)


def mix_kernel(scaled_ref, down_ref, *refs):
    width = down_ref.shape[1]
    half = LANES // 2
    step = 512
    for c in range(width // step):
        cols = slice(c * step, (c + 1) * step)
        part = dot(scaled_ref[0], down_ref[:, cols])
        for n in range(4):
            some = part[n * LANES : (n + 1) * LANES].reshape(2, half, step)
            if len(refs) == 1:
                refs[0][n, :, 0, :, cols] = some.astype(BF16)
            else:
                more = refs[0][n, :, 0, :, cols].astype(F32)
                refs[1 + n][:, 0, :, cols] = (some + more).astype(BF16)


def mix_call(scaled, down, *others):
    chips, count, units = scaled.shape
    width = down.shape[1]
    shape = (2, chips, LANES // 2, width)
    quad = pl.BlockSpec((2, 1, LANES // 2, width), lambda i: (0, i, 0, 0))
    quads = pl.BlockSpec((4, 2, 1, LANES // 2, width), lambda i: (0, 0, i, 0, 0))
    return pl.pallas_call(
        mix_kernel,
        grid=(chips,),
        in_specs=[
            pl.BlockSpec((1, count, units), lambda i: (i, 0, 0)),
            whole(down.shape),
        ]
        + [quads] * len(others),
        out_specs=[quad] * 4 if others else quads,
        out_shape=[out(shape, BF16)] * 4 if others else out((4,) + shape, BF16),
        cost_estimate=pl.CostEstimate(
            flops=2 * scaled.size * width,
            bytes_accessed=2 * scaled.size + 2 * down.size + 4 * chips * count * width,
            transcendentals=0,
        ),
        name="mix",
    )(scaled, down, *others)


def row_grad_kernel(count, *refs):
    rows_refs, grads_refs, out_ref = refs[:count], refs[count:-1], refs[-1]
    _, step, unit_part = out_ref.shape
    total = jnp.zeros((step, 2 * unit_part), F32)
    for n, ref in enumerate(rows_refs):
        total = total + t_dot(ref[...].reshape(-1, step), grads_refs[n // 2][n % 2])
    for e in range(2):
        out_ref[e] = total[:, e * unit_part : (e + 1) * unit_part]


def row_grad_call(groups, which):
    step = 256
    rows = [r for pair, _ in groups for r in pair]
    eight, half, width = rows[0].shape
    _, count, four = groups[0][1].shape
    units = four // 2
    held = pl.BlockSpec((2, count, units), lambda i: (0, 0, which), pipeline_mode=pl.Buffered(1))
    return pl.pallas_call(
        lambda *refs: row_grad_kernel(len(rows), *refs),
        grid=(width // step,),
        in_specs=[pl.BlockSpec((eight, half, step), lambda i: (0, 0, i))] * len(rows)
        + [held] * len(groups),
        out_specs=pl.BlockSpec((2, step, units // 2), lambda i: (0, i, 0)),
        out_shape=out((2, width, units // 2), F32),
        cost_estimate=pl.CostEstimate(
            flops=2 * len(rows) * count * width * units,
            bytes_accessed=2 * len(rows) * count * (width + units) + 4 * width * units,
            transcendentals=0,
        ),
        name="row_grads",
    )(*rows, *[g for _, g in groups])


def down_grad_kernel(count, at_ref, *refs):
    scaled_refs, cot_refs, out_ref = refs[:count], refs[count:-1], refs[-1]
    _, unit_part, step = out_ref.shape
    total = jnp.zeros((2 * unit_part, step), F32)
    for n, scaled_ref in enumerate(scaled_refs):
        for side in range(2):
            cot = cot_refs[2 * n + side][...].reshape(-1, step)
            total = total + t_dot(scaled_ref[side].reshape(-1, 2 * unit_part), cot)
    for e in range(2):
        out_ref[e] = total[e * unit_part : (e + 1) * unit_part]


def down_grad_call(at, scaled, cot):
    step = 256
    shards, _, _, two, half, columns = cot.shape
    _, eight, _, units = scaled[0].shape
    width = (columns // step) * step
    count = len(scaled)

    def tile(n, side):
        return pl.BlockSpec(
            (shards, 1, 1, two, half, step),
            lambda i, at: (0, at[1 + n], lax.rem(at[0] + side, 2), 0, 0, i),
        )

    return pl.pallas_call(
        lambda *refs: down_grad_kernel(count, *refs),
        grid_spec=pltpu.PrefetchScalarGridSpec(
            num_scalar_prefetch=1,
            grid=(width // step,),
            in_specs=[
                pl.BlockSpec(
                    s.shape, lambda i, _: (0, 0, 0, 0), pipeline_mode=pl.Buffered(1)
                )
                for s in scaled
            ]
            + [tile(n, side) for n in range(count) for side in range(2)],
            out_specs=pl.BlockSpec((2, units // 2, step), lambda i, _: (0, 0, i)),
        ),
        out_shape=out((2, units // 2, width), F32),
        cost_estimate=pl.CostEstimate(
            flops=4 * count * eight * half * width * units,
            bytes_accessed=4 * count * eight * half * (width + units) + 4 * width * units,
            transcendentals=0,
        ),
        name="down_grads",
    )(at, *scaled, *([cot] * (2 * count)))


def add_up(parts):
    total = parts[0]
    for part in parts[1:]:
        total = total + part
    return total


def turn_kernel(
    experts_all,
    ring_ref,
    a0,
    a1,
    a2,
    b0,
    b1,
    b2,
    residual_ref,
    cot_ref,
    mixed_ref,
    router_ref,
    router_rows_ref,
    gain_ref,
    grad_ref,
    grad_b_ref,
    gain_grad_ref,
    router_grad_ref,
):
    width = residual_ref.shape[2]
    half = residual_ref.shape[1]
    lane = lax.broadcasted_iota(jnp.int32, (half, LANES), 1)
    gain_grad, router_grad = None, None
    for n, refs in enumerate(((a0, a1, a2), (b0, b1, b2))):
        back = ring_ref[n].astype(F32) + total_of([r[...] for r in refs])
        mixed = mixed_ref[n]
        powers = jnp.where(lane < experts_all, jnp.exp(dot(mixed, router_ref[...])), 0.0)
        probs = powers / jnp.sum(powers, axis=-1, keepdims=True)
        prob_grad = back[:, width:]
        logit_grad = (
            probs * (prob_grad - jnp.sum(probs * prob_grad, axis=-1, keepdims=True))
        ).astype(BF16)
        mixed_grad = back[:, :width] + dot(logit_grad, router_rows_ref[...])
        residual = residual_ref[n]
        norm_grad, gain_now = norm_back(mixed_grad, residual, rms_scale(residual), gain_ref[...])
        total = cot_ref[n] + norm_grad
        grad_ref[n] = total
        grad_b_ref[n] = total.astype(BF16)
        router_now = t_dot(logit_grad, mixed)
        gain_grad = gain_now if gain_grad is None else gain_grad + gain_now
        router_grad = router_now if router_grad is None else router_grad + router_now
    gain_grad_ref[...] = jnp.broadcast_to(gain_grad, gain_grad_ref.shape)
    router_grad_ref[...] = router_grad[: router_grad_ref.shape[0]]


def output_grad_kernel(core_ref, g0, g1, g2, g3, attended_ref, own_ref, other_ref):
    blocks, half, step = own_ref.shape
    own_cols = pl.ds(pl.multiple_of(core_ref[0] * half, half), half)
    other_cols = pl.ds(pl.multiple_of((1 - core_ref[0]) * half, half), half)
    for c in range(blocks):
        cols = slice(c * step, (c + 1) * step)
        grads = jnp.concatenate(
            [g[:, :, cols].reshape(LANES, step) for g in (g0, g1, g2, g3)], axis=0
        )
        own_ref[c] = t_dot(attended_ref[:, own_cols], grads)
        other_ref[c] = t_dot(attended_ref[:, other_cols], grads).astype(BF16)


def attend_back_kernel(
    g0,
    g1,
    g2,
    g3,
    w_ref,
    attended_ref,
    q_ref,
    k_ref,
    v_ref,
    lse_ref,
    scales_ref,
    bias_ref,
    cos_ref,
    sin_ref,
    gain_q_ref,
    gain_k_ref,
    proj_ref,
    query_ref,
    key_ref,
    value_ref,
    stats_ref,
    gains_ref,
    grad_ref,
):
    part, width = w_ref.shape
    rows = proj_ref.shape[0]
    grad_ref[...] = jnp.concatenate(
        [g[...].reshape(LANES, width) for g in (g0, g1, g2, g3)], axis=0
    )
    q_scale, k_scale = scales_ref[:, 0:1], scales_ref[:, 1:2]
    cosine, sine_part = cos_ref[...], sin_ref[...]
    q_inner = jnp.zeros((rows, 1), F32)
    k_inner = jnp.zeros((rows, 1), F32)
    for h in range(part // HEAD_DIM):
        cols = slice(h * HEAD_DIM, (h + 1) * HEAD_DIM)
        k_cols = slice(part + h * HEAD_DIM, part + (h + 1) * HEAD_DIM)
        attended_grad = dot_t(grad_ref[...], w_ref[cols, :]).astype(BF16)
        query, key, value = q_ref[:, cols], k_ref[:, cols], v_ref[:, cols]
        probs = jnp.exp(
            dot_t(query, key) * SCORE_SCALE + bias_ref[...] - lse_ref[:, h : h + 1]
        )
        delta = jnp.sum(
            attended_grad.astype(F32) * attended_ref[:, cols].astype(F32), axis=-1, keepdims=True
        )
        score_grad = (probs * (dot_t(attended_grad, value) - delta)).astype(BF16)
        value_ref[:, cols] = t_dot(probs.astype(BF16), attended_grad).astype(BF16)
        query_grad = dot(score_grad, key) * SCORE_SCALE
        key_grad = t_dot(score_grad, query) * SCORE_SCALE
        query_pre = query_grad * cosine + pltpu.roll(query_grad * sine_part, HEAD_DIM // 2, 1)
        key_pre = key_grad * cosine + pltpu.roll(key_grad * sine_part, HEAD_DIM // 2, 1)
        q_proj, k_proj = proj_ref[:, cols], proj_ref[:, k_cols]
        gains_ref[0:1, cols] = jnp.sum(query_pre * q_proj * q_scale, axis=0, keepdims=True)
        gains_ref[1:2, cols] = jnp.sum(key_pre * k_proj * k_scale, axis=0, keepdims=True)
        query_pre = query_pre * gain_q_ref[:, cols]
        key_pre = key_pre * gain_k_ref[:, cols]
        query_ref[:, cols] = query_pre
        key_ref[:, cols] = key_pre
        q_inner = q_inner + jnp.sum(query_pre * q_proj, axis=-1, keepdims=True)
        k_inner = k_inner + jnp.sum(key_pre * k_proj, axis=-1, keepdims=True)
    for n, stats in enumerate(pack_stats(q_inner, k_inner)):
        stats_ref[n] = stats


def project_back_kernel(
    at_ref, s0, s1, s2, s3, query_ref, key_ref, value_ref, proj_ref, scales_ref, normed_ref, *refs
):
    weight_refs = refs[:8]
    part_refs, pair_ref, all_ref = refs[8:12], refs[12], refs[13]
    width = normed_ref.shape[1]
    part = query_ref.shape[1]
    inner = sum_stats(s0, s1, s2, s3) / width
    for n, (grad_ref, low) in enumerate(((query_ref, 0), (key_ref, part))):
        scale = scales_ref[:, n : n + 1]
        factor = scale * scale * inner[:, n : n + 1]
        all_ref[:, low : low + part] = (
            scale * (grad_ref[...] - proj_ref[:, low : low + part] * factor)
        ).astype(BF16)
    all_ref[:, 2 * part :] = value_ref[...]
    depth = weight_refs[0].shape[0]
    for n, ref in enumerate(weight_refs):
        at = pl.ds(pl.multiple_of(at_ref[n] * depth, depth), depth)
        got = dot_t(all_ref[...], ref[...]).astype(BF16)
        for k, part_ref in enumerate(part_refs):
            part_ref[:, :, at] = got[k * LANES : (k + 1) * LANES].reshape(2, LANES // 2, depth)
    members, parts, rows, _ = pair_ref.shape
    for p in range(parts):
        for third in range(2):
            cols = slice(third * part, (third + 1) * part)
            got = t_dot(normed_ref[:, p * part : (p + 1) * part], all_ref[:, cols]).astype(BF16)
            for e in range(members):
                pair_ref[e, p, :, cols] = got[e * rows : (e + 1) * rows]


def value_back_kernel(core_ref, value_ref, normed_ref, own_ref, other_ref):
    parts, depth, _ = own_ref.shape
    for p in range(parts):
        for ref, side in ((own_ref, core_ref[0]), (other_ref, 1 - core_ref[0])):
            at = pl.ds(pl.multiple_of((2 * p + side) * depth, depth), depth)
            ref[p] = t_dot(normed_ref[:, at], value_ref[...]).astype(ref.dtype)


def finish_kernel(a0, a1, a2, b0, b1, b2, x_ref, grad_ref, gain_ref, out_ref, gain_grad_ref):
    gain_grad = None
    for n, refs in enumerate(((a0, a1, a2), (b0, b1, b2))):
        source = x_ref[n].astype(F32)
        normed_grad = total_of([r[...] for r in refs])
        norm_grad, gain_now = norm_back(normed_grad, source, rms_scale(source), gain_ref[...])
        out_ref[n] = grad_ref[n] + norm_grad
        gain_grad = gain_now if gain_grad is None else gain_grad + gain_now
    gain_grad_ref[...] = jnp.broadcast_to(gain_grad, gain_grad_ref.shape)


def cut_kernel(at_ref, *refs):
    sources, (own_ref, spare_ref, x_ref, y_ref) = refs[:15], refs[15:]
    depth, part = sources[0].shape
    rows = depth // 2
    for w in range(3):
        cols = slice(w * part, (w + 1) * part)
        own_ref[:, cols] = sources[w][...]
        x_ref[:depth, cols] = sources[3 + w][...]
        y_ref[:depth, cols] = sources[6 + w][...]
        x_ref[depth:, cols] = sources[9 + w][:rows, :]
        y_ref[depth:, cols] = sources[9 + w][rows:, :]
        spare_ref[:, cols] = sources[12 + w][...]


def cut_call(at, w_query, w_key, w_value):
    rows, width = w_query.shape
    part = width // 4
    depth = rows // 2

    def block(member, core):
        return pl.BlockSpec((depth, part), lambda i, at: (at[core], at[member]))

    full, more = (depth, 3 * part), (3 * depth // 2, 3 * part)
    fulls = [full, full, more, more]
    return pl.pallas_call(
        cut_kernel,
        grid_spec=pltpu.PrefetchScalarGridSpec(
            num_scalar_prefetch=1,
            grid=(1,),
            in_specs=[block(d, 4) for d in range(4) for _ in range(3)]
            + [block(0, 5) for _ in range(3)],
            out_specs=[whole(s) for s in fulls],
        ),
        out_shape=[out(s, BF16) for s in fulls],
        name="cut",
    )(at, *([w_query, w_key, w_value] * 5))


def on_device(
    block_input,
    segment_ids,
    expert_routes,
    attn_gain,
    w_query,
    w_key,
    w_value,
    query_gain,
    key_gain,
    w_output,
    moe_gain,
    w_router,
    w_gate,
    w_up,
    w_down,
    out_cotangent,
):
    expert_count = lax.axis_size("expert")
    shard_count = lax.axis_size("shard")
    chips = expert_count // 2
    me = lax.axis_index("shard")
    place = lax.axis_index("expert")
    core = lax.rem(place, 2)
    chip = place // 2
    tok_count = block_input.shape[1]
    half = tok_count // 2
    group_count = segment_ids.shape[1]
    width = block_input.shape[2]
    part = width // shard_count
    local_experts = w_gate.shape[0]
    experts_all = local_experts * expert_count
    unit_part = w_gate.shape[2]
    units = local_experts * unit_part
    core_at = jnp.reshape(core, (1,))

    own_input = block_input.reshape(2, half, width)
    group_input = [b.reshape(2, half, width) for b in spread_xy(own_input[:1], own_input[1:])]

    small = jnp.concatenate([attn_gain[None], moe_gain[None], w_router.T], axis=0)
    small = jnp.pad(small, ((0, (-small.shape[0]) % 32), (0, 0)))
    small_all = jnp.zeros((small.shape[0], width), BF16)
    small_parts = gather_parts(small)
    for d, got in enumerate(small_parts):
        small_all = lax.dynamic_update_slice_in_dim(small_all, got, (me ^ d) * part, 1)
    gain_one = small_all[0:1].astype(F32)
    gain_two = small_all[1:2].astype(F32)
    router = small_all[2 : 2 + experts_all]
    router = jnp.pad(router, ((0, LANES - experts_all), (0, 0)))
    router_t = router.T

    depth = part // 2
    at = jnp.stack([me, me ^ 1, me ^ 2, me ^ 3, core, 1 - core])
    cuts = cut_call(at, w_query, w_key, w_value)
    gate_up_t, down_t = flip_call(w_gate, w_up, w_down)
    direct = exchange_blocks(
        *after(cuts[2:], group_input[0], group_input[2], small_parts), group_input, gate_up_t
    )
    passed = [swap_core(block) for block in direct]
    weight_blocks = list(cuts[:2]) + direct + passed
    weight_at = jnp.stack(
        [2 * me + core, 2 * me + 1 - core]
        + [2 * (me ^ d) + core for d in (1, 2, 3)]
        + [2 * (me ^ d) + 1 - core for d in (1, 2, 3)]
    )

    routes = expert_routes[0]
    routed = jnp.sum(
        (routes[:, :, None] == jnp.arange(experts_all)[None, None, :]).astype(F32), axis=1
    )
    cotangent = out_cotangent[0]
    cot_block = (
        jnp.concatenate(
            [cotangent, routed, jnp.zeros((tok_count, LANES - experts_all), F32)], axis=1
        )
        .astype(BF16)
    )
    cot = lax.all_gather(cot_block, ("shard", "expert"), axis=0, tiled=True)

    down_w = w_down.reshape(units, width)

    starts = [(me ^ d) * tok_count + side * half for pair in ORDER for side, d in pair]
    position = jnp.concatenate([p + jnp.arange(half) for p in starts])
    seg_all = segment_ids[0]
    seg_here = jnp.concatenate([lax.dynamic_slice_in_dim(seg_all, p, half) for p in starts])
    allowed = (seg_here[:, None] == seg_here[None, :]) & (position[None, :] <= position[:, None])
    bias = jnp.where(allowed, 0.0, -1e30).astype(F32)
    half_dim = HEAD_DIM // 2
    inverse = 10000.0 ** (-(jnp.arange(half_dim).astype(F32) * 2.0) / HEAD_DIM)
    angles = position.astype(F32)[:, None] * inverse[None, :]
    cosine = jnp.concatenate([jnp.cos(angles), jnp.cos(angles)], axis=-1)
    sine_part = jnp.concatenate([-jnp.sin(angles), jnp.sin(angles)], axis=-1)
    gain_query = query_gain.astype(F32)[None]
    gain_key = key_gain.astype(F32)[None]
    normed, proj, squares, scale_one = call(
        project_kernel,
        "project",
        [weight_at] + group_input + [gain_one] + weight_blocks,
        [
            out((group_count, width), BF16),
            out((group_count, 3 * part), F32),
            out((4, 8, LANES), F32),
            out((group_count, LANES), F32),
        ],
        2 * group_count * width * 3 * part,
        smem=(0,),
    )
    quad = out((2, half, width), BF16)
    square_parts = out((group_count, part), BF16)
    heads = call(
        lambda *refs: attend_kernel(width, *refs),
        "attend",
        [proj] + gather_parts(squares) + [gain_query, gain_key, cosine, sine_part, bias, w_output],
        [square_parts] * 3
        + [out((group_count, LANES), F32)] * 2
        + [square_parts]
        + [quad] * 4,
        4 * group_count * group_count * part + 2 * group_count * part * width,
    )
    q_heads, k_heads, v_heads, log_total, scales, attended = heads[:6]
    terms_a, terms_b = reduce_xy([b.reshape(2, 1, half, width) for b in heads[6:]])
    residual, mixed_in = call(
        settle_kernel,
        "settle",
        [own_input]
        + [t.reshape(half, width) for t in terms_a + terms_b]
        + [gain_two],
        [out((2, half, width), F32), out((2, half, width), BF16)],
        tok_count * width,
    )

    pieces = [mixed_in, ring_up(mixed_in)]
    cot = after(cot, mixed_in).reshape(shard_count, chips, 2, 2, half, width + LANES)
    lead = lead_call(cot, down_t)
    pieces[1] = after(pieces[1], lead)
    while len(pieces) < chips:
        pieces.append(ring_up(pieces[-1]))
    chip_at = [lax.rem(chip + chips - j, chips) for j in range(chips)]
    lows, low = [0, 1], 2
    while low < chips:
        lows.append(low)
        low *= 2
    lows.append(chips)
    all_rows, firsts = [], []
    for low, high in zip(lows[:-1], lows[1:]):
        sides = [jnp.stack([p[s] for p in pieces[low:high]]) for s in range(2)]
        pair_a = jnp.stack([sides[0], swap_x(sides[0])])
        pair_b = jnp.stack([sides[1], swap_y(sides[1])])
        firsts.append((pair_a, pair_b))
        if low > 1:
            pair_a, pair_b = after((pair_a, pair_b), all_rows[1][0])
        parts = [pair_a, swap_y(pair_a), pair_b, swap_x(pair_b)]
        for j in range(high - low):
            own = join_call(parts, j)
            all_rows.append((own, swap_core(own)))
    groups, totals_all = [], []
    for j in range(chips):
        at = jnp.stack([place, me, chip_at[j], core])
        at = after(at, totals_all[j - 2] if j > 1 else firsts[:3])
        got = expert_call(
            at, all_rows[j], cot, lead, w_gate, w_up, gate_up_t, router_t, experts_all
        )
        groups.append((all_rows[j], got[5], got[6], got[7]))
        if 0 < j < chips - 1:
            passed_back = swap_core(after(got[4], all_rows[j + 1][1]))
        else:
            passed_back = swap_core(got[4])
        totals_all.append(
            [
                (a.astype(F32) + passed_back[n].astype(F32)).astype(BF16)
                for n, a in enumerate(got[:4])
            ]
        )
    back_terms = [None] * chips

    def back_piece(j):
        return jnp.stack([total_of(terms) for terms in back_terms[j]])

    back_pieces, arrived = [], []
    for j in list(range(1, chips)) + [0]:
        totals = totals_all[j]
        if j == 0:
            totals = after(totals, totals_all[-1], back_pieces[min(1, chips - 2)])
        back_terms[j] = [
            [t[0] for t in terms]
            for terms in reduce_late(
                totals_all[-1] if j == 1 else (),
                after(totals, [r[0] for r in all_rows]),
                totals_all[-1] if j != 1 else (),
                back_pieces[-1:],
                arrived[-1:],
            )
        ]
        if j:
            back_pieces.append(back_piece(j))
        if j == 1:
            ring_total = back_pieces[0].astype(BF16)
        elif j:
            arrived.append(ring_up(ring_total))
            ring_total = (arrived[-1].astype(F32) + back_pieces[-1]).astype(BF16)
    scaled_sides = [
        jnp.concatenate([g[3][side : side + 1] for g in groups]) for side in range(2)
    ]
    mix_passed = swap_core(mix_call(after(scaled_sides[1], ring_total, back_terms[0]), down_w))

    ring_total = ring_up(ring_total)
    grad_res, grad_res_b, grad_gain_two, grad_router = call(
        lambda *refs: turn_kernel(experts_all, *refs),
        "turn",
        [ring_total]
        + back_terms[0][0]
        + back_terms[0][1]
        + [residual, cotangent.reshape(2, half, width), mixed_in, router_t, router]
        + [gain_two],
        [
            out((2, half, width), F32),
            out((2, half, width), BF16),
            out((8, width), F32),
            out((experts_all, width), F32),
        ],
        8 * tok_count * width * LANES,
    )

    group_grad = [b.reshape(2, half, width) for b in spread_xy(grad_res_b[:1], grad_res_b[1:])]
    out_totals = mix_call(
        after(scaled_sides[0], group_grad[0], group_grad[2]), down_w, mix_passed
    )
    output_own, output_other = call(
        output_grad_kernel,
        "output_grad",
        [core_at] + after(group_grad, out_totals) + [attended],
        [out((4, part // 2, width // 4), F32), out((4, part // 2, width // 4), BF16)],
        2 * group_count * part * width,
        smem=(0,),
    )
    query_pre, key_pre, value_grad, inner, gain_grads, _ = call(
        attend_back_kernel,
        "attend_back",
        after(group_grad, output_other)
        + [w_output, attended, q_heads, k_heads, v_heads, log_total, scales, bias]
        + [cosine, sine_part, gain_query, gain_key, proj],
        [
            out((group_count, part), F32),
            out((group_count, part), F32),
            square_parts,
            out((4, 8, LANES), F32),
            out((8, part), F32),
            out((group_count, width), BF16),
        ],
        10 * group_count * group_count * part + 2 * group_count * part * width,
    )
    def split_rows(own):
        parts, rows, columns = own.shape
        split = own.reshape(parts, chips, rows // chips, columns)
        return [lax.dynamic_index_in_dim(split, at, 1, keepdims=False) for at in chip_at]

    inner_parts = gather_parts(inner)
    keep_a, send_a, keep_b, send_b = after(out_totals, inner_parts)
    got_a, got_b = swap_y(send_a), swap_x(send_b)
    out_far = (
        (keep_a[1].astype(F32) + got_a[1].astype(F32)).astype(BF16),
        (keep_b[1].astype(F32) + got_b[1].astype(F32)).astype(BF16),
    )
    out_terms = (
        (keep_a[0], got_a[0], swap_x(out_far[0])),
        (keep_b[0], got_b[0], swap_y(out_far[1])),
    )

    def out_piece(j):
        return jnp.stack([total_of([t[j] for t in side]) for side in out_terms])

    def ring_add(total, pieces, *others):
        moved = after(ring_up(total), *others)
        return (moved.astype(F32) + pieces.pop(0)).astype(BF16)

    output_passed = after(swap_core(output_other), query_pre)
    output_pieces = split_rows(output_own + output_passed.astype(F32))
    output_pieces = output_pieces[1:] + output_pieces[:1]
    output_total = output_pieces.pop(0).astype(BF16)
    value_own, value_other = call(
        value_back_kernel,
        "value_back",
        [core_at] + after([value_grad], inner, output_total) + [normed],
        [out((4, depth, part), F32), out((4, depth, part), BF16)],
        2 * group_count * width * part,
        smem=(0,),
    )
    value_passed = swap_core(value_other)
    output_total = ring_add(output_total, output_pieces, value_other)
    got = call(
        project_back_kernel,
        "project_back",
        [weight_at]
        + inner_parts
        + after([query_pre, key_pre, value_grad, proj, scales, normed], output_total)
        + weight_blocks,
        [quad] * 4
        + [
            out((expert_count, 4, part // expert_count, 2 * part), BF16),
            out((group_count, 3 * part), BF16),
        ],
        4 * group_count * width * 3 * part,
        smem=(0,),
    )
    def exchange_grads(piece):
        sent = [lax.dynamic_index_in_dim(piece, me ^ d, 0, keepdims=False) for d in range(4)]
        low = sent[3].shape[0] // 2
        arrived = exchange_blocks(
            jnp.concatenate([sent[1], sent[3][:low]], axis=0),
            jnp.concatenate([sent[2], sent[3][low:]], axis=0),
        )
        return jnp.stack([sent[0]] + arrived)

    def whole_grads(rows):
        shares = [lax.dynamic_index_in_dim(rows, me ^ p, 0, keepdims=False) for p in range(4)]
        return [
            jnp.concatenate(
                [share[:, n * part : (n + 1) * part] for share in shares], axis=1
            ).astype(F32)
            for n in range(rows.shape[2] // part)
        ]

    pair_sums = lax.psum_scatter(got[4], "expert", scatter_dimension=0, tiled=True)[0]

    span = min(chips, 4)
    starts = range(0, chips, span)

    def row_grads(which, *others):
        late = after([g[1] for g in groups], *others)
        return add_up(
            [
                row_grad_call([(g[0], v) for g, v in zip(groups, late)][low : low + span], which)
                for low in starts
            ]
        )

    def down_grads(*others):
        late = after([g[2] for g in groups], *others)
        return add_up(
            [
                down_grad_call(
                    jnp.stack([core] + chip_at[low : low + span]), late[low : low + span], cot
                )
                for low in starts
            ]
        )

    expert_grads = [down_grads(got[0])]
    output_total = ring_add(output_total, output_pieces, expert_grads[0])
    value_pieces = split_rows(
        value_own + after(value_passed, expert_grads[0]).astype(F32)
    )
    value_pieces = value_pieces[1:] + value_pieces[:1]
    total = value_pieces.pop(0).astype(BF16)
    expert_grads.append(row_grads(0, total, output_total))
    total = ring_add(total, value_pieces, expert_grads[1])
    output_total = ring_add(output_total, output_pieces, expert_grads[1])
    first_kept, first_on = reduce_first(
        [b.reshape(2, 1, half, width) for b in got[:4]], total, output_total
    )
    expert_grads.append(row_grads(1, total, output_total, first_on, out_far))
    while output_pieces:
        output_total = ring_add(output_total, output_pieces, expert_grads[2])
    out_spread = [output_total]
    while len(value_pieces) > 1:
        total = ring_add(total, value_pieces, expert_grads[2])
    out_spread.append(after(ring_up(out_spread[-1]), total))
    terms_a, terms_b = reduce_last(first_kept, first_on)
    grad_input, grad_gain_one = call(
        finish_kernel,
        "finish",
        [t.reshape(half, width) for t in terms_a + terms_b]
        + [own_input, grad_res, after(gain_one, out_spread[-1])],
        [out((2, half, width), F32), out((8, width), F32)],
        tok_count * width,
    )
    out_now = after(out_piece(1), total).astype(BF16)
    pair_mine = exchange_grads(after(pair_sums, grad_gain_one, out_now))
    pair_rows = lax.all_gather(pair_mine, "expert", axis=0)
    total = ring_add(total, value_pieces, pair_mine)
    spread = [exchange_grads(total)]
    grad_w_down, grad_w_gate, grad_w_up = expert_grads
    for j in range(1, chips):
        moved = after(ring_up(out_now), spread[0])
        if j + 1 < chips:
            out_now = (moved.astype(F32) + out_piece(j + 1)).astype(BF16)
        spread.append(after(ring_up(spread[-1]), out_now if j + 1 < chips else moved))
        if len(out_spread) < chips:
            out_spread.append(after(ring_up(out_spread[-1]), spread[-1]))
    while len(out_spread) < chips:
        out_spread.append(ring_up(out_spread[-1]))
    block_output = residual + (moved.astype(F32) + out_piece(0))
    early_rows = expert_spread(out_spread, core, chip)
    grad_w_output = jnp.concatenate([early_rows[c] for c in range(4)], axis=1).astype(F32)
    (grad_w_value,) = whole_grads(expert_spread(spread, core, chip))
    pair_rows = jnp.transpose(pair_rows, (1, 0, 2, 3)).reshape(4, part, 2 * part)
    grad_w_query, grad_w_key = whole_grads(pair_rows)

    grad_gain_one = after(grad_gain_one, spread[0])
    packed = jnp.concatenate([grad_gain_one[:1], grad_gain_two[:1], grad_router], axis=0)
    rows_used = packed.shape[0]
    packed = jnp.pad(packed, ((0, (-rows_used) % 16), (0, 0)))
    quarters = jnp.stack(
        [lax.dynamic_slice_in_dim(packed, (me ^ d) * part, part, 1) for d in range(4)]
    )
    quarters = quarters[:2] + swap_y(quarters[2:])
    packed = (quarters[0] + swap_x(quarters[1]))[:rows_used]
    packed = after(jnp.concatenate([packed, gain_grads[:2]], axis=0), spread[-1])
    bit = 1
    while bit < expert_count:
        packed = packed + flip_expert(packed, bit)
        bit *= 2
    return (
        block_output.reshape(1, tok_count, width),
        grad_input.reshape(1, tok_count, width),
        packed[0],
        grad_w_query,
        grad_w_key,
        grad_w_value,
        packed[rows_used],
        packed[rows_used + 1],
        grad_w_output,
        packed[1],
        packed[2 : 2 + experts_all].T,
        grad_w_gate,
        grad_w_up,
        grad_w_down,
    )


def solution(mesh):
    placed = (
        P("expert", "shard", None),
        P("expert", None),
        P("expert", "shard", None),
        P("shard"),
        P("shard", None),
        P("shard", None),
        P("shard", None),
        P("shard"),
        P("shard"),
        P("shard", None),
        P("shard"),
        P("shard", None),
        P("expert", None, "shard"),
        P("expert", None, "shard"),
        P("expert", "shard", None),
        P("expert", "shard", None),
    )
    return jax.shard_map(
        on_device,
        mesh=mesh,
        in_specs=placed,
        out_specs=(
            P("expert", "shard", None),
            P("expert", "shard", None),
            P("shard"),
            P("shard", None),
            P("shard", None),
            P("shard", None),
            P("shard"),
            P("shard"),
            P("shard", None),
            P("shard"),
            P("shard", None),
            P("expert", None, "shard"),
            P("expert", None, "shard"),
            P("expert", "shard", None),
        ),
        check_vma=False,
    )
```
